128 devices in a mesh: lat: 8 (over y, z_lo), lon: 16 (over z_hi, x, core).
Axes of the slice: x: 4, y: 4, z: 4 (z_hi: 2, z_lo: 2; z = z_hi * 2 + z_lo), core: 2. Of those that a mesh axis runs over, the one named last changes fastest.
Arguments:
- ensemble: float32 [64, 4, 64, 2048], P(None, None, 'lat', 'lon'), may hold values from -6 to 6
- courant_lon: float32 [4, 64, 2048], P(None, 'lat', 'lon'), may hold values from -0.4 to 0.4
- courant_lat: float32 [4, 64, 2048], P(None, 'lat', 'lon'), may hold values from -0.4 to 0.4
- diffusion: float32 [4, 64, 2048], P(None, 'lat', 'lon'), may hold values from 0.02 to 0.05
- obs_cells: int32 [4, 4, 8, 256, 128], P(None, None, 'lat', 'lon'), may hold values from 0 to 255
- obs_counts: int32 [4, 8, 256], P(None, 'lat', 'lon'), may hold values from 1 to 128, as said below
- obs_values: float32 [4, 8, 256, 128], P(None, 'lat', 'lon'), may hold values from -6 to 6
- obs_errors: float32 [4, 8, 256, 128], P(None, 'lat', 'lon'), may hold values from 0.5 to 2
- owners: int32 [8, 256, 1], P('lat', 'lon'), may hold values from 0 to 15; in each aligned block of 16 rows (0 to 15, 16 to 31, ..., all dimensions but the last counted through in order) at most 2 rows name the same one
Outputs:
- analysis: float32 [64, 4, 64, 2048], P(None, None, 'lat', 'lon')
- held_transforms: float32 [8, 16, 16, 2, 64, 64], P('lat', 'lon')
The draws below stay inside these ranges and needn't reach their ends.
Inputs may be any that keep to these rules, and one draw needn't show every extreme that they name: `owners`: among the 16 patches of one device no owner is named more than 2 times, and some device names some owner exactly 2 times. `obs_counts`: in every slot some patch has all 128 rows live. `obs_cells`: flat cell index within the patch, in the order (level, row, column).
All inputs are finite; a program needn't handle non-finite values.
Results may differ from the reference program's by a relative error of at most 0.0019.
Values may be sent and summed in bfloat16 or wider, within the bound.
A program may use at most 128 MiB of HBM per device.

```python
import math
import jax
import jax.numpy as jnp
import numpy as np
from jax import lax

K = 64
L = 4
CLAT = 8
CLON = 128
P_DEV = 16
PCAP = 2
OBS = 128
SLOTS = 4
STEPS = 3
NS_ITERS = 6
NLAT = 64
NLON = 2048
PW = 8
PCOLS = 256
N_LAT = 8
N_LON = 16


def draw_obs_counts(key, part):
    keys = jax.random.split(jax.random.fold_in(key, 7), 4)
    shape = (SLOTS, N_LAT * PCOLS)
    dense = jax.random.randint(keys[0], shape, 0, 2)
    high = jax.random.randint(keys[1], shape, OBS // 2, OBS + 1)
    low = jax.random.randint(keys[2], shape, 1, OBS // 4 + 1)
    counts = jnp.where(dense == 1, high, low)
    place = jax.random.randint(keys[3], (SLOTS, 1), 0, N_LAT * PCOLS)
    counts = jnp.where(jnp.arange(N_LAT * PCOLS)[None, :] == place, OBS, counts)
    return counts.reshape(SLOTS, N_LAT, PCOLS).astype(jnp.int32)


def draw_courant_lon(key, part):
    streams = jax.random.split(jax.random.fold_in(key, 11), 2)
    phases = jax.random.uniform(streams[0], (L, 1, 1), jnp.float32, 0.0, 2.0 * jnp.pi)
    row_pos = jnp.arange(NLAT, dtype=jnp.float32)[None, :, None]
    heading = jnp.clip(4.0 * jnp.cos(jnp.pi * row_pos / CLAT + phases), -1.0, 1.0)
    unit_draw = jax.random.uniform(streams[1], (L, NLAT, NLON), jnp.float32)
    magnitude = 0.2 + 0.2 * unit_draw
    return (heading * magnitude).astype(jnp.float32)


def draw_courant_lat(key, part):
    streams = jax.random.split(jax.random.fold_in(key, 13), 2)
    phases = jax.random.uniform(streams[0], (L, 1, 1), jnp.float32, 0.0, 2.0 * jnp.pi)
    col_pos = jnp.arange(NLON, dtype=jnp.float32)[None, None, :]
    heading = jnp.clip(4.0 * jnp.cos(jnp.pi * col_pos / CLON + phases), -1.0, 1.0)
    unit_draw = jax.random.uniform(streams[1], (L, NLAT, NLON), jnp.float32)
    magnitude = 0.2 + 0.2 * unit_draw
    return (heading * magnitude).astype(jnp.float32)


def place_ends(drawn, rng, smallest, high):
    longest = drawn.shape.index(max(drawn.shape))
    spots = []
    for shift in (0, 1):
        where = [jax.random.randint(jax.random.fold_in(rng, axis), (), 0, length) for axis, length in enumerate(drawn.shape)]
        where[longest] = (where[longest] + shift) % drawn.shape[longest]
        spots.append(tuple(where))
    return drawn.at[spots[0]].set(smallest).at[spots[1]].set(high)


def block_levels(stream_key, shape, cuts, smallest, largest):
    def one(dim, blocks):
        steps = jax.random.uniform(jax.random.fold_in(jax.random.fold_in(stream_key, 6), dim), (blocks,), jnp.float32, smallest / len(cuts), largest / len(cuts))
        return jnp.repeat(jnp.exp(steps), shape[dim] // blocks).reshape((-1,) + (1,) * (len(shape) - dim - 1))

    loudness = one(*cuts[0])
    for cut in cuts[1:]:
        loudness = loudness * one(*cut)
    return loudness


def assign_block(own_key, own, number, rows, amount, top, limit, slope):
    ranking = jax.random.permutation(own_key, amount)
    heavy_load, ordinary = load_shares(amount, rows * top, limit, slope, True), load_shares(amount, rows * top, limit, slope, False)
    places = jnp.arange(amount)

    def named(tallies, rotation):
        used = int((tallies > 0).sum())
        fixed = max(1, used // 4)
        moved = fixed + (places - fixed + rotation * (used - fixed)) % max(1, amount - fixed)
        return jnp.zeros((amount,), jnp.int32).at[ranking[jnp.where(places < fixed, places, moved)]].set(jnp.asarray(tallies, jnp.int32))

    tallies = jnp.where(number % 4 == 0, named(heavy_load, number // 4), named(ordinary, number - number // 4 - 1))
    mixed = jax.random.permutation(jax.random.fold_in(own, 3), amount)
    giver, sink = mixed[0:amount // 2 * 2:2], mixed[1:amount // 2 * 2:2]
    room = jnp.minimum(tallies[giver] - 1, limit - tallies[sink]) // 2
    room = jnp.where((giver == ranking[0]) | (sink == ranking[0]) | (tallies[sink] == 0), 0, jnp.maximum(room, 0))
    moved = jax.random.randint(jax.random.fold_in(own, 4), (amount // 2,), 0, 1 << 20) % (room + 1)
    tallies = tallies.at[giver].add(-moved).at[sink].add(moved)
    members = jnp.searchsorted(jnp.cumsum(tallies), jnp.arange(rows * top), side="right").astype(jnp.int32)
    listing = members.reshape(top, rows).T
    listing = listing[jax.random.permutation(jax.random.fold_in(own, 1), rows)]
    rotation = jax.random.randint(jax.random.fold_in(own, 2), (rows, 1), 0, top)
    return jnp.take_along_axis(listing, (jnp.arange(top)[None, :] + rotation) % top, axis=1)


def load_shares(count, total, bound, skew, full):
    portions = [(1 << 20) // math.isqrt(grade ** skew) + 1 for grade in range(1, count + 1)]
    largest = bound if full else min(bound, max(-(-total // count), total * portions[0] // sum(portions)))
    least = 1 if total - largest >= count - 1 else 0
    given, rest = [largest] + [least] * (count - 1), total - largest - least * (count - 1)
    while rest > 0:
        movable = [i for i in range(1, count) if given[i] < largest] or [i for i in range(1, count) if given[i] < bound]
        whole, budget = sum([portions[i] for i in movable]), rest
        for i in movable:
            extra = min(bound - given[i], max(1, budget * portions[i] // whole), rest)
            given[i] = given[i] + extra
            rest = rest - extra
    return np.array(given)


def bell_draw(own_key, extent, width, limit, shards=(), held_as=jnp.bfloat16):
    entries = jax.random.normal(own_key, extent, jnp.float32) * width
    if len(shards) > 0:
        entries = block_levels(own_key, extent, shards, -0.22, 0.18) * entries
    return jnp.clip(entries, min=-limit, max=limit).astype(held_as)


def setup_inputs(seed: int = 0) -> dict:
    streams_of = jax.random.split(jax.random.key(seed), 10)
    ensemble = bell_draw(streams_of[0], (K, L, NLAT, NLON), 1.0, 6.0, ((2, 8), (3, 16)), jnp.float32)
    courant_lon = draw_courant_lon(jax.random.fold_in(streams_of[9], 71), 0)
    courant_lat = draw_courant_lat(jax.random.fold_in(streams_of[9], 71), 0)
    diffusion = jnp.clip(jnp.exp(math.log(0.05) - 0.91629077 * jax.random.uniform(streams_of[3], (L, NLAT, NLON), jnp.float32) ** block_levels(streams_of[3], (L, NLAT, NLON), ((1, 8), (2, 16)), -0.2, 0.2)), 0.02, 0.05)
    obs_cells = place_ends(jax.random.randint(streams_of[4], (SLOTS, 4, N_LAT, PCOLS, OBS), 0, L * CLAT * PW), jax.random.fold_in(streams_of[4], 1), 0, (L * CLAT * PW) - 1).astype(jnp.int32)
    obs_counts = draw_obs_counts(jax.random.fold_in(streams_of[9], 71), 0)
    obs_values = bell_draw(streams_of[6], (SLOTS, N_LAT, PCOLS, OBS), 1.0, 6.0, ((1, 8), (2, 16)), jnp.float32)
    obs_errors = jnp.clip(jnp.exp(math.log(2.0) - 1.3862944 * jax.random.uniform(streams_of[7], (SLOTS, N_LAT, PCOLS, OBS), jnp.float32) ** block_levels(streams_of[7], (SLOTS, N_LAT, PCOLS, OBS), ((1, 8), (2, 16)), -0.2, 0.2)), 0.5, 2.0)
    owners_keys = jax.random.split(jax.random.fold_in(streams_of[8], 1), N_LAT * PCOLS // P_DEV)
    owners_turns = jax.random.permutation(jax.random.fold_in(streams_of[8], 3), N_LAT * PCOLS // P_DEV)
    owners = jax.vmap(lambda own, number: assign_block(jax.random.fold_in(streams_of[8], 2), own, number, P_DEV, N_LON, 1, PCAP, 2))(owners_keys, owners_turns).reshape((N_LAT, PCOLS, 1))
    return {"ensemble": ensemble, "courant_lon": courant_lon, "courant_lat": courant_lat, "diffusion": diffusion, "obs_cells": obs_cells, "obs_counts": obs_counts, "obs_values": obs_values, "obs_errors": obs_errors, "owners": owners}


def advance(padded, cu, cv, dd):
    centre = padded[..., 1:-1, 1:-1]
    west = padded[..., 1:-1, :-2]
    east = padded[..., 1:-1, 2:]
    south = padded[..., :-2, 1:-1]
    north = padded[..., 2:, 1:-1]
    flux = jnp.maximum(cu, 0.0) * (centre - west) + jnp.minimum(cu, 0.0) * (east - centre)
    flux = flux + jnp.maximum(cv, 0.0) * (centre - south) + jnp.minimum(cv, 0.0) * (north - centre)
    return centre - flux + dd * (east + west + north + south - 4.0 * centre)

def wrap_pad(field):
    padded = jnp.pad(field, ((0, 0), (0, 0), (1, 1), (0, 0)))
    return jnp.concatenate([padded[..., -1:], padded, padded[..., :1]], axis=3)

def analyse(gram, along):
    size_k = gram.shape[-1]
    eye = jnp.eye(size_k, dtype=jnp.float32)
    amat = gram + (size_k - 1.0) * eye
    size = jnp.sqrt(lax.optimization_barrier(jnp.sum(amat * amat, axis=(1, 2))))
    yiter = amat / size[:, None, None]
    ziter = jnp.broadcast_to(eye, amat.shape)
    hi = lax.Precision.HIGHEST
    for index in range(NS_ITERS):
        mixer = 1.5 * eye - 0.5 * jnp.einsum('qij,qjk->qik', ziter, yiter, precision=hi)
        yiter = jnp.einsum('qij,qjk->qik', yiter, mixer, precision=hi)
        ziter = jnp.einsum('qij,qjk->qik', mixer, ziter, precision=hi)
    spread = ziter * jnp.sqrt((size_k - 1.0) / size)[:, None, None]
    first = jnp.einsum('qij,qj->qi', ziter, along, precision=hi)
    mean_w = jnp.einsum('qij,qj->qi', ziter, first, precision=hi) / size[:, None]
    return spread + mean_w[:, :, None]

def reference(ensemble, courant_lon, courant_lat, diffusion, obs_cells, obs_counts, obs_values, obs_errors, owners):
    hi = lax.Precision.HIGHEST
    state = ensemble
    gram = jnp.zeros((N_LAT, PCOLS, K, K), jnp.float32)
    along = jnp.zeros((N_LAT, PCOLS, K), jnp.float32)
    for slot in range(SLOTS):
        for step in range(STEPS):
            state = advance(wrap_pad(state), courant_lon, courant_lat, diffusion)
        patched = state.reshape(K, L, N_LAT, CLAT, PCOLS, PW).transpose(2, 4, 0, 1, 3, 5).reshape(N_LAT, PCOLS, K, L * CLAT * PW)
        total = jnp.zeros((N_LAT, PCOLS, K, OBS), jnp.float32)
        for corner in range(4):
            where_at = jnp.broadcast_to(obs_cells[slot, corner][:, :, None, :], (N_LAT, PCOLS, K, OBS))
            total = total + jnp.take_along_axis(patched, where_at, axis=3)
        equivalent = 0.25 * total
        obs_mean = lax.optimization_barrier(jnp.mean(equivalent, axis=2))
        live = jnp.arange(OBS)[None, None, :] < obs_counts[slot][:, :, None]
        weight = jnp.where(live, 1.0 / obs_errors[slot], 0.0)
        perturb = ((equivalent - obs_mean[:, :, None, :]) * weight[:, :, None, :]).astype(jnp.bfloat16)
        innov = ((obs_values[slot] - obs_mean) * weight).astype(jnp.bfloat16)
        pert_f = perturb.astype(jnp.float32)
        gram = gram + jnp.einsum('acko,aclo->ackl', pert_f, pert_f, precision=hi)
        along = along + jnp.einsum('acko,aco->ack', pert_f, innov.astype(jnp.float32), precision=hi)
    transform = analyse(gram.reshape(N_LAT * PCOLS, K, K), along.reshape(N_LAT * PCOLS, K)).reshape(N_LAT, PCOLS, K, K)
    grid = state.reshape(K, L, N_LAT, CLAT, PCOLS, PW)
    mean_state = lax.optimization_barrier(jnp.mean(grid, axis=0))
    analysis = mean_state[None] + jnp.einsum('klarcw,ackm->mlarcw', grid - mean_state[None], transform, precision=hi)
    owner_ids = owners[:, :, 0].reshape(N_LAT, N_LON, P_DEV)
    order = jnp.arange(P_DEV)
    earlier = (owner_ids[:, :, :, None] == owner_ids[:, :, None, :]) & (order[None, None, None, :] < order[None, None, :, None])
    rank = lax.optimization_barrier(jnp.sum(earlier.astype(jnp.int32), axis=3))
    empty = analyse(jnp.zeros((1, K, K), jnp.float32), jnp.zeros((1, K), jnp.float32))[0]
    held = jnp.broadcast_to(empty, (N_LAT, N_LON, N_LON, PCAP, K, K))
    row_idx = jnp.arange(N_LAT)[:, None, None]
    src_idx = jnp.arange(N_LON)[None, :, None]
    held = held.at[row_idx, owner_ids, src_idx, rank].set(transform.reshape(N_LAT, N_LON, P_DEV, K, K))
    return (analysis.reshape(K, L, NLAT, NLON), held)
```

```python
import functools

import jax
import jax.numpy as jnp
from jax import lax
from jax.experimental import pallas as pl
from jax.experimental.pallas import tpu as pltpu
from jax.sharding import PartitionSpec as P

PCAP = 2
SLOTS = 4
STEPS = 3
NS_ITERS = 6
MEM = 64
LEV = 4
ROWS = 8
COLS = 128
PATCH = 16
OBS = 128
N_LAT = 8
N_LON = 16
F32 = jnp.float32
BF16 = jnp.bfloat16
NEIGHBOURS = ((-1, 0), (1, 0), (0, -1), (0, 1), (-1, -1), (-1, 1), (1, -1), (1, 1))
S_, N_, W_, E_, SW_, SE_, NW_, NE_ = range(8)


def tile_to_device(row, col):
    return row, col


def lanes(shape):
    return lax.broadcasted_iota(jnp.int32, shape, len(shape) - 1)


def forecast_kernel(ens_ref, cu_ref, cv_ref, dd_ref, out_ref,
                    tiles, coef_got, coefs, field, row_send, edge_send,
                    row_got, edge_got, corner_got,
                    load_sem, csend_sem, crecv_sem, hsend_sem, hrecv_sem):
    lat, lon = lax.axis_index("lat"), lax.axis_index("lon")
    trow, tcol = tile_to_device(lat, lon)

    def device_at(step):
        row = lax.rem(trow + step[0] + N_LAT, N_LAT)
        col = lax.rem(tcol + step[1] + N_LON, N_LON)
        return tile_to_device(row, col)

    barrier = pltpu.get_barrier_semaphore()
    for step in NEIGHBOURS:
        pl.semaphore_signal(barrier, inc=1, device_id=device_at(step),
                            device_id_type=pl.DeviceIdType.MESH)
    loads = [pltpu.make_async_copy(ens_ref, tiles, load_sem.at[0])]
    loads[0].start()
    own = []
    for i, ref in enumerate((cu_ref, cv_ref, dd_ref)):
        own.append(pltpu.make_async_copy(ref, coef_got.at[8, i], load_sem.at[1 + i]))
        own[-1].start()
    for copy in own:
        copy.wait()
    pl.semaphore_wait(barrier, 8)
    opposite = (N_, S_, E_, W_, NE_, NW_, SE_, SW_)
    ccopies = []
    for d, step in enumerate(NEIGHBOURS):
        copy = pltpu.make_async_remote_copy(
            src_ref=coef_got.at[8], dst_ref=coef_got.at[opposite[d]],
            send_sem=csend_sem.at[d], recv_sem=crecv_sem.at[opposite[d]],
            device_id=device_at(step), device_id_type=pl.DeviceIdType.MESH)
        copy.start()
        ccopies.append(copy)
    loads[0].wait()

    @pl.loop(0, LEV * ROWS)
    def _(k):
        r = k // LEV
        l = k % LEV
        parts = [tiles[pl.ds(t * 256 + l * ROWS + r, 8, stride=32), :] for t in range(8)]
        out_ref[0, r, l] = jnp.concatenate(parts, axis=0)

    lane = lanes((MEM, COLS))

    def send_halos(src, s):
        @pl.loop(0, ROWS)
        def _(r):
            packed = out_ref[src, r, 0]
            for l in range(1, LEV):
                turned = pltpu.roll(out_ref[src, r, l], l * 32, 1)
                inside = ((lane + (16 - l * 32 + 128)) & 127) < 32
                packed = jnp.where(inside, turned, packed)
            edge_send[s, r] = packed.astype(BF16)
        for side, first in ((0, 0), (1, ROWS - 3)):
            @pl.loop(0, 3 * LEV)
            def _(k):
                row_send[s, side, k // LEV, k % LEV] = out_ref[src, first + k // LEV, k % LEV].astype(BF16)
        low, high = edge_send.at[s, pl.ds(0, 3)], edge_send.at[s, pl.ds(ROWS - 3, 3)]
        plan = (
            (S_, row_send.at[s, 0], row_got.at[s, 1], N_),
            (N_, row_send.at[s, 1], row_got.at[s, 0], S_),
            (W_, edge_send.at[s], edge_got.at[s, 1], E_),
            (E_, edge_send.at[s], edge_got.at[s, 0], W_),
            (SW_, low, corner_got.at[s, 3], NE_),
            (SE_, low, corner_got.at[s, 2], NW_),
            (NW_, high, corner_got.at[s, 1], SE_),
            (NE_, high, corner_got.at[s, 0], SW_),
        )
        copies = []
        for d, src_ref, dst_ref, landed in plan:
            copy = pltpu.make_async_remote_copy(
                src_ref=src_ref, dst_ref=dst_ref,
                send_sem=hsend_sem.at[s, d], recv_sem=hrecv_sem.at[s, landed],
                device_id=device_at(NEIGHBOURS[d]), device_id_type=pl.DeviceIdType.MESH)
            copy.start()
            copies.append(copy)
        return copies

    copies = send_halos(0, 0)
    for copy in ccopies:
        copy.wait()
    south_ok = jnp.where(trow > 0, 1.0, 0.0).astype(F32)
    north_ok = jnp.where(trow < N_LAT - 1, 1.0, 0.0).astype(F32)
    lane8 = lanes((ROWS, COLS))
    for block, (cen, west, east, ok) in enumerate(((S_, SW_, SE_, south_ok), (8, W_, E_, None), (N_, NW_, NE_, north_ok))):
        for half in range(2):
            for l in range(LEV):
                def pick(i):
                    if half == 0:
                        return jnp.where(lane8 < 96, coef_got[cen, i, l], coef_got[west, i, l])
                    return jnp.where(lane8 >= 32, coef_got[cen, i, l], coef_got[east, i, l])
                cu, cv, dd = pick(0), pick(1), pick(2)
                aw = jnp.maximum(cu, 0.0) + dd
                ae = dd - jnp.minimum(cu, 0.0)
                as_ = jnp.maximum(cv, 0.0) + dd
                an = dd - jnp.minimum(cv, 0.0)
                ac = 1.0 - (jnp.abs(cu) + jnp.abs(cv) + 4.0 * dd)
                for j, a in enumerate((ac, aw, ae, as_, an)):
                    coefs[half, l, j, pl.ds(block * 8, 8), :] = a if ok is None else a * ok

    for s in range(SLOTS):
        for copy in copies:
            copy.wait()
        @pl.loop(0, ROWS)
        def _(r):
            ring = jnp.where((lane & 31) >= 16, edge_got[s, 0, r].astype(F32), edge_got[s, 1, r].astype(F32))
            for l in range(LEV):
                aux = pltpu.roll(ring, 128 - l * 32, 1) if l else ring
                mine = out_ref[max(s - 1, 0), r, l]
                field[0, 0, l, r + 3] = jnp.where(lane < 96, mine, aux)
                field[0, 1, l, r + 3] = jnp.where(lane >= 32, mine, aux)
        for side, base, ok in ((0, 0, south_ok), (1, ROWS + 3, north_ok)):
            @pl.loop(0, 3)
            def _(r):
                ring = jnp.where((lane & 31) >= 16, corner_got[s, side * 2, r].astype(F32),
                                 corner_got[s, side * 2 + 1, r].astype(F32)) * ok
                for l in range(LEV):
                    aux = pltpu.roll(ring, 128 - l * 32, 1) if l else ring
                    mine = row_got[s, side, r, l].astype(F32) * ok
                    field[0, 0, l, r + base] = jnp.where(lane < 96, mine, aux)
                    field[0, 1, l, r + base] = jnp.where(lane >= 32, mine, aux)

        for step in range(STEPS):
            src, dst = step % 2, (step + 1) % 2

            def advance(half, l, r):
                def row(j):
                    return jnp.broadcast_to(coefs[half, l, j, pl.ds(r + 5, 1), :], (8, COLS))
                ac, aw, ae, as_, an = (row(j) for j in range(5))
                news = []
                for t in range(8):
                    ms = pl.ds(t * 8, 8)
                    v = field[src, half, l, r, ms, :]
                    new = ac * v
                    new = new + aw * pltpu.roll(v, 1, 1)
                    new = new + ae * pltpu.roll(v, COLS - 1, 1)
                    new = new + as_ * field[src, half, l, r - 1, ms, :]
                    new = new + an * field[src, half, l, r + 1, ms, :]
                    news.append(new)
                return news

            count = 12 - 2 * step
            if step < STEPS - 1:
                @pl.loop(0, 2 * LEV)
                def _(k):
                    half, l = k // LEV, k % LEV

                    @pl.loop(0, count)
                    def _(i):
                        r = i + 1 + step
                        for t, new in enumerate(advance(half, l, r)):
                            field[dst, half, l, r, pl.ds(t * 8, 8), :] = new
            else:
                lane1 = lanes((8, COLS))

                @pl.loop(0, LEV)
                def _(l):
                    @pl.loop(0, ROWS)
                    def _(i):
                        r = i + 3
                        left, right = advance(0, l, r), advance(1, l, r)
                        for t in range(8):
                            out_ref[s, i, l, pl.ds(t * 8, 8), :] = jnp.where(lane1 < 64, left[t], right[t])
        if s < SLOTS - 1:
            copies = send_halos(s, s + 1)


def forecast(ensemble, cu, cv, dd):
    anyspec = pl.BlockSpec(memory_space=pl.ANY)
    return pl.pallas_call(
        forecast_kernel,
        out_shape=jax.ShapeDtypeStruct((SLOTS, ROWS, LEV, MEM, COLS), F32),
        in_specs=[anyspec] * 4,
        out_specs=pl.BlockSpec(memory_space=pltpu.VMEM),
        scratch_shapes=[
            pltpu.VMEM((MEM * LEV * ROWS, COLS), F32),
            pltpu.VMEM((9, 3, LEV, ROWS, COLS), F32),
            pltpu.VMEM((2, LEV, 5, 24, COLS), F32),
            pltpu.VMEM((2, 2, LEV, 14, MEM, COLS), F32),
            pltpu.VMEM((SLOTS, 2, 3, LEV, MEM, COLS), BF16),
            pltpu.VMEM((SLOTS, ROWS, MEM, COLS), BF16),
            pltpu.VMEM((SLOTS, 2, 3, LEV, MEM, COLS), BF16),
            pltpu.VMEM((SLOTS, 2, ROWS, MEM, COLS), BF16),
            pltpu.VMEM((SLOTS, 4, 3, MEM, COLS), BF16),
            pltpu.SemaphoreType.DMA((4,)),
            pltpu.SemaphoreType.DMA((8,)),
            pltpu.SemaphoreType.DMA((8,)),
            pltpu.SemaphoreType.DMA((SLOTS, 8)),
            pltpu.SemaphoreType.DMA((SLOTS, 8)),
        ],
        compiler_params=pltpu.CompilerParams(
            collective_id=0, has_side_effects=True, vmem_limit_bytes=60 * 1024 * 1024),
        name="forecast",
    )(ensemble.reshape(MEM * LEV * ROWS, COLS), cu, cv, dd)


def butterfly(parts):
    parts = list(parts)
    lane = lanes(parts[0].shape)
    for bit in (1, 2, 4, 8):
        keep = (lane & (8 * bit)) == 0
        for i in range(16):
            if i & bit:
                continue
            a, b = parts[i], parts[i + bit]
            parts[i] = jnp.where(keep, a, pltpu.roll(b, 8 * bit, 1))
            parts[i + bit] = jnp.where(keep, pltpu.roll(a, 128 - 8 * bit, 1), b)
    return parts


def split(x):
    hi = x.astype(BF16)
    return hi, (x - hi.astype(F32)).astype(BF16)


def dot(a, b):
    return jnp.dot(a, b, preferred_element_type=F32)


def dot_t(a, b):
    return lax.dot_general(a, b, (((1,), (1,)), ((), ())), preferred_element_type=F32)


def block_diagonal(x):
    block = lanes(x.shape) // 64
    return jnp.concatenate([jnp.where(block == i, x, jnp.zeros_like(x)) for i in range(4)], axis=0)


def times(x_parts, y_parts):
    yh, yl = y_parts
    n = sum(h.shape[0] for h, _ in x_parts)
    his = [h for h, _ in x_parts]
    los = [l for _, l in x_parts]
    top = dot(jnp.concatenate(his + los, axis=0), yh)
    low = dot(jnp.concatenate(his, axis=0), yl)
    total = top[:n] + top[n:] + low
    outs, at = [], 0
    for h, _ in x_parts:
        outs.append(total[at:at + h.shape[0]])
        at += h.shape[0]
    return outs


def analysis_kernel(state_ref, cells_ref, counts_ref, values_ref, errors_ref, owners_ref,
                    out_ref, held_ref, xs, perts, innovs, last, result):
    def patchwise(slot, write):
        @pl.loop(0, 8)
        def _(k):
            q, t = k // 4, k % 4
            halves = []
            for u in range(2):
                ms = pl.ds(t * 16 + u * 8, 8)
                parts = [state_ref[slot, i % 8, q * 2 + i // 8, ms, :] for i in range(16)]
                halves.append(butterfly(parts))
            for p in range(16):
                write(q, t, p, jnp.concatenate([halves[0][p], halves[1][p]], axis=0))

    cell_id = lax.broadcasted_iota(jnp.int32, (256, OBS), 0).astype(F32).astype(BF16)
    one, zero = jnp.ones((256, OBS), BF16), jnp.zeros((256, OBS), BF16)
    for slot in range(SLOTS):
        def write(q, t, p, x):
            hi, lo = split(x)
            cs = pl.ds(pl.multiple_of(q * 128, 128), 128)
            xs[p, pl.ds(t * 16, 16), cs] = hi
            xs[p, pl.ds(MEM + t * 16, 16), cs] = lo
            if slot == SLOTS - 1:
                last[pl.ds(p * MEM + t * 16, 16), cs] = x
        patchwise(slot, write)

        @pl.loop(0, PATCH)
        def _(p):
            w = zero
            for corner in range(4):
                idx = cells_ref[slot, corner, 0, pl.ds(p, 1), :].astype(F32)
                idx = jnp.broadcast_to(idx, (256, OBS)).astype(BF16)
                w = w + jnp.where(cell_id == idx, one, zero)
            both = dot(xs[p], w)
            equivalent = 0.25 * (both[:MEM] + both[MEM:])
            mean = jnp.sum(equivalent, axis=0, keepdims=True) * (1.0 / MEM)
            live = lanes((1, OBS)) < counts_ref[slot, 0, p]
            weight = jnp.where(live, 1.0 / errors_ref[slot, 0, pl.ds(p, 1), :], 0.0)
            pert = ((equivalent - mean) * weight).astype(BF16)
            perts[p // 4, pl.ds((p % 4) * MEM, MEM), slot * OBS:(slot + 1) * OBS] = pert
            innovs[slot, pl.ds(p, 1), :] = (values_ref[slot, 0, pl.ds(p, 1), :] - mean) * weight

    shape = (MEM, 256)
    block = lanes(shape) // 64
    eye = (lax.broadcasted_iota(jnp.int32, shape, 0) == (lanes(shape) & 63)).astype(F32)
    innov = jnp.concatenate([innovs[s] for s in range(SLOTS)], axis=1).astype(BF16)
    ys, zs, alongs, sizes = [], [], [], []
    for g in range(4):
        pg = perts[g]
        full = dot_t(pg, pg)
        gram = full[0:MEM]
        for i in range(1, 4):
            gram = jnp.where(block == i, full[i * MEM:(i + 1) * MEM], gram)
        al = dot_t(innov, pg)
        row = lax.broadcasted_iota(jnp.int32, al.shape, 0)
        al = jnp.sum(jnp.where(row == g * 4 + lanes(al.shape) // 64, al, 0.0), axis=0, keepdims=True)
        alongs.append(al)
        amat = gram + (MEM - 1.0) * eye
        sq = jnp.sum(amat * amat, axis=0, keepdims=True)
        blk1 = lanes((1, 256)) // 64
        size = jnp.zeros((1, 256), F32)
        for i in range(4):
            total = jnp.sum(jnp.where(blk1 == i, sq, 0.0), axis=1, keepdims=True)
            size = jnp.where(blk1 == i, total, size)
        size = jnp.sqrt(size)
        sizes.append(size)
        ys.append(amat / size)
        zs.append(None)
    for it in range(NS_ITERS):
        mixers = []
        for g in range(4):
            yh, yl = split(ys[g])
            if it == 0:
                zy = ys[g]
            else:
                (zy,) = times([split(zs[g])], (block_diagonal(yh), block_diagonal(yl)))
            mixers.append(1.5 * eye - 0.5 * zy)
        for g in range(4):
            mh, ml = split(mixers[g])
            md = (block_diagonal(mh), block_diagonal(ml))
            if it == 0:
                (ys[g],) = times([split(ys[g])], md)
                zs[g] = mixers[g]
            elif it < NS_ITERS - 1:
                ys[g], zs[g] = times([split(ys[g]), split(zs[g])], md)
            else:
                (zs[g],) = times([split(zs[g])], md)
    eye2 = (lax.broadcasted_iota(jnp.int32, (MEM, 128), 0) == (lanes((MEM, 128)) & 63)).astype(F32)
    size0 = jnp.sqrt(jnp.full((1, 128), MEM * (MEM - 1.0) * (MEM - 1.0), F32))
    y0 = (MEM - 1.0) / size0
    z0 = jnp.ones((1, 128), F32)
    for it in range(NS_ITERS):
        m0 = 1.5 - 0.5 * z0 * y0
        y0, z0 = y0 * m0, m0 * z0
    empty = eye2 * (z0 * jnp.sqrt((MEM - 1.0) / size0))

    @pl.loop(0, N_LON)
    def _(o):
        held_ref[o] = empty

    half = lanes((MEM, 128)) // 64
    for g in range(4):
        zh, zl = split(zs[g])
        zd = (block_diagonal(zh), block_diagonal(zl))
        (first,) = times([split(jnp.broadcast_to(alongs[g], (16, 256)))], zd)
        (second,) = times([split(first)], zd)
        tt = zs[g] * jnp.sqrt((MEM - 1.0) / sizes[g]) + second[0:1] / sizes[g]
        th, tl = split(tt)
        thd, tld = block_diagonal(th), block_diagonal(tl)
        devs, means = [], []
        for i in range(4):
            x = last[pl.ds((g * 4 + i) * MEM, MEM), :]
            mean = jnp.sum(x, axis=0, keepdims=True) * (1.0 / MEM)
            devs.append(x - mean)
            means.append(mean)
        dh, dl = split(jnp.concatenate(devs, axis=0))
        ana = dot(thd, dh) + dot(tld, dh) + dot(thd, dl)
        for i in range(4):
            result[pl.ds((g * 4 + i) * MEM, MEM), :] = ana[i * MEM:(i + 1) * MEM] + means[i]
        turned = jnp.transpose(jnp.concatenate([tt, tt], axis=0))
        for i in range(4):
            p = g * 4 + i
            mine = owners_ref[0, p, 0]
            rank = jnp.int32(0)
            for q in range(p):
                rank = rank + (owners_ref[0, q, 0] == mine).astype(jnp.int32)
            held_ref[mine] = jnp.where(half == rank, turned[i * MEM:(i + 1) * MEM], held_ref[mine])

    @pl.loop(0, 16)
    def _(k):
        q, t = k // 8, k % 8
        cs = pl.ds(pl.multiple_of(q * 128, 128), 128)
        parts = [result[pl.ds(p * MEM + t * 8, 8), cs] for p in range(16)]
        for i, x in enumerate(butterfly(parts)):
            out_ref[pl.ds(t * 256 + q * 16 + i, 8, stride=32), :] = x


def analyse(states, cells, counts, values, errors, owners):
    vmem = pl.BlockSpec(memory_space=pltpu.VMEM)
    smem = pl.BlockSpec(memory_space=pltpu.SMEM)
    return pl.pallas_call(
        analysis_kernel,
        out_shape=(jax.ShapeDtypeStruct((MEM * LEV * ROWS, COLS), F32),
                   jax.ShapeDtypeStruct((N_LON, MEM, PCAP * MEM), F32)),
        in_specs=[vmem, vmem, smem, vmem, vmem, smem],
        out_specs=(vmem, vmem),
        scratch_shapes=[
            pltpu.VMEM((PATCH, 2 * MEM, 256), BF16),
            pltpu.VMEM((4, 256, SLOTS * OBS), BF16),
            pltpu.VMEM((SLOTS, PATCH, OBS), F32),
            pltpu.VMEM((PATCH * MEM, 256), F32),
            pltpu.VMEM((PATCH * MEM, 256), F32),
        ],
        compiler_params=pltpu.CompilerParams(vmem_limit_bytes=60 * 1024 * 1024),
        name="analysis",
    )(states, cells, counts, values, errors, owners)


def body(ensemble, courant_lon, courant_lat, diffusion, obs_cells, obs_counts, obs_values, obs_errors, owners):
    states = forecast(ensemble, courant_lon, courant_lat, diffusion)
    analysis, held = analyse(states, obs_cells, obs_counts, obs_values, obs_errors, owners)
    held = lax.all_to_all(held, "lon", split_axis=0, concat_axis=0, tiled=True)
    held = held.reshape(N_LON, MEM, PCAP, MEM).transpose(0, 2, 1, 3)
    return analysis.reshape(MEM, LEV, ROWS, COLS), held[None, None]


def solution(mesh):
    placed = (
        P(None, None, "lat", "lon"),
        P(None, "lat", "lon"),
        P(None, "lat", "lon"),
        P(None, "lat", "lon"),
        P(None, None, "lat", "lon", None),
        P(None, "lat", "lon"),
        P(None, "lat", "lon", None),
        P(None, "lat", "lon", None),
        P("lat", "lon", None),
    )
    return jax.shard_map(
        body,
        mesh=mesh,
        in_specs=placed,
        out_specs=(P(None, None, "lat", "lon"), P("lat", "lon", None, None, None, None)),
        check_vma=False,
    )
```

```python
import functools

import jax
import jax.numpy as jnp
from jax import lax
from jax.experimental import pallas as pl
from jax.experimental.pallas import tpu as pltpu
from jax.sharding import PartitionSpec as P

PCAP = 2
SLOTS = 4
STEPS = 3
NS_ITERS = 6
MEM = 64
LEV = 4
ROWS = 8
COLS = 128
PATCH = 16
OBS = 128
N_LAT = 8
N_LON = 16
F32 = jnp.float32
BF16 = jnp.bfloat16
NEIGHBOURS = ((-1, 0), (1, 0), (0, -1), (0, 1), (-1, -1), (-1, 1), (1, -1), (1, 1))
S_, N_, W_, E_, SW_, SE_, NW_, NE_ = range(8)


MESH = pl.DeviceIdType.MESH


def tile_to_device(row, col):
    return row - row % 2 + col % 2, col - col % 2 + row % 2


def swap_partner(lat, lon):
    swapping = (lat % 2 + lon % 2) % 2 == 1
    return swapping, (lat + 1 - 2 * (lat % 2), lon + 1 - 2 * (lon % 2))


def lanes(shape):
    return lax.broadcasted_iota(jnp.int32, shape, len(shape) - 1)


def forecast_kernel(ens_ref, cu_ref, cv_ref, dd_ref, *refs):
    obs_refs, (out_ref, *obs_outs), scratch = refs[:5], refs[5:11], refs[11:]
    forecast_body(ens_ref, cu_ref, cv_ref, dd_ref, obs_refs, out_ref, obs_outs, *scratch)


def forecast_body(ens_ref, cu_ref, cv_ref, dd_ref, obs_refs, out_ref, obs_outs,
                    tiles, coef_got, coefs, row_send, edge_send,
                    row_got, edge_got, corner_got,
                    load_sem, swap_sem, csend_sem, crecv_sem, hsend_sem, hrecv_sem):
    lat, lon = lax.axis_index("lat"), lax.axis_index("lon")
    trow, tcol = tile_to_device(lat, lon)

    def device_at(step):
        row = lax.rem(trow + step[0] + N_LAT, N_LAT)
        col = lax.rem(tcol + step[1] + N_LON, N_LON)
        return tile_to_device(row, col)

    barrier = pltpu.get_barrier_semaphore()
    for step in NEIGHBOURS:
        pl.semaphore_signal(barrier, inc=1, device_id=device_at(step),
                            device_id_type=MESH)
    swapping, partner = swap_partner(lat, lon)
    moves = [(ref, coef_got.at[8, i]) for i, ref in enumerate((cu_ref, cv_ref, dd_ref))]
    moves += [(ens_ref, tiles)] + list(zip(obs_refs, obs_outs))
    kept = [pltpu.make_async_copy(src, dst, load_sem.at[i]) for i, (src, dst) in enumerate(moves)]
    swapped = [
        pltpu.make_async_remote_copy(src_ref=src, dst_ref=dst, send_sem=load_sem.at[i], recv_sem=swap_sem.at[i],
                                     device_id=partner, device_id_type=MESH)
        for i, (src, dst) in enumerate(moves)]

    def arrive(first, last):
        @pl.when(swapping)
        def _():
            for copy in swapped[first:last]:
                copy.wait()

        @pl.when(jnp.logical_not(swapping))
        def _():
            for copy in kept[first:last]:
                copy.wait()

    pl.semaphore_wait(barrier, 8)

    @pl.when(swapping)
    def _():
        for copy in swapped:
            copy.start()

    @pl.when(jnp.logical_not(swapping))
    def _():
        for copy in kept:
            copy.start()

    arrive(0, 3)
    opposite = (N_, S_, E_, W_, NE_, NW_, SE_, SW_)
    ccopies = []
    for d, step in enumerate(NEIGHBOURS):
        copy = pltpu.make_async_remote_copy(
            src_ref=coef_got.at[8], dst_ref=coef_got.at[opposite[d]],
            send_sem=csend_sem.at[d], recv_sem=crecv_sem.at[opposite[d]],
            device_id=device_at(step), device_id_type=MESH)
        copy.start()
        ccopies.append(copy)
    arrive(3, 4)

    @pl.loop(0, LEV)
    def _(l):
        for r in range(ROWS):
            for t in range(8):
                out_ref[0, r, l, pl.ds(t * 8, 8), :] = tiles[pl.ds(t * 256 + l * ROWS + r, 8, stride=32), :]

    lane16 = lanes((16, COLS))
    lane1 = lanes((8, COLS))

    def send_halos(src, s):
        @pl.loop(0, MEM // 16)
        def _(t):
            ms = pl.ds(pl.multiple_of(t * 16, 16), 16)
            for r in range(ROWS):
                packed = out_ref[src, r, 0, ms, :]
                for l in range(1, LEV):
                    turned = pltpu.roll(out_ref[src, r, l, ms, :], l * 32, 1)
                    inside = ((lane16 + (16 - l * 32 + 128)) & 127) < 32
                    packed = jnp.where(inside, turned, packed)
                edge_send[s, r, ms, :] = packed.astype(BF16)
            for side, first in ((0, 0), (1, ROWS - 3)):
                for r in range(3):
                    for l in range(LEV):
                        row_send[s, side, r, l, ms, :] = out_ref[src, first + r, l, ms, :].astype(BF16)
        low, high = edge_send.at[s, pl.ds(0, 3)], edge_send.at[s, pl.ds(ROWS - 3, 3)]
        plan = (
            (S_, row_send.at[s, 0], row_got.at[s, 1], N_),
            (N_, row_send.at[s, 1], row_got.at[s, 0], S_),
            (W_, edge_send.at[s], edge_got.at[s, 1], E_),
            (E_, edge_send.at[s], edge_got.at[s, 0], W_),
            (SW_, low, corner_got.at[s, 3], NE_),
            (SE_, low, corner_got.at[s, 2], NW_),
            (NW_, high, corner_got.at[s, 1], SE_),
            (NE_, high, corner_got.at[s, 0], SW_),
        )
        copies = []
        for d, src_ref, dst_ref, landed in plan:
            copy = pltpu.make_async_remote_copy(
                src_ref=src_ref, dst_ref=dst_ref,
                send_sem=hsend_sem.at[s, d], recv_sem=hrecv_sem.at[s, landed],
                device_id=device_at(NEIGHBOURS[d]), device_id_type=MESH)
            copy.start()
            copies.append(copy)
        return copies

    copies = send_halos(0, 0)
    for copy in ccopies:
        copy.wait()
    south_ok = jnp.where(trow > 0, 1.0, 0.0).astype(F32)
    north_ok = jnp.where(trow < N_LAT - 1, 1.0, 0.0).astype(F32)
    lane8 = lanes((ROWS, COLS))
    for block, (cen, west, east, ok) in enumerate(((S_, SW_, SE_, south_ok), (8, W_, E_, None), (N_, NW_, NE_, north_ok))):
        for half in range(2):
            for l in range(LEV):
                def pick(i):
                    if half == 0:
                        return jnp.where(lane8 < 96, coef_got[cen, i, l], coef_got[west, i, l])
                    return jnp.where(lane8 >= 32, coef_got[cen, i, l], coef_got[east, i, l])
                cu, cv, dd = pick(0), pick(1), pick(2)
                aw = jnp.maximum(cu, 0.0) + dd
                ae = dd - jnp.minimum(cu, 0.0)
                as_ = jnp.maximum(cv, 0.0) + dd
                an = dd - jnp.minimum(cv, 0.0)
                ac = 1.0 - (jnp.abs(cu) + jnp.abs(cv) + 4.0 * dd)
                for j, a in enumerate((ac, aw, ae, as_, an)):
                    a = a if ok is None else a * ok
                    for r in ((6, 7), range(8), (0, 1))[block]:
                        coefs[half, l, j, block * 8 + r - 6] = jnp.broadcast_to(a[r:r + 1], (8, COLS))

    def step_row(half, l, r, south, v, north):
        ac, aw, ae, as_, an = (coefs[half, l, j, r] for j in range(5))
        return (ac * v + aw * pltpu.roll(v, 1, 1)) + (ae * pltpu.roll(v, COLS - 1, 1) + (as_ * south + an * north))

    for s in range(SLOTS):
        for copy in copies:
            copy.wait()
        prev = max(s - 1, 0)
        for l in range(LEV):
            @pl.loop(0, MEM // 16)
            def _(t):
                ms = pl.ds(pl.multiple_of(t * 16, 16), 16)
                mines, auxs = [], []
                for r in range(ROWS + 6):
                    if 3 <= r < ROWS + 3:
                        west, east = edge_got[s, 0, r - 3, ms, :], edge_got[s, 1, r - 3, ms, :]
                        mine, ok = out_ref[prev, r - 3, l, ms, :], None
                    else:
                        side, k, ok = (0, r, south_ok) if r < 3 else (1, r - ROWS - 3, north_ok)
                        west, east = corner_got[s, side * 2, k, ms, :], corner_got[s, side * 2 + 1, k, ms, :]
                        mine = row_got[s, side, k, l, ms, :].astype(F32) * ok
                    ring = jnp.where((lane16 & 31) >= 16, west.astype(F32), east.astype(F32))
                    if ok is not None:
                        ring = ring * ok
                    auxs.append(pltpu.roll(ring, 128 - l * 32, 1) if l else ring)
                    mines.append(mine)
                for u in range(2):
                    sub = slice(u * 8, u * 8 + 8)
                    sides = []
                    for half in range(2):
                        if half == 0:
                            v = [jnp.where(lane1 < 96, m[sub], a[sub]) for m, a in zip(mines, auxs)]
                        else:
                            v = [jnp.where(lane1 >= 32, m[sub], a[sub]) for m, a in zip(mines, auxs)]
                        for step in range(STEPS):
                            v = [step_row(half, l, r + step, v[r], v[r + 1], v[r + 2]) for r in range(len(v) - 2)]
                        sides.append(v)
                    for r in range(ROWS):
                        out_ref[s, r, l, pl.ds(pl.multiple_of(t * 16 + u * 8, 8), 8), :] = jnp.where(
                            lane1 < 64, sides[0][r], sides[1][r])
        if s < SLOTS - 1:
            copies = send_halos(s, s + 1)
    arrive(4, 9)


def forecast(ensemble, cu, cv, dd, *obs):
    anyspec = pl.BlockSpec(memory_space=pl.ANY)
    return pl.pallas_call(
        forecast_kernel,
        out_shape=(jax.ShapeDtypeStruct((SLOTS, ROWS, LEV, MEM, COLS), F32),
                   *(jax.ShapeDtypeStruct(x.shape, x.dtype) for x in obs)),
        in_specs=[anyspec] * 9,
        out_specs=(pl.BlockSpec(memory_space=pltpu.VMEM), *([anyspec] * 5)),
        scratch_shapes=[
            pltpu.VMEM((MEM * LEV * ROWS, COLS), F32),
            pltpu.VMEM((9, 3, LEV, ROWS, COLS), F32),
            pltpu.VMEM((2, LEV, 5, 12, 8, COLS), F32),
            pltpu.VMEM((SLOTS, 2, 3, LEV, MEM, COLS), BF16),
            pltpu.VMEM((SLOTS, ROWS, MEM, COLS), BF16),
            pltpu.VMEM((SLOTS, 2, 3, LEV, MEM, COLS), BF16),
            pltpu.VMEM((SLOTS, 2, ROWS, MEM, COLS), BF16),
            pltpu.VMEM((SLOTS, 4, 3, MEM, COLS), BF16),
            pltpu.SemaphoreType.DMA((9,)),
            pltpu.SemaphoreType.DMA((9,)),
            pltpu.SemaphoreType.DMA((8,)),
            pltpu.SemaphoreType.DMA((8,)),
            pltpu.SemaphoreType.DMA((SLOTS, 8)),
            pltpu.SemaphoreType.DMA((SLOTS, 8)),
        ],
        compiler_params=pltpu.CompilerParams(
            collective_id=0, has_side_effects=True, vmem_limit_bytes=60 * 1024 * 1024),
        name="forecast",
    )(ensemble.reshape(MEM * LEV * ROWS, COLS), cu, cv, dd, *obs)


def butterfly(parts):
    parts = list(parts)
    lane = lanes(parts[0].shape)
    for bit in (1, 2, 4, 8):
        keep = (lane & (8 * bit)) == 0
        for i in range(16):
            if i & bit:
                continue
            a, b = parts[i], parts[i + bit]
            parts[i] = jnp.where(keep, a, pltpu.roll(b, 8 * bit, 1))
            parts[i + bit] = jnp.where(keep, pltpu.roll(a, 128 - 8 * bit, 1), b)
    return parts


def split(x):
    hi = x.astype(BF16)
    return hi, (x - hi.astype(F32)).astype(BF16)


def dot(a, b):
    return jnp.dot(a, b, preferred_element_type=F32)


def dot_t(a, b):
    return lax.dot_general(a, b, (((1,), (1,)), ((), ())), preferred_element_type=F32)


def block_diagonal(x):
    block = lanes(x.shape) // 64
    return jnp.concatenate([jnp.where(block == i, x, jnp.zeros_like(x)) for i in range(4)], axis=0)


def times(x_parts, y_parts):
    yh, yl = y_parts
    n = sum(h.shape[0] for h, _ in x_parts)
    his = [h for h, _ in x_parts]
    los = [l for _, l in x_parts]
    top = dot(jnp.concatenate(his + los, axis=0), yh)
    low = dot(jnp.concatenate(his, axis=0), yl)
    total = top[:n] + top[n:] + low
    outs, at = [], 0
    for h, _ in x_parts:
        outs.append(total[at:at + h.shape[0]])
        at += h.shape[0]
    return outs


def analysis_kernel(state_ref, cells_ref, counts_ref, values_ref, errors_ref, owners_ref,
                    out_ref, held_ref, xs, perts, innovs, last, result):
    def patchwise(slot, write):
        @pl.loop(0, 8)
        def _(k):
            q, t = k // 4, k % 4
            halves = []
            for u in range(2):
                ms = pl.ds(t * 16 + u * 8, 8)
                parts = [state_ref[slot, i % 8, q * 2 + i // 8, ms, :] for i in range(16)]
                halves.append(butterfly(parts))
            for p in range(16):
                write(q, t, p, jnp.concatenate([halves[0][p], halves[1][p]], axis=0))

    cell_id = lax.broadcasted_iota(jnp.int32, (256, OBS), 0).astype(F32).astype(BF16)
    one, zero = jnp.ones((256, OBS), BF16), jnp.zeros((256, OBS), BF16)
    for slot in range(SLOTS):
        def write(q, t, p, x):
            hi, lo = split(x)
            cs = pl.ds(pl.multiple_of(q * 128, 128), 128)
            xs[p, pl.ds(t * 16, 16), cs] = hi
            xs[p, pl.ds(MEM + t * 16, 16), cs] = lo
            if slot == SLOTS - 1:
                last[pl.ds(p * MEM + t * 16, 16), cs] = x
        patchwise(slot, write)

        @pl.loop(0, PATCH)
        def _(p):
            w = zero
            for corner in range(4):
                idx = cells_ref[slot, corner, 0, pl.ds(p, 1), :].astype(F32)
                idx = jnp.broadcast_to(idx, (256, OBS)).astype(BF16)
                w = w + jnp.where(cell_id == idx, one, zero)
            both = dot(xs[p], w)
            equivalent = 0.25 * (both[:MEM] + both[MEM:])
            mean = jnp.sum(equivalent, axis=0, keepdims=True) * (1.0 / MEM)
            live = lanes((1, OBS)) < counts_ref[slot, 0, p]
            weight = jnp.where(live, 1.0 / errors_ref[slot, 0, pl.ds(p, 1), :], 0.0)
            pert = ((equivalent - mean) * weight).astype(BF16)
            perts[p // 4, pl.ds((p % 4) * MEM, MEM), slot * OBS:(slot + 1) * OBS] = pert
            innovs[slot, pl.ds(p, 1), :] = (values_ref[slot, 0, pl.ds(p, 1), :] - mean) * weight

    shape = (MEM, 256)
    block = lanes(shape) // 64
    eye = (lax.broadcasted_iota(jnp.int32, shape, 0) == (lanes(shape) & 63)).astype(F32)
    innov = jnp.concatenate([innovs[s] for s in range(SLOTS)], axis=1).astype(BF16)
    ys, zs, alongs, sizes = [], [], [], []
    for g in range(4):
        pg = perts[g]
        full = dot_t(pg, pg)
        gram = full[0:MEM]
        for i in range(1, 4):
            gram = jnp.where(block == i, full[i * MEM:(i + 1) * MEM], gram)
        al = dot_t(innov, pg)
        row = lax.broadcasted_iota(jnp.int32, al.shape, 0)
        al = jnp.sum(jnp.where(row == g * 4 + lanes(al.shape) // 64, al, 0.0), axis=0, keepdims=True)
        alongs.append(al)
        amat = gram + (MEM - 1.0) * eye
        sq = jnp.sum(amat * amat, axis=0, keepdims=True)
        blk1 = lanes((1, 256)) // 64
        size = jnp.zeros((1, 256), F32)
        for i in range(4):
            total = jnp.sum(jnp.where(blk1 == i, sq, 0.0), axis=1, keepdims=True)
            size = jnp.where(blk1 == i, total, size)
        size = jnp.sqrt(size)
        sizes.append(size)
        ys.append(amat / size)
        zs.append(None)
    for it in range(NS_ITERS):
        mixers = []
        for g in range(4):
            yh, yl = split(ys[g])
            if it == 0:
                zy = ys[g]
            else:
                (zy,) = times([split(zs[g])], (block_diagonal(yh), block_diagonal(yl)))
            mixers.append(1.5 * eye - 0.5 * zy)
        for g in range(4):
            mh, ml = split(mixers[g])
            md = (block_diagonal(mh), block_diagonal(ml))
            if it == 0:
                (ys[g],) = times([split(ys[g])], md)
                zs[g] = mixers[g]
            elif it < NS_ITERS - 1:
                ys[g], zs[g] = times([split(ys[g]), split(zs[g])], md)
            else:
                (zs[g],) = times([split(zs[g])], md)
    eye2 = (lax.broadcasted_iota(jnp.int32, (MEM, 128), 0) == (lanes((MEM, 128)) & 63)).astype(F32)
    size0 = jnp.sqrt(jnp.full((1, 128), MEM * (MEM - 1.0) * (MEM - 1.0), F32))
    y0 = (MEM - 1.0) / size0
    z0 = jnp.ones((1, 128), F32)
    for it in range(NS_ITERS):
        m0 = 1.5 - 0.5 * z0 * y0
        y0, z0 = y0 * m0, m0 * z0
    empty = eye2 * (z0 * jnp.sqrt((MEM - 1.0) / size0))

    @pl.loop(0, N_LON)
    def _(o):
        held_ref[o] = empty

    half = lanes((MEM, 128)) // 64
    for g in range(4):
        zh, zl = split(zs[g])
        zd = (block_diagonal(zh), block_diagonal(zl))
        (first,) = times([split(jnp.broadcast_to(alongs[g], (16, 256)))], zd)
        (second,) = times([split(first)], zd)
        tt = zs[g] * jnp.sqrt((MEM - 1.0) / sizes[g]) + second[0:1] / sizes[g]
        th, tl = split(tt)
        thd, tld = block_diagonal(th), block_diagonal(tl)
        devs, means = [], []
        for i in range(4):
            x = last[pl.ds((g * 4 + i) * MEM, MEM), :]
            mean = jnp.sum(x, axis=0, keepdims=True) * (1.0 / MEM)
            devs.append(x - mean)
            means.append(mean)
        dh, dl = split(jnp.concatenate(devs, axis=0))
        ana = dot(thd, dh) + dot(tld, dh) + dot(thd, dl)
        for i in range(4):
            result[pl.ds((g * 4 + i) * MEM, MEM), :] = ana[i * MEM:(i + 1) * MEM] + means[i]
        turned = jnp.transpose(jnp.concatenate([tt, tt], axis=0))
        for i in range(4):
            p = g * 4 + i
            mine = owners_ref[0, p, 0]
            rank = jnp.int32(0)
            for q in range(p):
                rank = rank + (owners_ref[0, q, 0] == mine).astype(jnp.int32)
            held_ref[mine] = jnp.where(half == rank, turned[i * MEM:(i + 1) * MEM], held_ref[mine])

    @pl.loop(0, 16)
    def _(k):
        q, t = k // 8, k % 8
        cs = pl.ds(pl.multiple_of(q * 128, 128), 128)
        parts = [result[pl.ds(p * MEM + t * 8, 8), cs] for p in range(16)]
        for i, x in enumerate(butterfly(parts)):
            out_ref[pl.ds(t * 256 + q * 16 + i, 8, stride=32), :] = x


def analyse(states, cells, counts, values, errors, owners):
    vmem = pl.BlockSpec(memory_space=pltpu.VMEM)
    smem = pl.BlockSpec(memory_space=pltpu.SMEM)
    return pl.pallas_call(
        analysis_kernel,
        out_shape=(jax.ShapeDtypeStruct((MEM * LEV * ROWS, COLS), F32),
                   jax.ShapeDtypeStruct((N_LON, MEM, PCAP * MEM), F32)),
        in_specs=[vmem, vmem, smem, vmem, vmem, smem],
        out_specs=(vmem, vmem),
        scratch_shapes=[
            pltpu.VMEM((PATCH, 2 * MEM, 256), BF16),
            pltpu.VMEM((4, 256, SLOTS * OBS), BF16),
            pltpu.VMEM((SLOTS, PATCH, OBS), F32),
            pltpu.VMEM((PATCH * MEM, 256), F32),
            pltpu.VMEM((PATCH * MEM, 256), F32),
        ],
        compiler_params=pltpu.CompilerParams(vmem_limit_bytes=60 * 1024 * 1024),
        name="analysis",
    )(states, cells, counts, values, errors, owners)


def deliver_kernel(ana_ref, held_ref, ana_out, held_out, send_sem, recv_sem):
    lat, lon = lax.axis_index("lat"), lax.axis_index("lon")
    trow, tcol = tile_to_device(lat, lon)
    swapping, partner = swap_partner(lat, lon)
    barrier = pltpu.get_barrier_semaphore()

    def greet(device):
        pl.semaphore_signal(barrier, inc=1, device_id=device, device_id_type=MESH)

    for k in range(1, N_LON):
        greet(tile_to_device(lat, lax.rem(tcol + k, N_LON)))

    @pl.when(swapping)
    def _():
        greet(tile_to_device(lat, tcol))
        greet(partner)

    pl.semaphore_wait(barrier, jnp.where(swapping, N_LON + 1, N_LON - 1))
    owner = [lax.rem(lon + k, N_LON) for k in range(N_LON)]
    sends = [
        pltpu.make_async_remote_copy(
            src_ref=held_ref.at[owner[k]], dst_ref=held_out.at[tcol], send_sem=send_sem.at[k], recv_sem=recv_sem.at[tcol],
            device_id=(trow, owner[k]), device_id_type=MESH)
        for k in range(N_LON)]

    def landed(k):
        source = lax.rem(tcol + k, N_LON)
        pltpu.make_async_remote_copy(
            src_ref=held_ref.at[0], dst_ref=held_out.at[source], send_sem=send_sem.at[k], recv_sem=recv_sem.at[source],
            device_id=(trow, owner[k]), device_id_type=MESH).wait_recv()

    keep = pltpu.make_async_copy(held_ref.at[lon], held_out.at[tcol], send_sem.at[0])
    swap = pltpu.make_async_remote_copy(
        src_ref=ana_ref, dst_ref=ana_out, send_sem=send_sem.at[N_LON], recv_sem=recv_sem.at[N_LON],
        device_id=partner, device_id_type=MESH)

    @pl.when(swapping)
    def _():
        swap.start()
        sends[0].start()

    @pl.when(jnp.logical_not(swapping))
    def _():
        keep.start()

    for copy in sends[1:]:
        copy.start()
    for k in range(1, N_LON):
        sends[k].wait_send()
        landed(k)

    @pl.when(swapping)
    def _():
        sends[0].wait_send()
        landed(0)
        swap.wait()

    @pl.when(jnp.logical_not(swapping))
    def _():
        keep.wait()


def deliver(analysis, held):
    anyspec = pl.BlockSpec(memory_space=pl.ANY)
    return pl.pallas_call(
        deliver_kernel,
        out_shape=(jax.ShapeDtypeStruct(analysis.shape, F32), jax.ShapeDtypeStruct(held.shape, F32)),
        in_specs=[anyspec] * 2,
        out_specs=(anyspec, anyspec),
        scratch_shapes=[pltpu.SemaphoreType.DMA((N_LON + 1,)), pltpu.SemaphoreType.DMA((N_LON + 1,))],
        compiler_params=pltpu.CompilerParams(collective_id=1, has_side_effects=True),
        name="deliver",
    )(analysis, held)


def body(ensemble, courant_lon, courant_lat, diffusion, obs_cells, obs_counts, obs_values, obs_errors, owners):
    states, *obs = forecast(ensemble, courant_lon, courant_lat, diffusion,
                            obs_cells, obs_counts, obs_values, obs_errors, owners)
    analysis, held = analyse(states, *obs)
    swapping, _ = swap_partner(lax.axis_index("lat"), lax.axis_index("lon"))
    got, held = deliver(analysis, held)
    analysis = jnp.where(swapping, got, analysis)
    held = held.reshape(N_LON, MEM, PCAP, MEM).transpose(0, 2, 1, 3)
    return analysis.reshape(MEM, LEV, ROWS, COLS), held[None, None]


def solution(mesh):
    placed = (
        P(None, None, "lat", "lon"),
        P(None, "lat", "lon"),
        P(None, "lat", "lon"),
        P(None, "lat", "lon"),
        P(None, None, "lat", "lon", None),
        P(None, "lat", "lon"),
        P(None, "lat", "lon", None),
        P(None, "lat", "lon", None),
        P("lat", "lon", None),
    )
    return jax.shard_map(
        body,
        mesh=mesh,
        in_specs=placed,
        out_specs=(P(None, None, "lat", "lon"), P("lat", "lon", None, None, None, None)),
        check_vma=False,
    )
```

```python
import functools

import jax
import jax.numpy as jnp
from jax import lax
from jax.experimental import pallas as pl
from jax.experimental.pallas import tpu as pltpu
from jax.sharding import PartitionSpec as P

PCAP = 2
SLOTS = 4
STEPS = 3
NS_ITERS = 6
MEM = 64
LEV = 4
ROWS = 8
COLS = 128
PATCH = 16
OBS = 128
N_LAT = 8
N_LON = 16
F32 = jnp.float32
BF16 = jnp.bfloat16
NEIGHBOURS = ((-1, 0), (1, 0), (0, -1), (0, 1), (-1, -1), (-1, 1), (1, -1), (1, 1))
S_, N_, W_, E_, SW_, SE_, NW_, NE_ = range(8)


MESH = pl.DeviceIdType.MESH


def tile_to_device(row, col):
    return row - row % 2 + col % 2, col - col % 2 + row % 2


def swap_partner(lat, lon):
    swapping = (lat % 2 + lon % 2) % 2 == 1
    return swapping, (lat + 1 - 2 * (lat % 2), lon + 1 - 2 * (lon % 2))


def lanes(shape):
    return lax.broadcasted_iota(jnp.int32, shape, len(shape) - 1)


CODE = 32767.0


def peaks_of(ref):
    def grow(m, peak):
        return jnp.maximum(peak, jnp.abs(ref[pl.ds(pl.multiple_of(m * 32, 32), 32), :]))
    return jnp.maximum(lax.fori_loop(0, MEM, grow, jnp.zeros((32, COLS), F32), unroll=8), 1e-30)


def encode(ref, peaks, code_ref, chunk):
    factor = CODE / peaks

    @pl.loop(chunk * 16, chunk * 16 + 16, unroll=4)
    def _(m):
        at = pl.ds(pl.multiple_of(m * 32, 32), 32)
        code_ref[at, :] = jnp.round(ref[at, :] * factor).astype(jnp.int32).astype(jnp.int16)


def forecast_kernel(ens_ref, cu_ref, cv_ref, dd_ref, *refs):
    obs_refs, (out_ref, *obs_outs), scratch = refs[:5], refs[5:11], refs[11:]
    forecast_body(ens_ref, cu_ref, cv_ref, dd_ref, obs_refs, out_ref, obs_outs, *scratch)


def forecast_body(ens_ref, cu_ref, cv_ref, dd_ref, obs_refs, out_ref, obs_outs,
                    tiles, coef_got, coefs, row_send, ring_send, edge_send,
                    row_got, edge_got, corner_got,
                    load_sem, swap_sem, code_send, code_got, peak_send, peak_got, code_sem, csend_sem, crecv_sem, hsend_sem, hrecv_sem):
    lat, lon = lax.axis_index("lat"), lax.axis_index("lon")
    trow, tcol = tile_to_device(lat, lon)

    def device_at(step):
        row = lax.rem(trow + step[0] + N_LAT, N_LAT)
        col = lax.rem(tcol + step[1] + N_LON, N_LON)
        return tile_to_device(row, col)

    barrier = pltpu.get_barrier_semaphore()
    for step in NEIGHBOURS:
        pl.semaphore_signal(barrier, inc=1, device_id=device_at(step),
                            device_id_type=MESH)
    swapping, partner = swap_partner(lat, lon)
    moves = [(ref, coef_got.at[8, i]) for i, ref in enumerate((cu_ref, cv_ref, dd_ref))]
    moves += list(zip(obs_refs, obs_outs))
    load = pltpu.make_async_copy(ens_ref, tiles, load_sem.at[8])
    load.start()
    rows = MEM * LEV * ROWS // 4
    sent = [
        pltpu.make_async_remote_copy(src_ref=src, dst_ref=dst, send_sem=code_sem.at[0, i], recv_sem=code_sem.at[1, i],
                                     device_id=partner, device_id_type=MESH)
        for i, (src, dst) in enumerate(
            [(code_send.at[pl.ds(c * rows, rows)], code_got.at[pl.ds(c * rows, rows)]) for c in range(4)]
            + [(peak_send, peak_got)])]
    kept = [pltpu.make_async_copy(src, dst, load_sem.at[i]) for i, (src, dst) in enumerate(moves)]
    swapped = [
        pltpu.make_async_remote_copy(src_ref=src, dst_ref=dst, send_sem=load_sem.at[i], recv_sem=swap_sem.at[i],
                                     device_id=partner, device_id_type=MESH)
        for i, (src, dst) in enumerate(moves)]

    def arrive(first, last):
        @pl.when(swapping)
        def _():
            for copy in swapped[first:last]:
                copy.wait()

        @pl.when(jnp.logical_not(swapping))
        def _():
            for copy in kept[first:last]:
                copy.wait()

    pl.semaphore_wait(barrier, 8)

    @pl.when(swapping)
    def _():
        for copy in swapped[:3]:
            copy.start()
        load.wait()
        peaks = peaks_of(tiles)
        peak_send[...] = peaks
        sent[4].start()
        for c in range(4):
            encode(tiles, peaks, code_send, c)
            sent[c].start()
        for copy in swapped[3:]:
            copy.start()
        sent[4].wait()
        peaks = peak_got[...]
        for c in range(4):
            sent[c].wait()

            @pl.loop(c * 16, c * 16 + 16)
            def _(m):
                at = pl.ds(pl.multiple_of(m * 32, 32), 32)
                tiles[at, :] = code_got[at, :].astype(jnp.int32).astype(F32) * (peaks * (1.0 / CODE))

    @pl.when(jnp.logical_not(swapping))
    def _():
        for copy in kept:
            copy.start()
        load.wait()

    arrive(0, 3)
    opposite = (N_, S_, E_, W_, NE_, NW_, SE_, SW_)
    ccopies = []
    for d, step in enumerate(NEIGHBOURS):
        copy = pltpu.make_async_remote_copy(
            src_ref=coef_got.at[8], dst_ref=coef_got.at[opposite[d]],
            send_sem=csend_sem.at[d], recv_sem=crecv_sem.at[opposite[d]],
            device_id=device_at(step), device_id_type=MESH)
        copy.start()
        ccopies.append(copy)

    @pl.loop(0, LEV)
    def _(l):
        for r in range(ROWS):
            for t in range(8):
                out_ref[0, r, l, pl.ds(t * 8, 8), :] = tiles[pl.ds(t * 256 + l * ROWS + r, 8, stride=32), :]

    lane16 = lanes((16, COLS))
    lane1 = lanes((8, COLS))

    def send_halos(src, s):
        @pl.loop(0, MEM // 16)
        def _(t):
            ms = pl.ds(pl.multiple_of(t * 16, 16), 16)
            rings = []
            for half in range(2):
                ring = out_ref[src, half * 4, 0, ms, :]
                for k in range(1, 16):
                    turned = pltpu.roll(out_ref[src, half * 4 + k // LEV, k % LEV, ms, :], k * 8, 1)
                    inside = ((lane16 + (4 - k * 8 + 128)) & 127) < 8
                    ring = jnp.where(inside, turned, ring)
                ring_send[s, half, ms, :] = ring.astype(BF16)
                rings.append(ring)
            edge_send[s, 0, ms, :] = jnp.where((lane16 & 7) < 4, rings[0], pltpu.roll(rings[1], 4, 1)).astype(BF16)
            edge_send[s, 1, ms, :] = jnp.where((lane16 & 7) >= 4, rings[0], pltpu.roll(rings[1], 124, 1)).astype(BF16)
            for side, first in ((0, 0), (1, ROWS - 3)):
                for r in range(3):
                    for l in range(LEV):
                        row_send[s, side, r, l, ms, :] = out_ref[src, first + r, l, ms, :].astype(BF16)
        low, high = ring_send.at[s, 0], ring_send.at[s, 1]
        plan = (
            (S_, row_send.at[s, 0], row_got.at[s, 1], N_),
            (N_, row_send.at[s, 1], row_got.at[s, 0], S_),
            (W_, edge_send.at[s, 0], edge_got.at[s, 1], E_),
            (E_, edge_send.at[s, 1], edge_got.at[s, 0], W_),
            (SW_, low, corner_got.at[s, 3], NE_),
            (SE_, low, corner_got.at[s, 2], NW_),
            (NW_, high, corner_got.at[s, 1], SE_),
            (NE_, high, corner_got.at[s, 0], SW_),
        )
        copies = []
        for d, src_ref, dst_ref, landed in plan:
            copy = pltpu.make_async_remote_copy(
                src_ref=src_ref, dst_ref=dst_ref,
                send_sem=hsend_sem.at[s, d], recv_sem=hrecv_sem.at[s, landed],
                device_id=device_at(NEIGHBOURS[d]), device_id_type=MESH)
            copy.start()
            copies.append(copy)
        return copies

    copies = send_halos(0, 0)
    for copy in ccopies:
        copy.wait()
    south_ok = jnp.where(trow > 0, 1.0, 0.0).astype(F32)
    north_ok = jnp.where(trow < N_LAT - 1, 1.0, 0.0).astype(F32)
    lane8 = lanes((ROWS, COLS))
    for block, (cen, west, east, ok) in enumerate(((S_, SW_, SE_, south_ok), (8, W_, E_, None), (N_, NW_, NE_, north_ok))):
        for half in range(2):
            for l in range(LEV):
                def pick(i):
                    if half == 0:
                        return jnp.where(lane8 < 96, coef_got[cen, i, l], coef_got[west, i, l])
                    return jnp.where(lane8 >= 32, coef_got[cen, i, l], coef_got[east, i, l])
                cu, cv, dd = pick(0), pick(1), pick(2)
                aw = jnp.maximum(cu, 0.0) + dd
                ae = dd - jnp.minimum(cu, 0.0)
                as_ = jnp.maximum(cv, 0.0) + dd
                an = dd - jnp.minimum(cv, 0.0)
                ac = 1.0 - (jnp.abs(cu) + jnp.abs(cv) + 4.0 * dd)
                for j, a in enumerate((ac, aw, ae, as_, an)):
                    a = a if ok is None else a * ok
                    for r in ((6, 7), range(8), (0, 1))[block]:
                        coefs[half, l, j, block * 8 + r - 6] = jnp.broadcast_to(a[r:r + 1], (8, COLS))

    def step_row(half, l, r, south, v, north):
        ac, aw, ae, as_, an = (coefs[half, l, j, r] for j in range(5))
        return (ac * v + aw * pltpu.roll(v, 1, 1)) + (ae * pltpu.roll(v, COLS - 1, 1) + (as_ * south + an * north))

    for s in range(SLOTS):
        for copy in copies:
            copy.wait()
        prev = max(s - 1, 0)
        for l in range(LEV):
            @pl.loop(0, MEM // 16)
            def _(t):
                ms = pl.ds(pl.multiple_of(t * 16, 16), 16)
                west, east = edge_got[s, 0, ms, :].astype(F32), edge_got[s, 1, ms, :].astype(F32)
                first = (lane16 & 7) < 4
                rings = [
                    jnp.where(first, corner_got[s, 1, ms, :].astype(F32), corner_got[s, 0, ms, :].astype(F32)) * south_ok,
                    jnp.where(first, east, west),
                    jnp.where(first, pltpu.roll(east, 124, 1), pltpu.roll(west, 4, 1)),
                    jnp.where(first, corner_got[s, 3, ms, :].astype(F32), corner_got[s, 2, ms, :].astype(F32)) * north_ok,
                ]
                mines, auxs = [], []
                for r in range(-3, ROWS + 3):
                    if 0 <= r < ROWS:
                        mine = out_ref[prev, r, l, ms, :]
                    elif r < 0:
                        mine = row_got[s, 0, r + 3, l, ms, :].astype(F32) * south_ok
                    else:
                        mine = row_got[s, 1, r - ROWS, l, ms, :].astype(F32) * north_ok
                    turn = (((r + 4) % 4) * LEV + l) * 8
                    ring = rings[(r + 4) // 4]
                    auxs.append(pltpu.roll(ring, 128 - turn, 1) if turn else ring)
                    mines.append(mine)
                for u in range(2):
                    sub = slice(u * 8, u * 8 + 8)
                    sides = []
                    for half in range(2):
                        if half == 0:
                            v = [jnp.where(lane1 < 96, m[sub], a[sub]) for m, a in zip(mines, auxs)]
                        else:
                            v = [jnp.where(lane1 >= 32, m[sub], a[sub]) for m, a in zip(mines, auxs)]
                        for step in range(STEPS):
                            v = [step_row(half, l, r + step, v[r], v[r + 1], v[r + 2]) for r in range(len(v) - 2)]
                        sides.append(v)
                    for r in range(ROWS):
                        out_ref[s, r, l, pl.ds(pl.multiple_of(t * 16 + u * 8, 8), 8), :] = jnp.where(
                            lane1 < 64, sides[0][r], sides[1][r])
        if s < SLOTS - 1:
            copies = send_halos(s, s + 1)
    arrive(3, 8)


def forecast(ensemble, cu, cv, dd, *obs):
    anyspec = pl.BlockSpec(memory_space=pl.ANY)
    return pl.pallas_call(
        forecast_kernel,
        out_shape=(jax.ShapeDtypeStruct((SLOTS, ROWS, LEV, MEM, COLS), F32),
                   *(jax.ShapeDtypeStruct(x.shape, x.dtype) for x in obs)),
        in_specs=[anyspec] * 9,
        out_specs=(pl.BlockSpec(memory_space=pltpu.VMEM), *([anyspec] * 5)),
        scratch_shapes=[
            pltpu.VMEM((MEM * LEV * ROWS, COLS), F32),
            pltpu.VMEM((9, 3, LEV, ROWS, COLS), F32),
            pltpu.VMEM((2, LEV, 5, 12, 8, COLS), F32),
            pltpu.VMEM((SLOTS, 2, 3, LEV, MEM, COLS), BF16),
            pltpu.VMEM((SLOTS, 2, MEM, COLS), BF16),
            pltpu.VMEM((SLOTS, 2, MEM, COLS), BF16),
            pltpu.VMEM((SLOTS, 2, 3, LEV, MEM, COLS), BF16),
            pltpu.VMEM((SLOTS, 2, MEM, COLS), BF16),
            pltpu.VMEM((SLOTS, 4, MEM, COLS), BF16),
            pltpu.SemaphoreType.DMA((9,)),
            pltpu.SemaphoreType.DMA((9,)),
            pltpu.VMEM((MEM * LEV * ROWS, COLS), jnp.int16),
            pltpu.VMEM((MEM * LEV * ROWS, COLS), jnp.int16),
            pltpu.VMEM((LEV * ROWS, COLS), F32),
            pltpu.VMEM((LEV * ROWS, COLS), F32),
            pltpu.SemaphoreType.DMA((2, 5)),
            pltpu.SemaphoreType.DMA((8,)),
            pltpu.SemaphoreType.DMA((8,)),
            pltpu.SemaphoreType.DMA((SLOTS, 8)),
            pltpu.SemaphoreType.DMA((SLOTS, 8)),
        ],
        compiler_params=pltpu.CompilerParams(
            collective_id=0, has_side_effects=True, vmem_limit_bytes=60 * 1024 * 1024),
        name="forecast",
    )(ensemble.reshape(MEM * LEV * ROWS, COLS), cu, cv, dd, *obs)


def butterfly(parts):
    parts = list(parts)
    lane = lanes(parts[0].shape)
    for bit in (1, 2, 4, 8):
        keep = (lane & (8 * bit)) == 0
        for i in range(16):
            if i & bit:
                continue
            a, b = parts[i], parts[i + bit]
            parts[i] = jnp.where(keep, a, pltpu.roll(b, 8 * bit, 1))
            parts[i + bit] = jnp.where(keep, pltpu.roll(a, 128 - 8 * bit, 1), b)
    return parts


def split(x):
    hi = x.astype(BF16)
    return hi, (x - hi.astype(F32)).astype(BF16)


def dot(a, b):
    return jnp.dot(a, b, preferred_element_type=F32)


def dot_t(a, b):
    return lax.dot_general(a, b, (((1,), (1,)), ((), ())), preferred_element_type=F32)


def block_diagonal(x):
    block = lanes(x.shape) // 64
    return jnp.concatenate([jnp.where(block == i, x, jnp.zeros_like(x)) for i in range(4)], axis=0)


def times(x_parts, y_parts):
    yh, yl = y_parts
    n = sum(h.shape[0] for h, _ in x_parts)
    his = [h for h, _ in x_parts]
    los = [l for _, l in x_parts]
    top = dot(jnp.concatenate(his + los, axis=0), yh)
    low = dot(jnp.concatenate(his, axis=0), yl)
    total = top[:n] + top[n:] + low
    outs, at = [], 0
    for h, _ in x_parts:
        outs.append(total[at:at + h.shape[0]])
        at += h.shape[0]
    return outs


def analysis_kernel(state_ref, cells_ref, counts_ref, values_ref, errors_ref, owners_ref,
                    out_ref, code_ref, peak_ref, held_ref, xs, perts, innovs, last, result):
    def patchwise(slot, write):
        @pl.loop(0, 8)
        def _(k):
            q, t = k // 4, k % 4
            halves = []
            for u in range(2):
                ms = pl.ds(t * 16 + u * 8, 8)
                parts = [state_ref[slot, i % 8, q * 2 + i // 8, ms, :] for i in range(16)]
                halves.append(butterfly(parts))
            for p in range(16):
                write(q, t, p, jnp.concatenate([halves[0][p], halves[1][p]], axis=0))

    cell_id = lax.broadcasted_iota(jnp.int32, (256, OBS), 0).astype(F32).astype(BF16)
    one, zero = jnp.ones((256, OBS), BF16), jnp.zeros((256, OBS), BF16)
    for slot in range(SLOTS):
        def write(q, t, p, x):
            hi, lo = split(x)
            cs = pl.ds(pl.multiple_of(q * 128, 128), 128)
            xs[p, pl.ds(t * 16, 16), cs] = hi
            xs[p, pl.ds(MEM + t * 16, 16), cs] = lo
            if slot == SLOTS - 1:
                last[pl.ds(p * MEM + t * 16, 16), cs] = x
        patchwise(slot, write)

        @pl.loop(0, PATCH)
        def _(p):
            w = zero
            for corner in range(4):
                idx = cells_ref[slot, corner, 0, pl.ds(p, 1), :].astype(F32)
                idx = jnp.broadcast_to(idx, (256, OBS)).astype(BF16)
                w = w + jnp.where(cell_id == idx, one, zero)
            both = dot(xs[p], w)
            equivalent = 0.25 * (both[:MEM] + both[MEM:])
            mean = jnp.sum(equivalent, axis=0, keepdims=True) * (1.0 / MEM)
            live = lanes((1, OBS)) < counts_ref[slot, 0, p]
            weight = jnp.where(live, 1.0 / errors_ref[slot, 0, pl.ds(p, 1), :], 0.0)
            pert = ((equivalent - mean) * weight).astype(BF16)
            perts[p // 4, pl.ds((p % 4) * MEM, MEM), slot * OBS:(slot + 1) * OBS] = pert
            innovs[slot, pl.ds(p, 1), :] = (values_ref[slot, 0, pl.ds(p, 1), :] - mean) * weight

    shape = (MEM, 256)
    block = lanes(shape) // 64
    eye = (lax.broadcasted_iota(jnp.int32, shape, 0) == (lanes(shape) & 63)).astype(F32)
    innov = jnp.concatenate([innovs[s] for s in range(SLOTS)], axis=1).astype(BF16)
    ys, zs, alongs, sizes = [], [], [], []
    for g in range(4):
        pg = perts[g]
        full = dot_t(pg, pg)
        gram = full[0:MEM]
        for i in range(1, 4):
            gram = jnp.where(block == i, full[i * MEM:(i + 1) * MEM], gram)
        al = dot_t(innov, pg)
        row = lax.broadcasted_iota(jnp.int32, al.shape, 0)
        al = jnp.sum(jnp.where(row == g * 4 + lanes(al.shape) // 64, al, 0.0), axis=0, keepdims=True)
        alongs.append(al)
        amat = gram + (MEM - 1.0) * eye
        sq = jnp.sum(amat * amat, axis=0, keepdims=True)
        blk1 = lanes((1, 256)) // 64
        size = jnp.zeros((1, 256), F32)
        for i in range(4):
            total = jnp.sum(jnp.where(blk1 == i, sq, 0.0), axis=1, keepdims=True)
            size = jnp.where(blk1 == i, total, size)
        size = jnp.sqrt(size)
        sizes.append(size)
        ys.append(amat / size)
        zs.append(None)
    for it in range(NS_ITERS):
        mixers = []
        for g in range(4):
            yh, yl = split(ys[g])
            if it == 0:
                zy = ys[g]
            else:
                (zy,) = times([split(zs[g])], (block_diagonal(yh), block_diagonal(yl)))
            mixers.append(1.5 * eye - 0.5 * zy)
        for g in range(4):
            mh, ml = split(mixers[g])
            md = (block_diagonal(mh), block_diagonal(ml))
            if it == 0:
                (ys[g],) = times([split(ys[g])], md)
                zs[g] = mixers[g]
            elif it < NS_ITERS - 1:
                ys[g], zs[g] = times([split(ys[g]), split(zs[g])], md)
            else:
                (zs[g],) = times([split(zs[g])], md)
    eye2 = (lax.broadcasted_iota(jnp.int32, (MEM, 128), 0) == (lanes((MEM, 128)) & 63)).astype(F32)
    size0 = jnp.sqrt(jnp.full((1, 128), MEM * (MEM - 1.0) * (MEM - 1.0), F32))
    y0 = (MEM - 1.0) / size0
    z0 = jnp.ones((1, 128), F32)
    for it in range(NS_ITERS):
        m0 = 1.5 - 0.5 * z0 * y0
        y0, z0 = y0 * m0, m0 * z0
    empty = eye2 * (z0 * jnp.sqrt((MEM - 1.0) / size0))

    @pl.loop(0, N_LON)
    def _(o):
        held_ref[o] = empty

    half = lanes((MEM, 128)) // 64
    for g in range(4):
        zh, zl = split(zs[g])
        zd = (block_diagonal(zh), block_diagonal(zl))
        (first,) = times([split(jnp.broadcast_to(alongs[g], (16, 256)))], zd)
        (second,) = times([split(first)], zd)
        tt = zs[g] * jnp.sqrt((MEM - 1.0) / sizes[g]) + second[0:1] / sizes[g]
        th, tl = split(tt)
        thd, tld = block_diagonal(th), block_diagonal(tl)
        devs, means = [], []
        for i in range(4):
            x = last[pl.ds((g * 4 + i) * MEM, MEM), :]
            mean = jnp.sum(x, axis=0, keepdims=True) * (1.0 / MEM)
            devs.append(x - mean)
            means.append(mean)
        dh, dl = split(jnp.concatenate(devs, axis=0))
        ana = dot(thd, dh) + dot(tld, dh) + dot(thd, dl)
        for i in range(4):
            result[pl.ds((g * 4 + i) * MEM, MEM), :] = ana[i * MEM:(i + 1) * MEM] + means[i]
        turned = jnp.transpose(jnp.concatenate([tt, tt], axis=0))
        for i in range(4):
            p = g * 4 + i
            mine = owners_ref[0, p, 0]
            rank = jnp.int32(0)
            for q in range(p):
                rank = rank + (owners_ref[0, q, 0] == mine).astype(jnp.int32)
            held_ref[mine] = jnp.where(half == rank, turned[i * MEM:(i + 1) * MEM], held_ref[mine])

    @pl.loop(0, 16)
    def _(k):
        q, t = k // 8, k % 8
        cs = pl.ds(pl.multiple_of(q * 128, 128), 128)
        parts = [result[pl.ds(p * MEM + t * 8, 8), cs] for p in range(16)]
        for i, x in enumerate(butterfly(parts)):
            out_ref[pl.ds(t * 256 + q * 16 + i, 8, stride=32), :] = x

    peaks = peaks_of(out_ref)
    peak_ref[...] = peaks
    for c in range(4):
        encode(out_ref, peaks, code_ref, c)


def analyse(states, cells, counts, values, errors, owners):
    vmem = pl.BlockSpec(memory_space=pltpu.VMEM)
    smem = pl.BlockSpec(memory_space=pltpu.SMEM)
    return pl.pallas_call(
        analysis_kernel,
        out_shape=(jax.ShapeDtypeStruct((MEM * LEV * ROWS, COLS), F32),
                   jax.ShapeDtypeStruct((MEM * LEV * ROWS, COLS), jnp.int16),
                   jax.ShapeDtypeStruct((LEV * ROWS, COLS), F32),
                   jax.ShapeDtypeStruct((N_LON, MEM, PCAP * MEM), F32)),
        in_specs=[vmem, vmem, smem, vmem, vmem, smem],
        out_specs=(vmem,) * 4,
        scratch_shapes=[
            pltpu.VMEM((PATCH, 2 * MEM, 256), BF16),
            pltpu.VMEM((4, 256, SLOTS * OBS), BF16),
            pltpu.VMEM((SLOTS, PATCH, OBS), F32),
            pltpu.VMEM((PATCH * MEM, 256), F32),
            pltpu.VMEM((PATCH * MEM, 256), F32),
        ],
        compiler_params=pltpu.CompilerParams(vmem_limit_bytes=60 * 1024 * 1024),
        name="analysis",
    )(states, cells, counts, values, errors, owners)


def deliver_kernel(code_ref, peak_ref, held_ref, code_out, peak_out, held_out, send_sem, recv_sem):
    lat, lon = lax.axis_index("lat"), lax.axis_index("lon")
    trow, tcol = tile_to_device(lat, lon)
    swapping, partner = swap_partner(lat, lon)
    barrier = pltpu.get_barrier_semaphore()

    def greet(device):
        pl.semaphore_signal(barrier, inc=1, device_id=device, device_id_type=MESH)

    for k in range(1, N_LON):
        greet(tile_to_device(lat, lax.rem(tcol + k, N_LON)))

    @pl.when(swapping)
    def _():
        greet(tile_to_device(lat, tcol))
        greet(partner)

    pl.semaphore_wait(barrier, jnp.where(swapping, N_LON + 1, N_LON - 1))
    owner = [lax.rem(lon + k, N_LON) for k in range(N_LON)]
    sends = [
        pltpu.make_async_remote_copy(
            src_ref=held_ref.at[owner[k]], dst_ref=held_out.at[tcol], send_sem=send_sem.at[k], recv_sem=recv_sem.at[tcol],
            device_id=(trow, owner[k]), device_id_type=MESH)
        for k in range(N_LON)]

    def landed(k):
        source = lax.rem(tcol + k, N_LON)
        pltpu.make_async_remote_copy(
            src_ref=held_ref.at[0], dst_ref=held_out.at[source], send_sem=send_sem.at[k], recv_sem=recv_sem.at[source],
            device_id=(trow, owner[k]), device_id_type=MESH).wait_recv()

    keep = pltpu.make_async_copy(held_ref.at[lon], held_out.at[tcol], send_sem.at[0])
    swaps = [
        pltpu.make_async_remote_copy(
            src_ref=src, dst_ref=dst, send_sem=send_sem.at[N_LON + i], recv_sem=recv_sem.at[N_LON + i],
            device_id=partner, device_id_type=MESH)
        for i, (src, dst) in enumerate(((code_ref, code_out), (peak_ref, peak_out)))]

    @pl.when(swapping)
    def _():
        for copy in swaps:
            copy.start()
        sends[0].start()

    @pl.when(jnp.logical_not(swapping))
    def _():
        keep.start()

    for copy in sends[1:]:
        copy.start()
    for k in range(1, N_LON):
        sends[k].wait_send()
        landed(k)

    @pl.when(swapping)
    def _():
        sends[0].wait_send()
        landed(0)
        for copy in swaps:
            copy.wait()

    @pl.when(jnp.logical_not(swapping))
    def _():
        keep.wait()


def deliver(*arrays):
    anyspec = pl.BlockSpec(memory_space=pl.ANY)
    return pl.pallas_call(
        deliver_kernel,
        out_shape=tuple(jax.ShapeDtypeStruct(x.shape, x.dtype) for x in arrays),
        in_specs=[anyspec] * 3,
        out_specs=(anyspec,) * 3,
        scratch_shapes=[pltpu.SemaphoreType.DMA((N_LON + 2,)), pltpu.SemaphoreType.DMA((N_LON + 2,))],
        compiler_params=pltpu.CompilerParams(collective_id=1, has_side_effects=True),
        name="deliver",
    )(*arrays)


def body(ensemble, courant_lon, courant_lat, diffusion, obs_cells, obs_counts, obs_values, obs_errors, owners):
    states, *obs = forecast(ensemble, courant_lon, courant_lat, diffusion,
                            obs_cells, obs_counts, obs_values, obs_errors, owners)
    analysis, code, peaks, held = analyse(states, *obs)
    swapping, _ = swap_partner(lax.axis_index("lat"), lax.axis_index("lon"))
    code, peaks, held = deliver(code, peaks, held)
    got = code.reshape(MEM, LEV * ROWS, COLS).astype(F32) * (peaks * (1.0 / CODE))
    analysis = jnp.where(swapping, got, analysis.reshape(MEM, LEV * ROWS, COLS))
    held = held.reshape(N_LON, MEM, PCAP, MEM).transpose(0, 2, 1, 3)
    return analysis.reshape(MEM, LEV, ROWS, COLS), held[None, None]


def solution(mesh):
    placed = (
        P(None, None, "lat", "lon"),
        P(None, "lat", "lon"),
        P(None, "lat", "lon"),
        P(None, "lat", "lon"),
        P(None, None, "lat", "lon", None),
        P(None, "lat", "lon"),
        P(None, "lat", "lon", None),
        P(None, "lat", "lon", None),
        P("lat", "lon", None),
    )
    return jax.shard_map(
        body,
        mesh=mesh,
        in_specs=placed,
        out_specs=(P(None, None, "lat", "lon"), P("lat", "lon", None, None, None, None)),
        check_vma=False,
    )
```

```python
import functools

import jax
import jax.numpy as jnp
from jax import lax
from jax.experimental import pallas as pl
from jax.experimental.pallas import tpu as pltpu
from jax.sharding import PartitionSpec as P

PCAP = 2
SLOTS = 4
STEPS = 3
NS_ITERS = 6
MEM = 64
LEV = 4
ROWS = 8
COLS = 128
PATCH = 16
OBS = 128
N_LAT = 8
N_LON = 16
F32 = jnp.float32
BF16 = jnp.bfloat16
NEIGHBOURS = ((-1, 0), (1, 0), (0, -1), (0, 1), (-1, -1), (-1, 1), (1, -1), (1, 1))
S_, N_, W_, E_, SW_, SE_, NW_, NE_ = range(8)


MESH = pl.DeviceIdType.MESH


def tile_to_device(row, col):
    return row - row % 2 + col % 2, col - col % 2 + row % 2


def swap_partner(lat, lon):
    swapping = (lat % 2 + lon % 2) % 2 == 1
    return swapping, (lat + 1 - 2 * (lat % 2), lon + 1 - 2 * (lon % 2))


def lanes(shape):
    return lax.broadcasted_iota(jnp.int32, shape, len(shape) - 1)


CODE = 32767.0


def peaks_of(ref):
    def grow(m, peak):
        return jnp.maximum(peak, jnp.abs(ref[pl.ds(pl.multiple_of(m * 32, 32), 32), :]))
    return jnp.maximum(lax.fori_loop(0, MEM, grow, jnp.zeros((32, COLS), F32), unroll=8), 1e-30)


def encode(ref, peaks, code_ref, chunk):
    factor = CODE / peaks

    @pl.loop(chunk * 16, chunk * 16 + 16, unroll=4)
    def _(m):
        at = pl.ds(pl.multiple_of(m * 32, 32), 32)
        code_ref[at, :] = jnp.round(ref[at, :] * factor).astype(jnp.int32).astype(jnp.int16)


def butterfly(parts):
    parts = list(parts)
    lane = lanes(parts[0].shape)
    for bit in (1, 2, 4, 8):
        keep = (lane & (8 * bit)) == 0
        for i in range(16):
            if i & bit:
                continue
            a, b = parts[i], parts[i + bit]
            parts[i] = jnp.where(keep, a, pltpu.roll(b, 8 * bit, 1))
            parts[i + bit] = jnp.where(keep, pltpu.roll(a, 128 - 8 * bit, 1), b)
    return parts


def split(x):
    hi = x.astype(BF16)
    return hi, (x - hi.astype(F32)).astype(BF16)


def dot(a, b):
    return jnp.dot(a, b, preferred_element_type=F32)


def dot_t(a, b):
    return lax.dot_general(a, b, (((1,), (1,)), ((), ())), preferred_element_type=F32)


def block_diagonal(x):
    block = lanes(x.shape) // 64
    return jnp.concatenate([jnp.where(block == i, x, jnp.zeros_like(x)) for i in range(4)], axis=0)


def times(x_parts, y_parts):
    yh, yl = y_parts
    n = sum(h.shape[0] for h, _ in x_parts)
    his = [h for h, _ in x_parts]
    los = [l for _, l in x_parts]
    top = dot(jnp.concatenate(his + los, axis=0), yh)
    low = dot(jnp.concatenate(his, axis=0), yl)
    total = top[:n] + top[n:] + low
    outs, at = [], 0
    for h, _ in x_parts:
        outs.append(total[at:at + h.shape[0]])
        at += h.shape[0]
    return outs


def cell_weights(counts_ref, errors_ref, slot):
    shape = (PATCH, OBS)
    patch = lax.broadcasted_iota(jnp.int32, shape, 0)
    count = jnp.zeros(shape, jnp.int32)
    for p in range(PATCH):
        count = jnp.where(patch == p, counts_ref[slot, 0, p], count)
    return jnp.where(lanes(shape) < count, 1.0 / errors_ref[slot, 0], 0.0)


def observe(states_ref, slot, cells, weights, values, xs, perts, innovs, last):
    @pl.loop(0, 8)
    def _(k):
        q, t = k // 4, k % 4
        halves = []
        for u in range(2):
            ms = pl.ds(pl.multiple_of(t * 16 + u * 8, 8), 8)
            parts = [states_ref[slot, i % 8, q * 2 + i // 8, ms, :] for i in range(16)]
            halves.append(butterfly(parts))
        cs = pl.ds(pl.multiple_of(q * 128, 128), 128)
        for p in range(PATCH):
            x = jnp.concatenate([halves[0][p], halves[1][p]], axis=0)
            hi, lo = split(x)
            xs[p, pl.ds(pl.multiple_of(t * 16, 16), 16), cs] = hi
            xs[p, pl.ds(pl.multiple_of(MEM + t * 16, 16), 16), cs] = lo
            if slot == SLOTS - 1:
                last[pl.ds(pl.multiple_of(p * MEM + t * 16, 16), 16), cs] = x

    cell_id = lax.broadcasted_iota(jnp.int32, (256, OBS), 0).astype(F32).astype(BF16)
    one, zero = jnp.ones((256, OBS), BF16), jnp.zeros((256, OBS), BF16)

    @pl.loop(0, PATCH, unroll=2)
    def _(p):
        w = zero
        for corner in range(4):
            idx = cells[slot, corner, 0, pl.ds(p, 1), :].astype(F32)
            idx = jnp.broadcast_to(idx, (256, OBS)).astype(BF16)
            w = w + jnp.where(cell_id == idx, one, zero)
        both = dot(xs[p], w)
        equivalent = 0.25 * (both[:MEM] + both[MEM:])
        mean = jnp.sum(equivalent, axis=0, keepdims=True) * (1.0 / MEM)
        weight = weights[slot, pl.ds(p, 1), :]
        pert = ((equivalent - mean) * weight).astype(BF16)
        perts[p // 4, pl.ds(pl.multiple_of((p % 4) * MEM, MEM), MEM), slot * OBS:(slot + 1) * OBS] = pert
        innovs[slot, pl.ds(p, 1), :] = (values[slot, 0, pl.ds(p, 1), :] - mean) * weight


def forecast_kernel(ens_ref, cu_ref, cv_ref, dd_ref, cells_ref, counts_ref, values_ref, errors_ref, owners_ref,
                    perts, innovs, last, owners_out,
                    out_ref, cells, weights, values, weight_send, xs,
                    tiles, coef_got, coefs, row_send, ring_send, edge_send,
                    row_got, edge_got, corner_got,
                    load_sem, swap_sem, code_send, code_got, peak_send, peak_got, code_sem, csend_sem, crecv_sem,
                    hsend_sem, hrecv_sem):
    lat, lon = lax.axis_index("lat"), lax.axis_index("lon")
    trow, tcol = tile_to_device(lat, lon)

    def device_at(step):
        row = lax.rem(trow + step[0] + N_LAT, N_LAT)
        col = lax.rem(tcol + step[1] + N_LON, N_LON)
        return tile_to_device(row, col)

    barrier = pltpu.get_barrier_semaphore()
    for step in NEIGHBOURS:
        pl.semaphore_signal(barrier, inc=1, device_id=device_at(step),
                            device_id_type=MESH)
    swapping, partner = swap_partner(lat, lon)
    moves = [(ref, coef_got.at[8, i]) for i, ref in enumerate((cu_ref, cv_ref, dd_ref))]
    moves += [(cells_ref, cells), (weight_send, weights), (values_ref, values), (owners_ref, owners_out)]
    for slot in range(SLOTS):
        weight_send[slot] = cell_weights(counts_ref, errors_ref, slot)
    load = pltpu.make_async_copy(ens_ref, tiles, load_sem.at[8])
    load.start()
    rows = MEM * LEV * ROWS // 4
    sent = [
        pltpu.make_async_remote_copy(src_ref=src, dst_ref=dst, send_sem=code_sem.at[0, i], recv_sem=code_sem.at[1, i],
                                     device_id=partner, device_id_type=MESH)
        for i, (src, dst) in enumerate(
            [(code_send.at[pl.ds(c * rows, rows)], code_got.at[pl.ds(c * rows, rows)]) for c in range(4)]
            + [(peak_send, peak_got)])]
    kept = [pltpu.make_async_copy(src, dst, load_sem.at[i]) for i, (src, dst) in enumerate(moves)]
    swapped = [
        pltpu.make_async_remote_copy(src_ref=src, dst_ref=dst, send_sem=load_sem.at[i], recv_sem=swap_sem.at[i],
                                     device_id=partner, device_id_type=MESH)
        for i, (src, dst) in enumerate(moves)]

    def arrive(first, last):
        @pl.when(swapping)
        def _():
            for copy in swapped[first:last]:
                copy.wait()

        @pl.when(jnp.logical_not(swapping))
        def _():
            for copy in kept[first:last]:
                copy.wait()

    pl.semaphore_wait(barrier, 8)

    @pl.when(swapping)
    def _():
        for copy in swapped[:3]:
            copy.start()
        load.wait()
        peaks = peaks_of(tiles)
        peak_send[...] = peaks
        sent[4].start()
        for c in range(4):
            encode(tiles, peaks, code_send, c)
            sent[c].start()
        for copy in swapped[3:]:
            copy.start()
        sent[4].wait()
        peaks = peak_got[...]
        for c in range(4):
            sent[c].wait()

            @pl.loop(c * 16, c * 16 + 16)
            def _(m):
                at = pl.ds(pl.multiple_of(m * 32, 32), 32)
                tiles[at, :] = code_got[at, :].astype(jnp.int32).astype(F32) * (peaks * (1.0 / CODE))

    @pl.when(jnp.logical_not(swapping))
    def _():
        for copy in kept:
            copy.start()
        load.wait()

    arrive(0, 3)
    opposite = (N_, S_, E_, W_, NE_, NW_, SE_, SW_)
    ccopies = []
    for d, step in enumerate(NEIGHBOURS):
        copy = pltpu.make_async_remote_copy(
            src_ref=coef_got.at[8], dst_ref=coef_got.at[opposite[d]],
            send_sem=csend_sem.at[d], recv_sem=crecv_sem.at[opposite[d]],
            device_id=device_at(step), device_id_type=MESH)
        copy.start()
        ccopies.append(copy)

    @pl.loop(0, LEV)
    def _(l):
        for r in range(ROWS):
            for t in range(8):
                out_ref[0, r, l, pl.ds(t * 8, 8), :] = tiles[pl.ds(t * 256 + l * ROWS + r, 8, stride=32), :]

    lane16 = lanes((16, COLS))
    lane1 = lanes((8, COLS))

    def send_halos(src, s):
        @pl.loop(0, MEM // 16)
        def _(t):
            ms = pl.ds(pl.multiple_of(t * 16, 16), 16)
            rings = []
            for half in range(2):
                ring = out_ref[src, half * 4, 0, ms, :]
                for k in range(1, 16):
                    turned = pltpu.roll(out_ref[src, half * 4 + k // LEV, k % LEV, ms, :], k * 8, 1)
                    inside = ((lane16 + (4 - k * 8 + 128)) & 127) < 8
                    ring = jnp.where(inside, turned, ring)
                ring_send[s, half, ms, :] = ring.astype(BF16)
                rings.append(ring)
            edge_send[s, 0, ms, :] = jnp.where((lane16 & 7) < 4, rings[0], pltpu.roll(rings[1], 4, 1)).astype(BF16)
            edge_send[s, 1, ms, :] = jnp.where((lane16 & 7) >= 4, rings[0], pltpu.roll(rings[1], 124, 1)).astype(BF16)
            for side, first in ((0, 0), (1, ROWS - 3)):
                for r in range(3):
                    for l in range(LEV):
                        row_send[s, side, r, l, ms, :] = out_ref[src, first + r, l, ms, :].astype(BF16)
        low, high = ring_send.at[s, 0], ring_send.at[s, 1]
        plan = (
            (S_, row_send.at[s, 0], row_got.at[s, 1], N_),
            (N_, row_send.at[s, 1], row_got.at[s, 0], S_),
            (W_, edge_send.at[s, 0], edge_got.at[s, 1], E_),
            (E_, edge_send.at[s, 1], edge_got.at[s, 0], W_),
            (SW_, low, corner_got.at[s, 3], NE_),
            (SE_, low, corner_got.at[s, 2], NW_),
            (NW_, high, corner_got.at[s, 1], SE_),
            (NE_, high, corner_got.at[s, 0], SW_),
        )
        copies = []
        for d, src_ref, dst_ref, landed in plan:
            copy = pltpu.make_async_remote_copy(
                src_ref=src_ref, dst_ref=dst_ref,
                send_sem=hsend_sem.at[s, d], recv_sem=hrecv_sem.at[s, landed],
                device_id=device_at(NEIGHBOURS[d]), device_id_type=MESH)
            copy.start()
            copies.append(copy)
        return copies

    copies = send_halos(0, 0)
    for copy in ccopies:
        copy.wait()
    south_ok = jnp.where(trow > 0, 1.0, 0.0).astype(F32)
    north_ok = jnp.where(trow < N_LAT - 1, 1.0, 0.0).astype(F32)
    lane8 = lanes((ROWS, COLS))
    for block, (cen, west, east, ok) in enumerate(((S_, SW_, SE_, south_ok), (8, W_, E_, None), (N_, NW_, NE_, north_ok))):
        for half in range(2):
            for l in range(LEV):
                def pick(i):
                    if half == 0:
                        return jnp.where(lane8 < 96, coef_got[cen, i, l], coef_got[west, i, l])
                    return jnp.where(lane8 >= 32, coef_got[cen, i, l], coef_got[east, i, l])
                cu, cv, dd = pick(0), pick(1), pick(2)
                aw = jnp.maximum(cu, 0.0) + dd
                ae = dd - jnp.minimum(cu, 0.0)
                as_ = jnp.maximum(cv, 0.0) + dd
                an = dd - jnp.minimum(cv, 0.0)
                ac = 1.0 - (jnp.abs(cu) + jnp.abs(cv) + 4.0 * dd)
                for j, a in enumerate((ac, aw, ae, as_, an)):
                    a = a if ok is None else a * ok
                    for r in ((6, 7), range(8), (0, 1))[block]:
                        coefs[half, l, j, block * 8 + r - 6] = jnp.broadcast_to(a[r:r + 1], (8, COLS))

    def step_row(half, l, r, south, v, north):
        ac, aw, ae, as_, an = (coefs[half, l, j, r] for j in range(5))
        return (ac * v + aw * pltpu.roll(v, 1, 1)) + (ae * pltpu.roll(v, COLS - 1, 1) + (as_ * south + an * north))

    for s in range(SLOTS):
        for copy in copies:
            copy.wait()
        prev = max(s - 1, 0)
        for l in range(LEV):
            @pl.loop(0, MEM // 16)
            def _(t):
                ms = pl.ds(pl.multiple_of(t * 16, 16), 16)
                west, east = edge_got[s, 0, ms, :].astype(F32), edge_got[s, 1, ms, :].astype(F32)
                first = (lane16 & 7) < 4
                rings = [
                    jnp.where(first, corner_got[s, 1, ms, :].astype(F32), corner_got[s, 0, ms, :].astype(F32)) * south_ok,
                    jnp.where(first, east, west),
                    jnp.where(first, pltpu.roll(east, 124, 1), pltpu.roll(west, 4, 1)),
                    jnp.where(first, corner_got[s, 3, ms, :].astype(F32), corner_got[s, 2, ms, :].astype(F32)) * north_ok,
                ]
                mines, auxs = [], []
                for r in range(-3, ROWS + 3):
                    if 0 <= r < ROWS:
                        mine = out_ref[prev, r, l, ms, :]
                    elif r < 0:
                        mine = row_got[s, 0, r + 3, l, ms, :].astype(F32) * south_ok
                    else:
                        mine = row_got[s, 1, r - ROWS, l, ms, :].astype(F32) * north_ok
                    turn = (((r + 4) % 4) * LEV + l) * 8
                    ring = rings[(r + 4) // 4]
                    auxs.append(pltpu.roll(ring, 128 - turn, 1) if turn else ring)
                    mines.append(mine)
                for u in range(2):
                    sub = slice(u * 8, u * 8 + 8)
                    sides = []
                    for half in range(2):
                        if half == 0:
                            v = [jnp.where(lane1 < 96, m[sub], a[sub]) for m, a in zip(mines, auxs)]
                        else:
                            v = [jnp.where(lane1 >= 32, m[sub], a[sub]) for m, a in zip(mines, auxs)]
                        for step in range(STEPS):
                            v = [step_row(half, l, r + step, v[r], v[r + 1], v[r + 2]) for r in range(len(v) - 2)]
                        sides.append(v)
                    for r in range(ROWS):
                        out_ref[s, r, l, pl.ds(pl.multiple_of(t * 16 + u * 8, 8), 8), :] = jnp.where(
                            lane1 < 64, sides[0][r], sides[1][r])
        if s < SLOTS - 1:
            copies = send_halos(s, s + 1)
        if s == 0:
            arrive(3, 7)
        observe(out_ref, s, cells, weights, values, xs, perts, innovs, last)


VMEM_SPEC = pl.BlockSpec(memory_space=pltpu.VMEM)
SMEM_SPEC = pl.BlockSpec(memory_space=pltpu.SMEM)
ANY_SPEC = pl.BlockSpec(memory_space=pl.ANY)


def forecast(ensemble, cu, cv, dd, cells, counts, values, errors, owners):
    return pl.pallas_call(
        forecast_kernel,
        out_shape=(jax.ShapeDtypeStruct((4, 256, SLOTS * OBS), BF16),
                   jax.ShapeDtypeStruct((SLOTS, PATCH, OBS), F32),
                   jax.ShapeDtypeStruct((PATCH * MEM, 256), F32),
                   jax.ShapeDtypeStruct(owners.shape, jnp.int32)),
        in_specs=[ANY_SPEC] * 5 + [SMEM_SPEC, ANY_SPEC, VMEM_SPEC, ANY_SPEC],
        out_specs=(VMEM_SPEC, VMEM_SPEC, VMEM_SPEC, ANY_SPEC),
        scratch_shapes=[
            pltpu.VMEM((SLOTS, ROWS, LEV, MEM, COLS), F32),
            pltpu.VMEM((SLOTS, 4, 1, PATCH, OBS), jnp.int32),
            pltpu.VMEM((SLOTS, PATCH, OBS), F32),
            pltpu.VMEM((SLOTS, 1, PATCH, OBS), F32),
            pltpu.VMEM((SLOTS, PATCH, OBS), F32),
            pltpu.VMEM((PATCH, 2 * MEM, 256), BF16),
            pltpu.VMEM((MEM * LEV * ROWS, COLS), F32),
            pltpu.VMEM((9, 3, LEV, ROWS, COLS), F32),
            pltpu.VMEM((2, LEV, 5, 12, 8, COLS), F32),
            pltpu.VMEM((SLOTS, 2, 3, LEV, MEM, COLS), BF16),
            pltpu.VMEM((SLOTS, 2, MEM, COLS), BF16),
            pltpu.VMEM((SLOTS, 2, MEM, COLS), BF16),
            pltpu.VMEM((SLOTS, 2, 3, LEV, MEM, COLS), BF16),
            pltpu.VMEM((SLOTS, 2, MEM, COLS), BF16),
            pltpu.VMEM((SLOTS, 4, MEM, COLS), BF16),
            pltpu.SemaphoreType.DMA((9,)),
            pltpu.SemaphoreType.DMA((9,)),
            pltpu.VMEM((MEM * LEV * ROWS, COLS), jnp.int16),
            pltpu.VMEM((MEM * LEV * ROWS, COLS), jnp.int16),
            pltpu.VMEM((LEV * ROWS, COLS), F32),
            pltpu.VMEM((LEV * ROWS, COLS), F32),
            pltpu.SemaphoreType.DMA((2, 5)),
            pltpu.SemaphoreType.DMA((8,)),
            pltpu.SemaphoreType.DMA((8,)),
            pltpu.SemaphoreType.DMA((SLOTS, 8)),
            pltpu.SemaphoreType.DMA((SLOTS, 8)),
        ],
        compiler_params=pltpu.CompilerParams(
            collective_id=0, has_side_effects=True, vmem_limit_bytes=60 * 1024 * 1024),
        name="forecast",
    )(ensemble.reshape(MEM * LEV * ROWS, COLS), cu, cv, dd, cells, counts, values, errors, owners)


def analysis_kernel(perts, innovs, last, owners_ref, out_ref, code_ref, peak_ref, held_ref, result):
    shape = (MEM, 256)
    block = lanes(shape) // 64
    eye = (lax.broadcasted_iota(jnp.int32, shape, 0) == (lanes(shape) & 63)).astype(F32)
    innov = jnp.concatenate([innovs[s] for s in range(SLOTS)], axis=1).astype(BF16)
    ys, zs, alongs, sizes = [], [], [], []
    for g in range(4):
        pg = perts[g]
        full = dot_t(pg, pg)
        gram = full[0:MEM]
        for i in range(1, 4):
            gram = jnp.where(block == i, full[i * MEM:(i + 1) * MEM], gram)
        al = dot_t(innov, pg)
        row = lax.broadcasted_iota(jnp.int32, al.shape, 0)
        al = jnp.sum(jnp.where(row == g * 4 + lanes(al.shape) // 64, al, 0.0), axis=0, keepdims=True)
        alongs.append(al)
        amat = gram + (MEM - 1.0) * eye
        sq = jnp.sum(amat * amat, axis=0, keepdims=True)
        blk1 = lanes((1, 256)) // 64
        size = jnp.zeros((1, 256), F32)
        for i in range(4):
            total = jnp.sum(jnp.where(blk1 == i, sq, 0.0), axis=1, keepdims=True)
            size = jnp.where(blk1 == i, total, size)
        size = jnp.sqrt(size)
        sizes.append(size)
        ys.append(amat / size)
        zs.append(None)
    for it in range(NS_ITERS):
        mixers = []
        for g in range(4):
            yh, yl = split(ys[g])
            if it == 0:
                zy = ys[g]
            else:
                (zy,) = times([split(zs[g])], (block_diagonal(yh), block_diagonal(yl)))
            mixers.append(1.5 * eye - 0.5 * zy)
        for g in range(4):
            mh, ml = split(mixers[g])
            md = (block_diagonal(mh), block_diagonal(ml))
            if it == 0:
                (ys[g],) = times([split(ys[g])], md)
                zs[g] = mixers[g]
            elif it < NS_ITERS - 1:
                ys[g], zs[g] = times([split(ys[g]), split(zs[g])], md)
            else:
                (zs[g],) = times([split(zs[g])], md)
    eye2 = (lax.broadcasted_iota(jnp.int32, (MEM, 128), 0) == (lanes((MEM, 128)) & 63)).astype(F32)
    size0 = jnp.sqrt(jnp.full((1, 128), MEM * (MEM - 1.0) * (MEM - 1.0), F32))
    y0 = (MEM - 1.0) / size0
    z0 = jnp.ones((1, 128), F32)
    for it in range(NS_ITERS):
        m0 = 1.5 - 0.5 * z0 * y0
        y0, z0 = y0 * m0, m0 * z0
    empty = eye2 * (z0 * jnp.sqrt((MEM - 1.0) / size0))

    @pl.loop(0, N_LON)
    def _(o):
        held_ref[o] = empty

    half = lanes((MEM, 128)) // 64
    for g in range(4):
        zh, zl = split(zs[g])
        zd = (block_diagonal(zh), block_diagonal(zl))
        (first,) = times([split(jnp.broadcast_to(alongs[g], (16, 256)))], zd)
        (second,) = times([split(first)], zd)
        tt = zs[g] * jnp.sqrt((MEM - 1.0) / sizes[g]) + second[0:1] / sizes[g]
        th, tl = split(tt)
        thd, tld = block_diagonal(th), block_diagonal(tl)
        devs, means = [], []
        for i in range(4):
            x = last[pl.ds((g * 4 + i) * MEM, MEM), :]
            mean = jnp.sum(x, axis=0, keepdims=True) * (1.0 / MEM)
            devs.append(x - mean)
            means.append(mean)
        dh, dl = split(jnp.concatenate(devs, axis=0))
        ana = dot(thd, dh) + dot(tld, dh) + dot(thd, dl)
        for i in range(4):
            result[pl.ds((g * 4 + i) * MEM, MEM), :] = ana[i * MEM:(i + 1) * MEM] + means[i]
        turned = jnp.transpose(jnp.concatenate([tt, tt], axis=0))
        for i in range(4):
            p = g * 4 + i
            mine = owners_ref[0, p, 0]
            rank = jnp.int32(0)
            for q in range(p):
                rank = rank + (owners_ref[0, q, 0] == mine).astype(jnp.int32)
            held_ref[mine] = jnp.where(half == rank, turned[i * MEM:(i + 1) * MEM], held_ref[mine])

    @pl.loop(0, 16)
    def _(k):
        q, t = k // 8, k % 8
        cs = pl.ds(pl.multiple_of(q * 128, 128), 128)
        parts = [result[pl.ds(p * MEM + t * 8, 8), cs] for p in range(16)]
        for i, x in enumerate(butterfly(parts)):
            out_ref[pl.ds(t * 256 + q * 16 + i, 8, stride=32), :] = x

    peaks = peaks_of(out_ref)
    peak_ref[...] = peaks
    for c in range(4):
        encode(out_ref, peaks, code_ref, c)


def analyse(perts, innovs, last, owners):
    return pl.pallas_call(
        analysis_kernel,
        out_shape=(jax.ShapeDtypeStruct((MEM * LEV * ROWS, COLS), F32),
                   jax.ShapeDtypeStruct((MEM * LEV * ROWS, COLS), jnp.int16),
                   jax.ShapeDtypeStruct((LEV * ROWS, COLS), F32),
                   jax.ShapeDtypeStruct((N_LON, MEM, PCAP * MEM), F32)),
        in_specs=[VMEM_SPEC] * 3 + [SMEM_SPEC],
        out_specs=(VMEM_SPEC,) * 4,
        scratch_shapes=[pltpu.VMEM((PATCH * MEM, 256), F32)],
        compiler_params=pltpu.CompilerParams(vmem_limit_bytes=60 * 1024 * 1024),
        name="analysis",
    )(perts, innovs, last, owners)


def deliver_kernel(code_ref, peak_ref, held_ref, code_out, peak_out, held_out, send_sem, recv_sem):
    lat, lon = lax.axis_index("lat"), lax.axis_index("lon")
    trow, tcol = tile_to_device(lat, lon)
    swapping, partner = swap_partner(lat, lon)
    barrier = pltpu.get_barrier_semaphore()

    def greet(device):
        pl.semaphore_signal(barrier, inc=1, device_id=device, device_id_type=MESH)

    for k in range(1, N_LON):
        greet(tile_to_device(lat, lax.rem(tcol + k, N_LON)))

    @pl.when(swapping)
    def _():
        greet(tile_to_device(lat, tcol))
        greet(partner)

    pl.semaphore_wait(barrier, jnp.where(swapping, N_LON + 1, N_LON - 1))
    owner = [lax.rem(lon + k, N_LON) for k in range(N_LON)]
    sends = [
        pltpu.make_async_remote_copy(
            src_ref=held_ref.at[owner[k]], dst_ref=held_out.at[tcol], send_sem=send_sem.at[k], recv_sem=recv_sem.at[tcol],
            device_id=(trow, owner[k]), device_id_type=MESH)
        for k in range(N_LON)]

    def landed(k):
        source = lax.rem(tcol + k, N_LON)
        pltpu.make_async_remote_copy(
            src_ref=held_ref.at[0], dst_ref=held_out.at[source], send_sem=send_sem.at[k], recv_sem=recv_sem.at[source],
            device_id=(trow, owner[k]), device_id_type=MESH).wait_recv()

    keep = pltpu.make_async_copy(held_ref.at[lon], held_out.at[tcol], send_sem.at[0])
    swaps = [
        pltpu.make_async_remote_copy(
            src_ref=src, dst_ref=dst, send_sem=send_sem.at[N_LON + i], recv_sem=recv_sem.at[N_LON + i],
            device_id=partner, device_id_type=MESH)
        for i, (src, dst) in enumerate(((code_ref, code_out), (peak_ref, peak_out)))]

    @pl.when(swapping)
    def _():
        for copy in swaps:
            copy.start()
        sends[0].start()

    @pl.when(jnp.logical_not(swapping))
    def _():
        keep.start()

    for copy in sends[1:]:
        copy.start()
    for k in range(1, N_LON):
        sends[k].wait_send()
        landed(k)

    @pl.when(swapping)
    def _():
        sends[0].wait_send()
        landed(0)
        for copy in swaps:
            copy.wait()

    @pl.when(jnp.logical_not(swapping))
    def _():
        keep.wait()


def deliver(*arrays):
    anyspec = pl.BlockSpec(memory_space=pl.ANY)
    return pl.pallas_call(
        deliver_kernel,
        out_shape=tuple(jax.ShapeDtypeStruct(x.shape, x.dtype) for x in arrays),
        in_specs=[anyspec] * 3,
        out_specs=(anyspec,) * 3,
        scratch_shapes=[pltpu.SemaphoreType.DMA((N_LON + 2,)), pltpu.SemaphoreType.DMA((N_LON + 2,))],
        compiler_params=pltpu.CompilerParams(collective_id=1, has_side_effects=True),
        name="deliver",
    )(*arrays)


def body(ensemble, courant_lon, courant_lat, diffusion, obs_cells, obs_counts, obs_values, obs_errors, owners):
    found = forecast(ensemble, courant_lon, courant_lat, diffusion, obs_cells, obs_counts, obs_values, obs_errors, owners)
    analysis, code, peaks, held = analyse(*found)
    swapping, _ = swap_partner(lax.axis_index("lat"), lax.axis_index("lon"))
    code, peaks, held = deliver(code, peaks, held)
    got = code.reshape(MEM, LEV * ROWS, COLS).astype(F32) * (peaks * (1.0 / CODE))
    analysis = jnp.where(swapping, got, analysis.reshape(MEM, LEV * ROWS, COLS))
    held = held.reshape(N_LON, MEM, PCAP, MEM).transpose(0, 2, 1, 3)
    return analysis.reshape(MEM, LEV, ROWS, COLS), held[None, None]


def solution(mesh):
    placed = (
        P(None, None, "lat", "lon"),
        P(None, "lat", "lon"),
        P(None, "lat", "lon"),
        P(None, "lat", "lon"),
        P(None, None, "lat", "lon", None),
        P(None, "lat", "lon"),
        P(None, "lat", "lon", None),
        P(None, "lat", "lon", None),
        P("lat", "lon", None),
    )
    return jax.shard_map(
        body,
        mesh=mesh,
        in_specs=placed,
        out_specs=(P(None, None, "lat", "lon"), P("lat", "lon", None, None, None, None)),
        check_vma=False,
    )
```

```python
import functools

import jax
import jax.numpy as jnp
from jax import lax
from jax.experimental import pallas as pl
from jax.experimental.pallas import tpu as pltpu
from jax.sharding import PartitionSpec as P

PCAP = 2
SLOTS = 4
STEPS = 3
NS_ITERS = 6
MEM = 64
LEV = 4
ROWS = 8
COLS = 128
PATCH = 16
OBS = 128
N_LAT = 8
N_LON = 16
F32 = jnp.float32
BF16 = jnp.bfloat16
NEIGHBOURS = ((-1, 0), (1, 0), (0, -1), (0, 1), (-1, -1), (-1, 1), (1, -1), (1, 1))
S_, N_, W_, E_, SW_, SE_, NW_, NE_ = range(8)


MESH = pl.DeviceIdType.MESH


def tile_to_device(row, col):
    return row - row % 2 + col % 2, col - col % 2 + row % 2


def swap_partner(lat, lon):
    swapping = (lat % 2 + lon % 2) % 2 == 1
    return swapping, (lat + 1 - 2 * (lat % 2), lon + 1 - 2 * (lon % 2))


def lanes(shape):
    return lax.broadcasted_iota(jnp.int32, shape, len(shape) - 1)


CODE = 32767.0


def peaks_of(ref):
    def grow(m, peak):
        return jnp.maximum(peak, jnp.abs(ref[pl.ds(pl.multiple_of(m * 32, 32), 32), :]))
    return jnp.maximum(lax.fori_loop(0, MEM, grow, jnp.zeros((32, COLS), F32), unroll=8), 1e-30)


def encode(ref, peaks, code_ref, chunk):
    factor = CODE / peaks

    @pl.loop(chunk * 16, chunk * 16 + 16, unroll=4)
    def _(m):
        at = pl.ds(pl.multiple_of(m * 32, 32), 32)
        code_ref[at, :] = jnp.round(ref[at, :] * factor).astype(jnp.int32).astype(jnp.int16)


def butterfly(parts):
    parts = list(parts)
    lane = lanes(parts[0].shape)
    for bit in (1, 2, 4, 8):
        keep = (lane & (8 * bit)) == 0
        for i in range(16):
            if i & bit:
                continue
            a, b = parts[i], parts[i + bit]
            parts[i] = jnp.where(keep, a, pltpu.roll(b, 8 * bit, 1))
            parts[i + bit] = jnp.where(keep, pltpu.roll(a, 128 - 8 * bit, 1), b)
    return parts


def split(x):
    hi = x.astype(BF16)
    return hi, (x - hi.astype(F32)).astype(BF16)


def dot(a, b):
    return jnp.dot(a, b, preferred_element_type=F32)


def dot_t(a, b):
    return lax.dot_general(a, b, (((1,), (1,)), ((), ())), preferred_element_type=F32)


def block_diagonal(x):
    block = lanes(x.shape) // 64
    return jnp.concatenate([jnp.where(block == i, x, jnp.zeros_like(x)) for i in range(4)], axis=0)


def times(x_parts, y_parts):
    yh, yl = y_parts
    n = sum(h.shape[0] for h, _ in x_parts)
    his = [h for h, _ in x_parts]
    los = [l for _, l in x_parts]
    top = dot(jnp.concatenate(his + los, axis=0), yh)
    low = dot(jnp.concatenate(his, axis=0), yl)
    total = top[:n] + top[n:] + low
    outs, at = [], 0
    for h, _ in x_parts:
        outs.append(total[at:at + h.shape[0]])
        at += h.shape[0]
    return outs


def cell_weights(counts_ref, errors_ref, slot):
    shape = (PATCH, OBS)
    patch = lax.broadcasted_iota(jnp.int32, shape, 0)
    count = jnp.zeros(shape, jnp.int32)
    for p in range(PATCH):
        count = jnp.where(patch == p, counts_ref[slot, 0, p], count)
    return jnp.where(lanes(shape) < count, 1.0 / errors_ref[slot, 0], 0.0)


def observe(states_ref, slot, cells, weights, values, xs, perts, innovs, last):
    @pl.loop(0, 8)
    def _(k):
        q, t = k // 4, k % 4
        halves = []
        for u in range(2):
            ms = pl.ds(pl.multiple_of(t * 16 + u * 8, 8), 8)
            parts = [states_ref[slot, i % 8, q * 2 + i // 8, ms, :] for i in range(16)]
            halves.append(butterfly(parts))
        cs = pl.ds(pl.multiple_of(q * 128, 128), 128)
        for p in range(PATCH):
            x = jnp.concatenate([halves[0][p], halves[1][p]], axis=0)
            hi, lo = split(x)
            xs[p, pl.ds(pl.multiple_of(t * 16, 16), 16), cs] = hi
            xs[p, pl.ds(pl.multiple_of(MEM + t * 16, 16), 16), cs] = lo
            if slot == SLOTS - 1:
                last[pl.ds(pl.multiple_of(p * MEM + t * 16, 16), 16), cs] = x

    cell_id = lax.broadcasted_iota(jnp.int32, (256, OBS), 0).astype(F32).astype(BF16)
    one, zero = jnp.ones((256, OBS), BF16), jnp.zeros((256, OBS), BF16)

    @pl.loop(0, PATCH, unroll=2)
    def _(p):
        w = zero
        for corner in range(4):
            idx = cells[slot, corner, 0, pl.ds(p, 1), :].astype(F32)
            idx = jnp.broadcast_to(idx, (256, OBS)).astype(BF16)
            w = w + jnp.where(cell_id == idx, one, zero)
        both = dot(xs[p], w)
        equivalent = 0.25 * (both[:MEM] + both[MEM:])
        mean = jnp.sum(equivalent, axis=0, keepdims=True) * (1.0 / MEM)
        weight = weights[slot, pl.ds(p, 1), :]
        pert = ((equivalent - mean) * weight).astype(BF16)
        perts[p // 4, pl.ds(pl.multiple_of((p % 4) * MEM, MEM), MEM), slot * OBS:(slot + 1) * OBS] = pert
        innovs[slot, pl.ds(p, 1), :] = (values[slot, 0, pl.ds(p, 1), :] - mean) * weight


def transforms_of(perts, innovs, tts):
    shape = (MEM, 256)
    block = lanes(shape) // 64
    eye = (lax.broadcasted_iota(jnp.int32, shape, 0) == (lanes(shape) & 63)).astype(F32)
    innov = jnp.concatenate([innovs[s] for s in range(SLOTS)], axis=1).astype(BF16)
    ys, zs, alongs, sizes = [], [], [], []
    for g in range(4):
        pg = perts[g]
        full = dot_t(pg, pg)
        gram = full[0:MEM]
        for i in range(1, 4):
            gram = jnp.where(block == i, full[i * MEM:(i + 1) * MEM], gram)
        al = dot_t(innov, pg)
        row = lax.broadcasted_iota(jnp.int32, al.shape, 0)
        al = jnp.sum(jnp.where(row == g * 4 + lanes(al.shape) // 64, al, 0.0), axis=0, keepdims=True)
        alongs.append(al)
        amat = gram + (MEM - 1.0) * eye
        sq = jnp.sum(amat * amat, axis=0, keepdims=True)
        blk1 = lanes((1, 256)) // 64
        size = jnp.zeros((1, 256), F32)
        for i in range(4):
            total = jnp.sum(jnp.where(blk1 == i, sq, 0.0), axis=1, keepdims=True)
            size = jnp.where(blk1 == i, total, size)
        size = jnp.sqrt(size)
        sizes.append(size)
        ys.append(amat / size)
        zs.append(None)
    for it in range(NS_ITERS):
        mixers = []
        for g in range(4):
            yh, yl = split(ys[g])
            if it == 0:
                zy = ys[g]
            else:
                (zy,) = times([split(zs[g])], (block_diagonal(yh), block_diagonal(yl)))
            mixers.append(1.5 * eye - 0.5 * zy)
        for g in range(4):
            mh, ml = split(mixers[g])
            md = (block_diagonal(mh), block_diagonal(ml))
            if it == 0:
                (ys[g],) = times([split(ys[g])], md)
                zs[g] = mixers[g]
            elif it < NS_ITERS - 1:
                ys[g], zs[g] = times([split(ys[g]), split(zs[g])], md)
            else:
                (zs[g],) = times([split(zs[g])], md)
    eye2 = (lax.broadcasted_iota(jnp.int32, (MEM, 128), 0) == (lanes((MEM, 128)) & 63)).astype(F32)
    size0 = jnp.sqrt(jnp.full((1, 128), MEM * (MEM - 1.0) * (MEM - 1.0), F32))
    y0 = (MEM - 1.0) / size0
    z0 = jnp.ones((1, 128), F32)
    for it in range(NS_ITERS):
        m0 = 1.5 - 0.5 * z0 * y0
        y0, z0 = y0 * m0, m0 * z0
    empty = eye2 * (z0 * jnp.sqrt((MEM - 1.0) / size0))

    tts[PATCH] = empty
    turned = []
    for g in range(4):
        zh, zl = split(zs[g])
        zd = (block_diagonal(zh), block_diagonal(zl))
        (first,) = times([split(jnp.broadcast_to(alongs[g], (16, 256)))], zd)
        (second,) = times([split(first)], zd)
        tt = zs[g] * jnp.sqrt((MEM - 1.0) / sizes[g]) + second[0:1] / sizes[g]
        turned.append(tt)
        both = jnp.transpose(jnp.concatenate([tt, tt], axis=0))
        for i in range(4):
            tts[g * 4 + i] = both[i * MEM:(i + 1) * MEM]
    return turned


def analyse_members(turned, last, result, out_ref):
    for g in range(4):
        th, tl = split(turned[g])
        thd, tld = block_diagonal(th), block_diagonal(tl)
        devs, means = [], []
        for i in range(4):
            x = last[pl.ds((g * 4 + i) * MEM, MEM), :]
            mean = jnp.sum(x, axis=0, keepdims=True) * (1.0 / MEM)
            devs.append(x - mean)
            means.append(mean)
        dh, dl = split(jnp.concatenate(devs, axis=0))
        ana = dot(thd, dh) + dot(tld, dh) + dot(thd, dl)
        for i in range(4):
            result[pl.ds((g * 4 + i) * MEM, MEM), :] = ana[i * MEM:(i + 1) * MEM] + means[i]

    @pl.loop(0, 16)
    def _(k):
        q, t = k // 8, k % 8
        cs = pl.ds(pl.multiple_of(q * 128, 128), 128)
        parts = [result[pl.ds(pl.multiple_of(p * MEM + t * 8, 8), 8), cs] for p in range(16)]
        for i, x in enumerate(butterfly(parts)):
            out_ref[pl.ds(t * 256 + q * 16 + i, 8, stride=32), :] = x


def cycle_kernel(ens_ref, cu_ref, cv_ref, dd_ref, cells_ref, counts_ref, values_ref, errors_ref, owners_ref,
                 ana_out, held_out, owners_out,
                 perts, innovs, last, owners,
                 out_ref, cells, weights, values, weight_send, xs,
                 tiles, coef_got, coefs, row_send, ring_send, edge_send,
                 row_got, edge_got, corner_got,
                 load_sem, swap_sem, code_send, code_got, peak_send, peak_got, code_sem, csend_sem, crecv_sem,
                 hsend_sem, hrecv_sem,
                 result, tts, back_send, back_got, back_peak, back_peak_got, back_sem,
                 held_send, held_got, held_peak, held_peak_got, tsend_sem, trecv_sem):
    lat, lon = lax.axis_index("lat"), lax.axis_index("lon")
    trow, tcol = tile_to_device(lat, lon)

    def device_at(step):
        row = lax.rem(trow + step[0] + N_LAT, N_LAT)
        col = lax.rem(tcol + step[1] + N_LON, N_LON)
        return tile_to_device(row, col)

    barrier = pltpu.get_barrier_semaphore()
    for step in NEIGHBOURS:
        pl.semaphore_signal(barrier, inc=1, device_id=device_at(step),
                            device_id_type=MESH)
    swapping, partner = swap_partner(lat, lon)
    for k in range(1, N_LON):
        pl.semaphore_signal(barrier, inc=1, device_id=tile_to_device(lat, lax.rem(tcol + k, N_LON)), device_id_type=MESH)

    @pl.when(swapping)
    def _():
        pl.semaphore_signal(barrier, inc=1, device_id=tile_to_device(lat, tcol), device_id_type=MESH)

    moves = [(ref, coef_got.at[8, i]) for i, ref in enumerate((cu_ref, cv_ref, dd_ref))]
    moves += [(cells_ref, cells), (weight_send, weights), (values_ref, values), (owners_ref, owners_out)]
    for slot in range(SLOTS):
        weight_send[slot] = cell_weights(counts_ref, errors_ref, slot)
    load = pltpu.make_async_copy(ens_ref, tiles, load_sem.at[8])
    load.start()
    rows = MEM * LEV * ROWS // 4
    sent = [
        pltpu.make_async_remote_copy(src_ref=src, dst_ref=dst, send_sem=code_sem.at[0, i], recv_sem=code_sem.at[1, i],
                                     device_id=partner, device_id_type=MESH)
        for i, (src, dst) in enumerate(
            [(code_send.at[pl.ds(c * rows, rows)], code_got.at[pl.ds(c * rows, rows)]) for c in range(4)]
            + [(peak_send, peak_got)])]
    kept = [pltpu.make_async_copy(src, dst, load_sem.at[i]) for i, (src, dst) in enumerate(moves)]
    swapped = [
        pltpu.make_async_remote_copy(src_ref=src, dst_ref=dst, send_sem=load_sem.at[i], recv_sem=swap_sem.at[i],
                                     device_id=partner, device_id_type=MESH)
        for i, (src, dst) in enumerate(moves)]

    def arrive(first, last):
        @pl.when(swapping)
        def _():
            for copy in swapped[first:last]:
                copy.wait()

        @pl.when(jnp.logical_not(swapping))
        def _():
            for copy in kept[first:last]:
                copy.wait()

    pl.semaphore_wait(barrier, jnp.where(swapping, 8 + N_LON, 7 + N_LON))

    @pl.when(swapping)
    def _():
        for copy in swapped[:3]:
            copy.start()
        load.wait()
        peaks = peaks_of(tiles)
        peak_send[...] = peaks
        sent[4].start()
        for c in range(4):
            encode(tiles, peaks, code_send, c)
            sent[c].start()
        for copy in swapped[3:]:
            copy.start()
        sent[4].wait()
        peaks = peak_got[...]
        for c in range(4):
            sent[c].wait()

            @pl.loop(c * 16, c * 16 + 16)
            def _(m):
                at = pl.ds(pl.multiple_of(m * 32, 32), 32)
                tiles[at, :] = code_got[at, :].astype(jnp.int32).astype(F32) * (peaks * (1.0 / CODE))

    @pl.when(jnp.logical_not(swapping))
    def _():
        for copy in kept:
            copy.start()
        load.wait()

    arrive(0, 3)
    opposite = (N_, S_, E_, W_, NE_, NW_, SE_, SW_)
    ccopies = []
    for d, step in enumerate(NEIGHBOURS):
        copy = pltpu.make_async_remote_copy(
            src_ref=coef_got.at[8], dst_ref=coef_got.at[opposite[d]],
            send_sem=csend_sem.at[d], recv_sem=crecv_sem.at[opposite[d]],
            device_id=device_at(step), device_id_type=MESH)
        copy.start()
        ccopies.append(copy)

    @pl.loop(0, LEV)
    def _(l):
        for r in range(ROWS):
            for t in range(8):
                out_ref[0, r, l, pl.ds(t * 8, 8), :] = tiles[pl.ds(t * 256 + l * ROWS + r, 8, stride=32), :]

    lane16 = lanes((16, COLS))
    lane1 = lanes((8, COLS))

    def send_halos(src, s):
        @pl.loop(0, MEM // 16)
        def _(t):
            ms = pl.ds(pl.multiple_of(t * 16, 16), 16)
            rings = []
            for half in range(2):
                ring = out_ref[src, half * 4, 0, ms, :]
                for k in range(1, 16):
                    turned = pltpu.roll(out_ref[src, half * 4 + k // LEV, k % LEV, ms, :], k * 8, 1)
                    inside = ((lane16 + (4 - k * 8 + 128)) & 127) < 8
                    ring = jnp.where(inside, turned, ring)
                ring_send[s, half, ms, :] = ring.astype(BF16)
                rings.append(ring)
            edge_send[s, 0, ms, :] = jnp.where((lane16 & 7) < 4, rings[0], pltpu.roll(rings[1], 4, 1)).astype(BF16)
            edge_send[s, 1, ms, :] = jnp.where((lane16 & 7) >= 4, rings[0], pltpu.roll(rings[1], 124, 1)).astype(BF16)
            for side, first in ((0, 0), (1, ROWS - 3)):
                for r in range(3):
                    for l in range(LEV):
                        row_send[s, side, r, l, ms, :] = out_ref[src, first + r, l, ms, :].astype(BF16)
        low, high = ring_send.at[s, 0], ring_send.at[s, 1]
        plan = (
            (S_, row_send.at[s, 0], row_got.at[s, 1], N_),
            (N_, row_send.at[s, 1], row_got.at[s, 0], S_),
            (W_, edge_send.at[s, 0], edge_got.at[s, 1], E_),
            (E_, edge_send.at[s, 1], edge_got.at[s, 0], W_),
            (SW_, low, corner_got.at[s, 3], NE_),
            (SE_, low, corner_got.at[s, 2], NW_),
            (NW_, high, corner_got.at[s, 1], SE_),
            (NE_, high, corner_got.at[s, 0], SW_),
        )
        copies = []
        for d, src_ref, dst_ref, landed in plan:
            copy = pltpu.make_async_remote_copy(
                src_ref=src_ref, dst_ref=dst_ref,
                send_sem=hsend_sem.at[s, d], recv_sem=hrecv_sem.at[s, landed],
                device_id=device_at(NEIGHBOURS[d]), device_id_type=MESH)
            copy.start()
            copies.append(copy)
        return copies

    copies = send_halos(0, 0)
    for copy in ccopies:
        copy.wait()
    south_ok = jnp.where(trow > 0, 1.0, 0.0).astype(F32)
    north_ok = jnp.where(trow < N_LAT - 1, 1.0, 0.0).astype(F32)
    lane8 = lanes((ROWS, COLS))
    for block, (cen, west, east, ok) in enumerate(((S_, SW_, SE_, south_ok), (8, W_, E_, None), (N_, NW_, NE_, north_ok))):
        for half in range(2):
            for l in range(LEV):
                def pick(i):
                    if half == 0:
                        return jnp.where(lane8 < 96, coef_got[cen, i, l], coef_got[west, i, l])
                    return jnp.where(lane8 >= 32, coef_got[cen, i, l], coef_got[east, i, l])
                cu, cv, dd = pick(0), pick(1), pick(2)
                aw = jnp.maximum(cu, 0.0) + dd
                ae = dd - jnp.minimum(cu, 0.0)
                as_ = jnp.maximum(cv, 0.0) + dd
                an = dd - jnp.minimum(cv, 0.0)
                ac = 1.0 - (jnp.abs(cu) + jnp.abs(cv) + 4.0 * dd)
                for j, a in enumerate((ac, aw, ae, as_, an)):
                    a = a if ok is None else a * ok
                    for r in ((6, 7), range(8), (0, 1))[block]:
                        coefs[half, l, j, block * 8 + r - 6] = jnp.broadcast_to(a[r:r + 1], (8, COLS))

    def step_row(half, l, r, south, v, north):
        ac, aw, ae, as_, an = (coefs[half, l, j, r] for j in range(5))
        return (ac * v + aw * pltpu.roll(v, 1, 1)) + (ae * pltpu.roll(v, COLS - 1, 1) + (as_ * south + an * north))

    for s in range(SLOTS):
        for copy in copies:
            copy.wait()
        prev = max(s - 1, 0)
        for l in range(LEV):
            @pl.loop(0, MEM // 16)
            def _(t):
                ms = pl.ds(pl.multiple_of(t * 16, 16), 16)
                west, east = edge_got[s, 0, ms, :].astype(F32), edge_got[s, 1, ms, :].astype(F32)
                first = (lane16 & 7) < 4
                rings = [
                    jnp.where(first, corner_got[s, 1, ms, :].astype(F32), corner_got[s, 0, ms, :].astype(F32)) * south_ok,
                    jnp.where(first, east, west),
                    jnp.where(first, pltpu.roll(east, 124, 1), pltpu.roll(west, 4, 1)),
                    jnp.where(first, corner_got[s, 3, ms, :].astype(F32), corner_got[s, 2, ms, :].astype(F32)) * north_ok,
                ]
                mines, auxs = [], []
                for r in range(-3, ROWS + 3):
                    if 0 <= r < ROWS:
                        mine = out_ref[prev, r, l, ms, :]
                    elif r < 0:
                        mine = row_got[s, 0, r + 3, l, ms, :].astype(F32) * south_ok
                    else:
                        mine = row_got[s, 1, r - ROWS, l, ms, :].astype(F32) * north_ok
                    turn = (((r + 4) % 4) * LEV + l) * 8
                    ring = rings[(r + 4) // 4]
                    auxs.append(pltpu.roll(ring, 128 - turn, 1) if turn else ring)
                    mines.append(mine)
                for u in range(2):
                    sub = slice(u * 8, u * 8 + 8)
                    sides = []
                    for half in range(2):
                        if half == 0:
                            v = [jnp.where(lane1 < 96, m[sub], a[sub]) for m, a in zip(mines, auxs)]
                        else:
                            v = [jnp.where(lane1 >= 32, m[sub], a[sub]) for m, a in zip(mines, auxs)]
                        for step in range(STEPS):
                            v = [step_row(half, l, r + step, v[r], v[r + 1], v[r + 2]) for r in range(len(v) - 2)]
                        sides.append(v)
                    for r in range(ROWS):
                        out_ref[s, r, l, pl.ds(pl.multiple_of(t * 16 + u * 8, 8), 8), :] = jnp.where(
                            lane1 < 64, sides[0][r], sides[1][r])
        if s < SLOTS - 1:
            copies = send_halos(s, s + 1)
        if s == 0:
            arrive(3, 7)
            listed = pltpu.make_async_copy(owners_out, owners, load_sem.at[7])
            listed.start()
            listed.wait()
        observe(out_ref, s, cells, weights, values, xs, perts, innovs, last)


    turned = transforms_of(perts, innovs, tts)

    ids = [owners[0, p, 0] for p in range(PATCH)]
    left = lanes((MEM, COLS)) < MEM
    for o in range(N_LON):
        first, second = jnp.int32(PATCH), jnp.int32(PATCH)
        for p in range(PATCH):
            named = ids[p] == o
            second = jnp.where(jnp.logical_and(named, first < PATCH), p, second)
            first = jnp.where(jnp.logical_and(named, first == PATCH), p, first)
        pair = jnp.where(left, tts[first], tts[second])
        peak = jnp.maximum(jnp.max(jnp.abs(pair), axis=0, keepdims=True), 1e-30)
        held_peak[o] = peak
        held_send[o] = jnp.round(pair * (CODE / peak)).astype(jnp.int32).astype(jnp.int16)

    def parcel(k, half):
        owner = lax.rem(lon + k, N_LON)
        src, dst = ((held_send, held_got), (held_peak, held_peak_got))[half]
        return pltpu.make_async_remote_copy(
            src_ref=src.at[owner], dst_ref=dst.at[tcol], send_sem=tsend_sem.at[half, k],
            recv_sem=trecv_sem.at[half, tcol], device_id=(trow, owner), device_id_type=MESH)

    def landed(k, half):
        source = lax.rem(tcol + k, N_LON)
        src, dst = ((held_send, held_got), (held_peak, held_peak_got))[half]
        pltpu.make_async_remote_copy(
            src_ref=src.at[0], dst_ref=dst.at[source], send_sem=tsend_sem.at[half, k],
            recv_sem=trecv_sem.at[half, source], device_id=(trow, lon), device_id_type=MESH).wait_recv()

    keeps = [pltpu.make_async_copy(src.at[lon], dst.at[tcol], tsend_sem.at[i, 0])
             for i, (src, dst) in enumerate(((held_send, held_got), (held_peak, held_peak_got)))]

    @pl.when(swapping)
    def _():
        for half in range(2):
            parcel(0, half).start()

    @pl.when(jnp.logical_not(swapping))
    def _():
        for copy in keeps:
            copy.start()

    for k in range(1, N_LON):
        for half in range(2):
            parcel(k, half).start()

    analyse_members(turned, last, result, ana_out)
    backs = [
        pltpu.make_async_remote_copy(src_ref=src, dst_ref=dst, send_sem=back_sem.at[0, i], recv_sem=back_sem.at[1, i],
                                     device_id=partner, device_id_type=MESH)
        for i, (src, dst) in enumerate(
            [(back_send.at[pl.ds(c * rows, rows)], back_got.at[pl.ds(c * rows, rows)]) for c in range(4)]
            + [(back_peak, back_peak_got)])]

    @pl.when(swapping)
    def _():
        peaks = peaks_of(ana_out)
        back_peak[...] = peaks
        backs[4].start()
        for c in range(4):
            encode(ana_out, peaks, back_send, c)
            backs[c].start()
        for half in range(2):
            parcel(0, half).wait_send()
            landed(0, half)

    @pl.when(jnp.logical_not(swapping))
    def _():
        for copy in keeps:
            copy.wait()

    for k in range(1, N_LON):
        for half in range(2):
            parcel(k, half).wait_send()
            landed(k, half)

    @pl.loop(0, N_LON, unroll=2)
    def _(o):
        pair = held_got[o].astype(jnp.int32).astype(F32) * (held_peak_got[o] * (1.0 / CODE))
        held_out[2 * o] = pair[:, :MEM]
        held_out[2 * o + 1] = pltpu.roll(pair, MEM, 1)[:, :MEM]

    @pl.when(swapping)
    def _():
        backs[4].wait()
        peaks = back_peak_got[...] * (1.0 / CODE)
        for c in range(4):
            backs[c].wait()

            @pl.loop(c * 16, c * 16 + 16, unroll=4)
            def _(m):
                at = pl.ds(pl.multiple_of(m * 32, 32), 32)
                ana_out[at, :] = back_got[at, :].astype(jnp.int32).astype(F32) * peaks


VMEM_SPEC = pl.BlockSpec(memory_space=pltpu.VMEM)
SMEM_SPEC = pl.BlockSpec(memory_space=pltpu.SMEM)
ANY_SPEC = pl.BlockSpec(memory_space=pl.ANY)


def cycle(ensemble, cu, cv, dd, cells, counts, values, errors, owners):
    return pl.pallas_call(
        cycle_kernel,
        out_shape=(jax.ShapeDtypeStruct((MEM * LEV * ROWS, COLS), F32),
                   jax.ShapeDtypeStruct((N_LON * PCAP, MEM, MEM), F32),
                   jax.ShapeDtypeStruct(owners.shape, jnp.int32)),
        in_specs=[ANY_SPEC] * 5 + [SMEM_SPEC, ANY_SPEC, VMEM_SPEC, ANY_SPEC],
        out_specs=(VMEM_SPEC, VMEM_SPEC, ANY_SPEC),
        scratch_shapes=[
            pltpu.VMEM((4, 256, SLOTS * OBS), BF16),
            pltpu.VMEM((SLOTS, PATCH, OBS), F32),
            pltpu.VMEM((PATCH * MEM, 256), F32),
            pltpu.SMEM((1, PATCH, 1), jnp.int32),
            pltpu.VMEM((SLOTS, ROWS, LEV, MEM, COLS), F32),
            pltpu.VMEM((SLOTS, 4, 1, PATCH, OBS), jnp.int32),
            pltpu.VMEM((SLOTS, PATCH, OBS), F32),
            pltpu.VMEM((SLOTS, 1, PATCH, OBS), F32),
            pltpu.VMEM((SLOTS, PATCH, OBS), F32),
            pltpu.VMEM((PATCH, 2 * MEM, 256), BF16),
            pltpu.VMEM((MEM * LEV * ROWS, COLS), F32),
            pltpu.VMEM((9, 3, LEV, ROWS, COLS), F32),
            pltpu.VMEM((2, LEV, 5, 12, 8, COLS), F32),
            pltpu.VMEM((SLOTS, 2, 3, LEV, MEM, COLS), BF16),
            pltpu.VMEM((SLOTS, 2, MEM, COLS), BF16),
            pltpu.VMEM((SLOTS, 2, MEM, COLS), BF16),
            pltpu.VMEM((SLOTS, 2, 3, LEV, MEM, COLS), BF16),
            pltpu.VMEM((SLOTS, 2, MEM, COLS), BF16),
            pltpu.VMEM((SLOTS, 4, MEM, COLS), BF16),
            pltpu.SemaphoreType.DMA((9,)),
            pltpu.SemaphoreType.DMA((9,)),
            pltpu.VMEM((MEM * LEV * ROWS, COLS), jnp.int16),
            pltpu.VMEM((MEM * LEV * ROWS, COLS), jnp.int16),
            pltpu.VMEM((LEV * ROWS, COLS), F32),
            pltpu.VMEM((LEV * ROWS, COLS), F32),
            pltpu.SemaphoreType.DMA((2, 5)),
            pltpu.SemaphoreType.DMA((8,)),
            pltpu.SemaphoreType.DMA((8,)),
            pltpu.SemaphoreType.DMA((SLOTS, 8)),
            pltpu.SemaphoreType.DMA((SLOTS, 8)),
            pltpu.VMEM((PATCH * MEM, 256), F32),
            pltpu.VMEM((PATCH + 1, MEM, COLS), F32),
            pltpu.VMEM((MEM * LEV * ROWS, COLS), jnp.int16),
            pltpu.VMEM((MEM * LEV * ROWS, COLS), jnp.int16),
            pltpu.VMEM((LEV * ROWS, COLS), F32),
            pltpu.VMEM((LEV * ROWS, COLS), F32),
            pltpu.SemaphoreType.DMA((2, 5)),
            pltpu.VMEM((N_LON, MEM, COLS), jnp.int16),
            pltpu.VMEM((N_LON, MEM, COLS), jnp.int16),
            pltpu.VMEM((N_LON, 1, COLS), F32),
            pltpu.VMEM((N_LON, 1, COLS), F32),
            pltpu.SemaphoreType.DMA((2, N_LON)),
            pltpu.SemaphoreType.DMA((2, N_LON)),
        ],
        compiler_params=pltpu.CompilerParams(
            collective_id=0, has_side_effects=True, vmem_limit_bytes=60 * 1024 * 1024),
        name="cycle",
    )(ensemble.reshape(MEM * LEV * ROWS, COLS), cu, cv, dd, cells, counts, values, errors, owners)


def body(ensemble, courant_lon, courant_lat, diffusion, obs_cells, obs_counts, obs_values, obs_errors, owners):
    analysis, held, _ = cycle(ensemble, courant_lon, courant_lat, diffusion,
                              obs_cells, obs_counts, obs_values, obs_errors, owners)
    return analysis.reshape(MEM, LEV, ROWS, COLS), held.reshape(1, 1, N_LON, PCAP, MEM, MEM)


def solution(mesh):
    placed = (
        P(None, None, "lat", "lon"),
        P(None, "lat", "lon"),
        P(None, "lat", "lon"),
        P(None, "lat", "lon"),
        P(None, None, "lat", "lon", None),
        P(None, "lat", "lon"),
        P(None, "lat", "lon", None),
        P(None, "lat", "lon", None),
        P("lat", "lon", None),
    )
    return jax.shard_map(
        body,
        mesh=mesh,
        in_specs=placed,
        out_specs=(P(None, None, "lat", "lon"), P("lat", "lon", None, None, None, None)),
        check_vma=False,
    )
```

```python
import functools

import jax
import jax.numpy as jnp
from jax import lax
from jax.experimental import pallas as pl
from jax.experimental.pallas import tpu as pltpu
from jax.sharding import PartitionSpec as P

PCAP = 2
SLOTS = 4
STEPS = 3
NS_ITERS = 6
MEM = 64
LEV = 4
ROWS = 8
COLS = 128
PATCH = 16
OBS = 128
N_LAT = 8
N_LON = 16
F32 = jnp.float32
BF16 = jnp.bfloat16
NEIGHBOURS = ((-1, 0), (1, 0), (0, -1), (0, 1), (-1, -1), (-1, 1), (1, -1), (1, 1))
S_, N_, W_, E_, SW_, SE_, NW_, NE_ = range(8)


MESH = pl.DeviceIdType.MESH


def tile_to_device(row, col):
    return row - row % 2 + col % 2, col - col % 2 + row % 2


def swap_partner(lat, lon):
    swapping = (lat % 2 + lon % 2) % 2 == 1
    return swapping, (lat + 1 - 2 * (lat % 2), lon + 1 - 2 * (lon % 2))


def lanes(shape):
    return lax.broadcasted_iota(jnp.int32, shape, len(shape) - 1)


CODE = 32767.0


def peaks_of(ref):
    def grow(m, peak):
        return jnp.maximum(peak, jnp.abs(ref[pl.ds(pl.multiple_of(m * 32, 32), 32), :]))
    return jnp.maximum(lax.fori_loop(0, MEM, grow, jnp.zeros((32, COLS), F32), unroll=8), 1e-30)


def encode(ref, peaks, code_ref, chunk):
    factor = CODE / peaks

    @pl.loop(chunk * 16, chunk * 16 + 16, unroll=4)
    def _(m):
        at = pl.ds(pl.multiple_of(m * 32, 32), 32)
        code_ref[at, :] = jnp.round(ref[at, :] * factor).astype(jnp.int32).astype(jnp.int16)


def butterfly(parts):
    parts = list(parts)
    lane = lanes(parts[0].shape)
    for bit in (1, 2, 4, 8):
        keep = (lane & (8 * bit)) == 0
        for i in range(16):
            if i & bit:
                continue
            a, b = parts[i], parts[i + bit]
            parts[i] = jnp.where(keep, a, pltpu.roll(b, 8 * bit, 1))
            parts[i + bit] = jnp.where(keep, pltpu.roll(a, 128 - 8 * bit, 1), b)
    return parts


def split(x):
    hi = x.astype(BF16)
    return hi, (x - hi.astype(F32)).astype(BF16)


def dot(a, b):
    return jnp.dot(a, b, preferred_element_type=F32)


def dot_t(a, b):
    return lax.dot_general(a, b, (((1,), (1,)), ((), ())), preferred_element_type=F32)


def block_diagonal(x):
    block = lanes(x.shape) // 64
    return jnp.concatenate([jnp.where(block == i, x, jnp.zeros_like(x)) for i in range(4)], axis=0)


def times(x_parts, y_parts):
    yh, yl = y_parts
    n = sum(h.shape[0] for h, _ in x_parts)
    his = [h for h, _ in x_parts]
    los = [l for _, l in x_parts]
    top = dot(jnp.concatenate(his + los, axis=0), yh)
    low = dot(jnp.concatenate(his, axis=0), yl)
    total = top[:n] + top[n:] + low
    outs, at = [], 0
    for h, _ in x_parts:
        outs.append(total[at:at + h.shape[0]])
        at += h.shape[0]
    return outs


def cell_weights(counts_ref, errors_ref, slot):
    shape = (PATCH, OBS)
    patch = lax.broadcasted_iota(jnp.int32, shape, 0)
    count = jnp.zeros(shape, jnp.int32)
    for p in range(PATCH):
        count = jnp.where(patch == p, counts_ref[slot, 0, p], count)
    return jnp.where(lanes(shape) < count, 1.0 / errors_ref[slot, 0], 0.0)


def observe(states_ref, slot, cells, weights, values, xs, perts, innovs, last):
    @pl.loop(0, 8)
    def _(k):
        q, t = k // 4, k % 4
        halves = []
        for u in range(2):
            ms = pl.ds(pl.multiple_of(t * 16 + u * 8, 8), 8)
            parts = [states_ref[slot, i % 8, q * 2 + i // 8, ms, :] for i in range(16)]
            halves.append(butterfly(parts))
        cs = pl.ds(pl.multiple_of(q * 128, 128), 128)
        for p in range(PATCH):
            x = jnp.concatenate([halves[0][p], halves[1][p]], axis=0)
            hi, lo = split(x)
            xs[p, pl.ds(pl.multiple_of(t * 16, 16), 16), cs] = hi
            xs[p, pl.ds(pl.multiple_of(MEM + t * 16, 16), 16), cs] = lo
            if slot == SLOTS - 1:
                last[pl.ds(pl.multiple_of(p * MEM + t * 16, 16), 16), cs] = x

    cell_id = lax.broadcasted_iota(jnp.int32, (256, OBS), 0).astype(F32).astype(BF16)
    one, zero = jnp.ones((256, OBS), BF16), jnp.zeros((256, OBS), BF16)

    @pl.loop(0, PATCH, unroll=4)
    def _(p):
        w = zero
        for corner in range(4):
            idx = cells[slot, corner, 0, pl.ds(p, 1), :].astype(F32)
            idx = jnp.broadcast_to(idx, (256, OBS)).astype(BF16)
            w = w + jnp.where(cell_id == idx, one, zero)
        both = dot(xs[p], w)
        equivalent = 0.25 * (both[:MEM] + both[MEM:])
        mean = jnp.sum(equivalent, axis=0, keepdims=True) * (1.0 / MEM)
        weight = weights[slot, pl.ds(p, 1), :]
        pert = ((equivalent - mean) * weight).astype(BF16)
        perts[p // 4, pl.ds(pl.multiple_of((p % 4) * MEM, MEM), MEM), slot * OBS:(slot + 1) * OBS] = pert
        innovs[slot, pl.ds(p, 1), :] = (values[slot, 0, pl.ds(p, 1), :] - mean) * weight


def transforms_of(perts, innovs, tts):
    shape = (MEM, 256)
    block = lanes(shape) // 64
    eye = (lax.broadcasted_iota(jnp.int32, shape, 0) == (lanes(shape) & 63)).astype(F32)
    innov = jnp.concatenate([innovs[s] for s in range(SLOTS)], axis=1).astype(BF16)
    ys, zs, alongs, sizes = [], [], [], []
    for g in range(4):
        pg = perts[g]
        full = dot_t(pg, pg)
        gram = full[0:MEM]
        for i in range(1, 4):
            gram = jnp.where(block == i, full[i * MEM:(i + 1) * MEM], gram)
        al = dot_t(innov, pg)
        row = lax.broadcasted_iota(jnp.int32, al.shape, 0)
        al = jnp.sum(jnp.where(row == g * 4 + lanes(al.shape) // 64, al, 0.0), axis=0, keepdims=True)
        alongs.append(al)
        amat = gram + (MEM - 1.0) * eye
        sq = jnp.sum(amat * amat, axis=0, keepdims=True)
        blk1 = lanes((1, 256)) // 64
        size = jnp.zeros((1, 256), F32)
        for i in range(4):
            total = jnp.sum(jnp.where(blk1 == i, sq, 0.0), axis=1, keepdims=True)
            size = jnp.where(blk1 == i, total, size)
        size = jnp.sqrt(size)
        sizes.append(size)
        ys.append(amat / size)
        zs.append(None)
    for it in range(NS_ITERS):
        mixers = []
        for g in range(4):
            yh, yl = split(ys[g])
            if it == 0:
                zy = ys[g]
            else:
                (zy,) = times([split(zs[g])], (block_diagonal(yh), block_diagonal(yl)))
            mixers.append(1.5 * eye - 0.5 * zy)
        for g in range(4):
            mh, ml = split(mixers[g])
            md = (block_diagonal(mh), block_diagonal(ml))
            if it == 0:
                (ys[g],) = times([split(ys[g])], md)
                zs[g] = mixers[g]
            elif it < NS_ITERS - 1:
                ys[g], zs[g] = times([split(ys[g]), split(zs[g])], md)
            else:
                (zs[g],) = times([split(zs[g])], md)
    eye2 = (lax.broadcasted_iota(jnp.int32, (MEM, 128), 0) == (lanes((MEM, 128)) & 63)).astype(F32)
    size0 = jnp.sqrt(jnp.full((1, 128), MEM * (MEM - 1.0) * (MEM - 1.0), F32))
    y0 = (MEM - 1.0) / size0
    z0 = jnp.ones((1, 128), F32)
    for it in range(NS_ITERS):
        m0 = 1.5 - 0.5 * z0 * y0
        y0, z0 = y0 * m0, m0 * z0
    empty = eye2 * (z0 * jnp.sqrt((MEM - 1.0) / size0))

    tts[PATCH] = empty
    turned = []
    for g in range(4):
        zh, zl = split(zs[g])
        zd = (block_diagonal(zh), block_diagonal(zl))
        (first,) = times([split(jnp.broadcast_to(alongs[g], (16, 256)))], zd)
        (second,) = times([split(first)], zd)
        tt = zs[g] * jnp.sqrt((MEM - 1.0) / sizes[g]) + second[0:1] / sizes[g]
        turned.append(tt)
        both = jnp.transpose(jnp.concatenate([tt, tt], axis=0))
        for i in range(4):
            tts[g * 4 + i] = both[i * MEM:(i + 1) * MEM]
    return turned


def analyse_members(turned, last, result, out_ref):
    for g in range(4):
        th, tl = split(turned[g])
        thd, tld = block_diagonal(th), block_diagonal(tl)
        devs, means = [], []
        for i in range(4):
            x = last[pl.ds((g * 4 + i) * MEM, MEM), :]
            mean = jnp.sum(x, axis=0, keepdims=True) * (1.0 / MEM)
            devs.append(x - mean)
            means.append(mean)
        dh, dl = split(jnp.concatenate(devs, axis=0))
        ana = dot(thd, dh) + dot(tld, dh) + dot(thd, dl)
        for i in range(4):
            result[pl.ds((g * 4 + i) * MEM, MEM), :] = ana[i * MEM:(i + 1) * MEM] + means[i]

    @pl.loop(0, 16)
    def _(k):
        q, t = k // 8, k % 8
        cs = pl.ds(pl.multiple_of(q * 128, 128), 128)
        parts = [result[pl.ds(pl.multiple_of(p * MEM + t * 8, 8), 8), cs] for p in range(16)]
        for i, x in enumerate(butterfly(parts)):
            out_ref[pl.ds(t * 256 + q * 16 + i, 8, stride=32), :] = x


def cycle_kernel(ens_ref, cu_ref, cv_ref, dd_ref, cells_ref, counts_ref, values_ref, errors_ref, owners_ref,
                 ana_out, held_out, owners_out,
                 perts, innovs, last, owners,
                 out_ref, cells, weights, values, weight_send, xs,
                 tiles, coef_got, coefs, row_send, ring_send, edge_send,
                 row_got, edge_got, corner_got,
                 load_sem, swap_sem, code_send, code_got, peak_send, peak_got, code_sem, csend_sem, crecv_sem,
                 hsend_sem, hrecv_sem,
                 result, tts, back_send, back_got, back_peak, back_peak_got, back_sem,
                 held_send, held_got, held_peak, held_peak_got, tsend_sem, trecv_sem, rings, field, shifts):
    lat, lon = lax.axis_index("lat"), lax.axis_index("lon")
    trow, tcol = tile_to_device(lat, lon)

    def device_at(step):
        row = lax.rem(trow + step[0] + N_LAT, N_LAT)
        col = lax.rem(tcol + step[1] + N_LON, N_LON)
        return tile_to_device(row, col)

    barrier = pltpu.get_barrier_semaphore()
    for step in NEIGHBOURS:
        pl.semaphore_signal(barrier, inc=1, device_id=device_at(step),
                            device_id_type=MESH)
    swapping, partner = swap_partner(lat, lon)
    for k in range(1, N_LON):
        pl.semaphore_signal(barrier, inc=1, device_id=tile_to_device(lat, lax.rem(tcol + k, N_LON)), device_id_type=MESH)

    @pl.when(swapping)
    def _():
        pl.semaphore_signal(barrier, inc=1, device_id=tile_to_device(lat, tcol), device_id_type=MESH)

    moves = [(ref, coef_got.at[8, i]) for i, ref in enumerate((cu_ref, cv_ref, dd_ref))]
    moves += [(cells_ref, cells), (weight_send, weights), (values_ref, values), (owners_ref, owners_out)]
    for slot in range(SLOTS):
        weight_send[slot] = cell_weights(counts_ref, errors_ref, slot)
    load = pltpu.make_async_copy(ens_ref, tiles, load_sem.at[8])
    load.start()
    rows = MEM * LEV * ROWS // 4
    sent = [
        pltpu.make_async_remote_copy(src_ref=src, dst_ref=dst, send_sem=code_sem.at[0, i], recv_sem=code_sem.at[1, i],
                                     device_id=partner, device_id_type=MESH)
        for i, (src, dst) in enumerate(
            [(code_send.at[pl.ds(c * rows, rows)], code_got.at[pl.ds(c * rows, rows)]) for c in range(4)]
            + [(peak_send, peak_got)])]
    kept = [pltpu.make_async_copy(src, dst, load_sem.at[i]) for i, (src, dst) in enumerate(moves)]
    swapped = [
        pltpu.make_async_remote_copy(src_ref=src, dst_ref=dst, send_sem=load_sem.at[i], recv_sem=swap_sem.at[i],
                                     device_id=partner, device_id_type=MESH)
        for i, (src, dst) in enumerate(moves)]

    def arrive(first, last):
        @pl.when(swapping)
        def _():
            for copy in swapped[first:last]:
                copy.wait()

        @pl.when(jnp.logical_not(swapping))
        def _():
            for copy in kept[first:last]:
                copy.wait()

    pl.semaphore_wait(barrier, jnp.where(swapping, 8 + N_LON, 7 + N_LON))

    @pl.when(swapping)
    def _():
        for copy in swapped[:3]:
            copy.start()
        load.wait()
        peaks = peaks_of(tiles)
        peak_send[...] = peaks
        sent[4].start()
        for c in range(4):
            encode(tiles, peaks, code_send, c)
            sent[c].start()
        for copy in swapped[3:]:
            copy.start()
        sent[4].wait()
        peaks = peak_got[...]
        for c in range(4):
            sent[c].wait()

            @pl.loop(c * 16, c * 16 + 16)
            def _(m):
                at = pl.ds(pl.multiple_of(m * 32, 32), 32)
                tiles[at, :] = code_got[at, :].astype(jnp.int32).astype(F32) * (peaks * (1.0 / CODE))

    @pl.when(jnp.logical_not(swapping))
    def _():
        for copy in kept:
            copy.start()
        load.wait()

    arrive(0, 3)
    opposite = (N_, S_, E_, W_, NE_, NW_, SE_, SW_)
    ccopies = []
    for d, step in enumerate(NEIGHBOURS):
        copy = pltpu.make_async_remote_copy(
            src_ref=coef_got.at[8], dst_ref=coef_got.at[opposite[d]],
            send_sem=csend_sem.at[d], recv_sem=crecv_sem.at[opposite[d]],
            device_id=device_at(step), device_id_type=MESH)
        copy.start()
        ccopies.append(copy)

    @pl.loop(0, LEV)
    def _(l):
        for r in range(ROWS):
            for t in range(8):
                out_ref[0, r, l, pl.ds(t * 8, 8), :] = tiles[pl.ds(t * 256 + l * ROWS + r, 8, stride=32), :]

    lane16 = lanes((16, COLS))
    lane1 = lanes((8, COLS))

    def send_halos(src, s):
        @pl.loop(0, MEM // 16)
        def _(t):
            ms = pl.ds(pl.multiple_of(t * 16, 16), 16)
            rings = []
            for half in range(2):
                ring = out_ref[src, half * 4, 0, ms, :]
                for k in range(1, 16):
                    turned = pltpu.roll(out_ref[src, half * 4 + k // LEV, k % LEV, ms, :], k * 8, 1)
                    inside = ((lane16 + (4 - k * 8 + 128)) & 127) < 8
                    ring = jnp.where(inside, turned, ring)
                ring_send[s, half, ms, :] = ring.astype(BF16)
                rings.append(ring)
            edge_send[s, 0, ms, :] = jnp.where((lane16 & 7) < 4, rings[0], pltpu.roll(rings[1], 4, 1)).astype(BF16)
            edge_send[s, 1, ms, :] = jnp.where((lane16 & 7) >= 4, rings[0], pltpu.roll(rings[1], 124, 1)).astype(BF16)
            for side, first in ((0, 0), (1, ROWS - 3)):
                for r in range(3):
                    for l in range(LEV):
                        row_send[s, side, r, l, ms, :] = out_ref[src, first + r, l, ms, :].astype(BF16)
        low, high = ring_send.at[s, 0], ring_send.at[s, 1]
        plan = (
            (S_, row_send.at[s, 0], row_got.at[s, 1], N_),
            (N_, row_send.at[s, 1], row_got.at[s, 0], S_),
            (W_, edge_send.at[s, 0], edge_got.at[s, 1], E_),
            (E_, edge_send.at[s, 1], edge_got.at[s, 0], W_),
            (SW_, low, corner_got.at[s, 3], NE_),
            (SE_, low, corner_got.at[s, 2], NW_),
            (NW_, high, corner_got.at[s, 1], SE_),
            (NE_, high, corner_got.at[s, 0], SW_),
        )
        copies = []
        for d, src_ref, dst_ref, landed in plan:
            copy = pltpu.make_async_remote_copy(
                src_ref=src_ref, dst_ref=dst_ref,
                send_sem=hsend_sem.at[s, d], recv_sem=hrecv_sem.at[s, landed],
                device_id=device_at(NEIGHBOURS[d]), device_id_type=MESH)
            copy.start()
            copies.append(copy)
        return copies

    copies = send_halos(0, 0)
    for copy in ccopies:
        copy.wait()
    south_ok = jnp.where(trow > 0, 1.0, 0.0).astype(F32)
    north_ok = jnp.where(trow < N_LAT - 1, 1.0, 0.0).astype(F32)
    lane8 = lanes((ROWS, COLS))
    for block, (cen, west, east, ok) in enumerate(((S_, SW_, SE_, south_ok), (8, W_, E_, None), (N_, NW_, NE_, north_ok))):
        for half in range(2):
            for l in range(LEV):
                def pick(i):
                    if half == 0:
                        return jnp.where(lane8 < 96, coef_got[cen, i, l], coef_got[west, i, l])
                    return jnp.where(lane8 >= 32, coef_got[cen, i, l], coef_got[east, i, l])
                cu, cv, dd = pick(0), pick(1), pick(2)
                aw = jnp.maximum(cu, 0.0) + dd
                ae = dd - jnp.minimum(cu, 0.0)
                as_ = jnp.maximum(cv, 0.0) + dd
                an = dd - jnp.minimum(cv, 0.0)
                ac = 1.0 - (jnp.abs(cu) + jnp.abs(cv) + 4.0 * dd)
                for j, a in enumerate((ac, aw, ae, as_, an)):
                    a = a if ok is None else a * ok
                    for r in ((6, 7), range(8), (0, 1))[block]:
                        coefs[half, l, j, block * 8 + r - 6] = jnp.broadcast_to(a[r:r + 1], (8, COLS))

    from_at = lax.broadcasted_iota(jnp.int32, (256, 256), 0) & 127
    to_at = lanes((256, 256))
    step_at = jnp.where(to_at < 128, 1, 127)
    shifts[...] = jnp.where(((from_at + step_at) & 127) == (to_at & 127), 1.0, 0.0).astype(BF16)

    for s in range(SLOTS):
        for copy in copies:
            copy.wait()
        prev = max(s - 1, 0)

        for t in range(MEM // 16):
            ms = pl.ds(t * 16, 16)
            west, east = edge_got[s, 0, ms, :].astype(F32), edge_got[s, 1, ms, :].astype(F32)
            first = (lane16 & 7) < 4
            rings[0, ms, :] = jnp.where(first, corner_got[s, 1, ms, :].astype(F32), corner_got[s, 0, ms, :].astype(F32)) * south_ok
            rings[1, ms, :] = jnp.where(first, east, west)
            rings[2, ms, :] = jnp.where(first, pltpu.roll(east, 124, 1), pltpu.roll(west, 4, 1))
            rings[3, ms, :] = jnp.where(first, corner_got[s, 3, ms, :].astype(F32), corner_got[s, 2, ms, :].astype(F32)) * north_ok

        for l in range(LEV):
            @pl.loop(0, MEM // 16)
            def _(t):
                ms = pl.ds(pl.multiple_of(t * 16, 16), 16)
                for r in range(-3, ROWS + 3):
                    if 0 <= r < ROWS:
                        mine = out_ref[prev, r, l, ms, :]
                    elif r < 0:
                        mine = row_got[s, 0, r + 3, l, ms, :].astype(F32) * south_ok
                    else:
                        mine = row_got[s, 1, r - ROWS, l, ms, :].astype(F32) * north_ok
                    turn = (((r + 4) % 4) * LEV + l) * 8
                    aux = rings[(r + 4) // 4, ms, :]
                    aux = pltpu.roll(aux, 128 - turn, 1) if turn else aux
                    field[0, l, 0, r + 3, ms, :] = jnp.where(lane16 < 96, mine, aux)
                    field[0, l, 1, r + 3, ms, :] = jnp.where(lane16 >= 32, mine, aux)

        for step in range(STEPS):
            src, dst = step % 2, (step + 1) % 2

            @pl.loop(0, LEV)
            def _(l):
                inner = range(1 + step, ROWS + 5 - step)
                pieces = [jnp.concatenate(split(field[src, l, half, r, pl.ds(0, MEM // 2), :]), axis=1)
                          for r in inner for half in range(2)]
                moved = dot(jnp.concatenate(pieces, axis=0), shifts[...])
                for r in inner:
                    factors = [[coefs[half, l, j, r - 1] for j in range(5)] for half in range(2)]
                    for t in range(MEM // 8):
                        ms = pl.ds(t * 8, 8)
                        new = []
                        for half in range(2):
                            ac, aw, ae, as_, an = factors[half]
                            v = field[src, l, half, r, ms, :]
                            if t < MEM // 16:
                                at = ((r - inner[0]) * 2 + half) * (MEM // 2) + t * 8
                                west, east = moved[at:at + 8, :COLS], moved[at:at + 8, COLS:]
                            else:
                                west, east = pltpu.roll(v, 1, 1), pltpu.roll(v, COLS - 1, 1)
                            new.append((ac * v + as_ * field[src, l, half, r - 1, ms, :])
                                       + an * field[src, l, half, r + 1, ms, :]
                                       + (aw * west + ae * east))
                        if step < STEPS - 1:
                            field[dst, l, 0, r, ms, :] = new[0]
                            field[dst, l, 1, r, ms, :] = new[1]
                        else:
                            out_ref[s, r - 3, l, ms, :] = jnp.where(lane1 < 64, new[0], new[1])

        if s < SLOTS - 1:
            copies = send_halos(s, s + 1)
        if s == 0:
            arrive(3, 7)
            listed = pltpu.make_async_copy(owners_out, owners, load_sem.at[7])
            listed.start()
            listed.wait()
        observe(out_ref, s, cells, weights, values, xs, perts, innovs, last)


    turned = transforms_of(perts, innovs, tts)

    ids = [owners[0, 0, p] for p in range(PATCH)]
    left = lanes((MEM, COLS)) < MEM
    for o in range(N_LON):
        first, second = jnp.int32(PATCH), jnp.int32(PATCH)
        for p in range(PATCH):
            named = ids[p] == o
            second = jnp.where(jnp.logical_and(named, first < PATCH), p, second)
            first = jnp.where(jnp.logical_and(named, first == PATCH), p, first)
        pair = jnp.where(left, tts[first], tts[second])
        peak = jnp.maximum(jnp.max(jnp.abs(pair), axis=0, keepdims=True), 1e-30)
        held_peak[o] = peak
        held_send[o] = jnp.round(pair * (CODE / peak)).astype(jnp.int32).astype(jnp.int16)

    def parcel(k, half):
        owner = lax.rem(lon + k, N_LON)
        src, dst = ((held_send, held_got), (held_peak, held_peak_got))[half]
        return pltpu.make_async_remote_copy(
            src_ref=src.at[owner], dst_ref=dst.at[tcol], send_sem=tsend_sem.at[half, k],
            recv_sem=trecv_sem.at[half, tcol], device_id=(trow, owner), device_id_type=MESH)

    def landed(k, half):
        source = lax.rem(tcol + k, N_LON)
        src, dst = ((held_send, held_got), (held_peak, held_peak_got))[half]
        pltpu.make_async_remote_copy(
            src_ref=src.at[0], dst_ref=dst.at[source], send_sem=tsend_sem.at[half, k],
            recv_sem=trecv_sem.at[half, source], device_id=(trow, lon), device_id_type=MESH).wait_recv()

    keeps = [pltpu.make_async_copy(src.at[lon], dst.at[tcol], tsend_sem.at[i, 0])
             for i, (src, dst) in enumerate(((held_send, held_got), (held_peak, held_peak_got)))]

    @pl.when(swapping)
    def _():
        for half in range(2):
            parcel(0, half).start()

    @pl.when(jnp.logical_not(swapping))
    def _():
        for copy in keeps:
            copy.start()

    for k in range(1, N_LON):
        for half in range(2):
            parcel(k, half).start()

    analyse_members(turned, last, result, ana_out)
    backs = [
        pltpu.make_async_remote_copy(src_ref=src, dst_ref=dst, send_sem=back_sem.at[0, i], recv_sem=back_sem.at[1, i],
                                     device_id=partner, device_id_type=MESH)
        for i, (src, dst) in enumerate(
            [(back_send.at[pl.ds(c * rows, rows)], back_got.at[pl.ds(c * rows, rows)]) for c in range(4)]
            + [(back_peak, back_peak_got)])]

    @pl.when(swapping)
    def _():
        peaks = peaks_of(ana_out)
        back_peak[...] = peaks
        backs[4].start()
        for c in range(4):
            encode(ana_out, peaks, back_send, c)
            backs[c].start()
        for half in range(2):
            parcel(0, half).wait_send()
            landed(0, half)

    @pl.when(jnp.logical_not(swapping))
    def _():
        for copy in keeps:
            copy.wait()

    for k in range(1, N_LON):
        for half in range(2):
            parcel(k, half).wait_send()
            landed(k, half)

    @pl.loop(0, N_LON, unroll=2)
    def _(o):
        pair = held_got[o].astype(jnp.int32).astype(F32) * (held_peak_got[o] * (1.0 / CODE))
        held_out[2 * o] = pair[:, :MEM]
        held_out[2 * o + 1] = pltpu.roll(pair, MEM, 1)[:, :MEM]

    @pl.when(swapping)
    def _():
        backs[4].wait()
        peaks = back_peak_got[...] * (1.0 / CODE)
        for c in range(4):
            backs[c].wait()

            @pl.loop(c * 16, c * 16 + 16, unroll=4)
            def _(m):
                at = pl.ds(pl.multiple_of(m * 32, 32), 32)
                ana_out[at, :] = back_got[at, :].astype(jnp.int32).astype(F32) * peaks


VMEM_SPEC = pl.BlockSpec(memory_space=pltpu.VMEM)
SMEM_SPEC = pl.BlockSpec(memory_space=pltpu.SMEM)
ANY_SPEC = pl.BlockSpec(memory_space=pl.ANY)


def cycle(ensemble, cu, cv, dd, cells, counts, values, errors, owners):
    return pl.pallas_call(
        cycle_kernel,
        out_shape=(jax.ShapeDtypeStruct((MEM * LEV * ROWS, COLS), F32),
                   jax.ShapeDtypeStruct((N_LON * PCAP, MEM, MEM), F32),
                   jax.ShapeDtypeStruct(owners.shape, jnp.int32)),
        in_specs=[ANY_SPEC] * 5 + [SMEM_SPEC, ANY_SPEC, VMEM_SPEC, ANY_SPEC],
        out_specs=(VMEM_SPEC, VMEM_SPEC, ANY_SPEC),
        scratch_shapes=[
            pltpu.VMEM((4, 256, SLOTS * OBS), BF16),
            pltpu.VMEM((SLOTS, PATCH, OBS), F32),
            pltpu.VMEM((PATCH * MEM, 256), F32),
            pltpu.SMEM((1, 1, PATCH), jnp.int32),
            pltpu.VMEM((SLOTS, ROWS, LEV, MEM, COLS), F32),
            pltpu.VMEM((SLOTS, 4, 1, PATCH, OBS), jnp.int32),
            pltpu.VMEM((SLOTS, PATCH, OBS), F32),
            pltpu.VMEM((SLOTS, 1, PATCH, OBS), F32),
            pltpu.VMEM((SLOTS, PATCH, OBS), F32),
            pltpu.VMEM((PATCH, 2 * MEM, 256), BF16),
            pltpu.VMEM((MEM * LEV * ROWS, COLS), F32),
            pltpu.VMEM((9, 3, LEV, ROWS, COLS), F32),
            pltpu.VMEM((2, LEV, 5, 12, 8, COLS), F32),
            pltpu.VMEM((SLOTS, 2, 3, LEV, MEM, COLS), BF16),
            pltpu.VMEM((SLOTS, 2, MEM, COLS), BF16),
            pltpu.VMEM((SLOTS, 2, MEM, COLS), BF16),
            pltpu.VMEM((SLOTS, 2, 3, LEV, MEM, COLS), BF16),
            pltpu.VMEM((SLOTS, 2, MEM, COLS), BF16),
            pltpu.VMEM((SLOTS, 4, MEM, COLS), BF16),
            pltpu.SemaphoreType.DMA((9,)),
            pltpu.SemaphoreType.DMA((9,)),
            pltpu.VMEM((MEM * LEV * ROWS, COLS), jnp.int16),
            pltpu.VMEM((MEM * LEV * ROWS, COLS), jnp.int16),
            pltpu.VMEM((LEV * ROWS, COLS), F32),
            pltpu.VMEM((LEV * ROWS, COLS), F32),
            pltpu.SemaphoreType.DMA((2, 5)),
            pltpu.SemaphoreType.DMA((8,)),
            pltpu.SemaphoreType.DMA((8,)),
            pltpu.SemaphoreType.DMA((SLOTS, 8)),
            pltpu.SemaphoreType.DMA((SLOTS, 8)),
            pltpu.VMEM((PATCH * MEM, 256), F32),
            pltpu.VMEM((PATCH + 1, MEM, COLS), F32),
            pltpu.VMEM((MEM * LEV * ROWS, COLS), jnp.int16),
            pltpu.VMEM((MEM * LEV * ROWS, COLS), jnp.int16),
            pltpu.VMEM((LEV * ROWS, COLS), F32),
            pltpu.VMEM((LEV * ROWS, COLS), F32),
            pltpu.SemaphoreType.DMA((2, 5)),
            pltpu.VMEM((N_LON, MEM, COLS), jnp.int16),
            pltpu.VMEM((N_LON, MEM, COLS), jnp.int16),
            pltpu.VMEM((N_LON, 1, COLS), F32),
            pltpu.VMEM((N_LON, 1, COLS), F32),
            pltpu.SemaphoreType.DMA((2, N_LON)),
            pltpu.SemaphoreType.DMA((2, N_LON)),
            pltpu.VMEM((4, MEM, COLS), F32),
            pltpu.VMEM((2, LEV, 2, ROWS + 6, MEM, COLS), F32),
            pltpu.VMEM((256, 256), BF16),
        ],
        compiler_params=pltpu.CompilerParams(
            collective_id=0, has_side_effects=True, vmem_limit_bytes=60 * 1024 * 1024),
        name="cycle",
    )(ensemble.reshape(MEM * LEV * ROWS, COLS), cu, cv, dd, cells, counts, values, errors, owners)


def body(ensemble, courant_lon, courant_lat, diffusion, obs_cells, obs_counts, obs_values, obs_errors, owners):
    analysis, held, _ = cycle(ensemble, courant_lon, courant_lat, diffusion,
                              obs_cells, obs_counts, obs_values, obs_errors, owners.transpose(0, 2, 1))
    return analysis.reshape(MEM, LEV, ROWS, COLS), held.reshape(1, 1, N_LON, PCAP, MEM, MEM)


def solution(mesh):
    placed = (
        P(None, None, "lat", "lon"),
        P(None, "lat", "lon"),
        P(None, "lat", "lon"),
        P(None, "lat", "lon"),
        P(None, None, "lat", "lon", None),
        P(None, "lat", "lon"),
        P(None, "lat", "lon", None),
        P(None, "lat", "lon", None),
        P("lat", "lon", None),
    )
    return jax.shard_map(
        body,
        mesh=mesh,
        in_specs=placed,
        out_specs=(P(None, None, "lat", "lon"), P("lat", "lon", None, None, None, None)),
        check_vma=False,
    )
```

```python
import functools

import jax
import jax.numpy as jnp
from jax import lax
from jax.experimental import pallas as pl
from jax.experimental.pallas import tpu as pltpu
from jax.sharding import PartitionSpec as P

PCAP = 2
SLOTS = 4
STEPS = 3
NS_ITERS = 6
MEM = 64
LEV = 4
ROWS = 8
COLS = 128
PATCH = 16
OBS = 128
N_LAT = 8
N_LON = 16
F32 = jnp.float32
BF16 = jnp.bfloat16
NEIGHBOURS = ((-1, 0), (1, 0), (0, -1), (0, 1), (-1, -1), (-1, 1), (1, -1), (1, 1))
S_, N_, W_, E_, SW_, SE_, NW_, NE_ = range(8)


MESH = pl.DeviceIdType.MESH


def tile_to_device(row, col):
    return row - row % 2 + col % 2, col - col % 2 + row % 2


def swap_partner(lat, lon):
    swapping = (lat % 2 + lon % 2) % 2 == 1
    return swapping, (lat + 1 - 2 * (lat % 2), lon + 1 - 2 * (lon % 2))


def lanes(shape):
    return lax.broadcasted_iota(jnp.int32, shape, len(shape) - 1)


CODE = 32767.0


def peaks_of(ref, chunk):
    def grow(m, peak):
        return jnp.maximum(peak, jnp.abs(ref[pl.ds(pl.multiple_of(m * 32, 32), 32), :]))
    start = chunk * 16
    return jnp.maximum(lax.fori_loop(start, start + 16, grow, jnp.zeros((32, COLS), F32), unroll=8), 1e-30)


def encode(ref, code_ref, peak_ref, chunk):
    peaks = peaks_of(ref, chunk)
    peak_ref[chunk] = peaks
    factor = CODE / peaks

    @pl.loop(chunk * 16, chunk * 16 + 16, unroll=4)
    def _(m):
        at = pl.ds(pl.multiple_of(m * 32, 32), 32)
        code_ref[at, :] = jnp.round(ref[at, :] * factor).astype(jnp.int32).astype(jnp.int16)


def decode(code_ref, peak_ref, ref, chunk):
    steps = peak_ref[chunk] * (1.0 / CODE)

    @pl.loop(chunk * 16, chunk * 16 + 16, unroll=4)
    def _(m):
        at = pl.ds(pl.multiple_of(m * 32, 32), 32)
        ref[at, :] = code_ref[at, :].astype(jnp.int32).astype(F32) * steps


def butterfly(parts):
    parts = list(parts)
    lane = lanes(parts[0].shape)
    for bit in (1, 2, 4, 8):
        keep = (lane & (8 * bit)) == 0
        for i in range(16):
            if i & bit:
                continue
            a, b = parts[i], parts[i + bit]
            parts[i] = jnp.where(keep, a, pltpu.roll(b, 8 * bit, 1))
            parts[i + bit] = jnp.where(keep, pltpu.roll(a, 128 - 8 * bit, 1), b)
    return parts


def split(x):
    hi = x.astype(BF16)
    return hi, (x - hi.astype(F32)).astype(BF16)


def dot(a, b):
    return jnp.dot(a, b, preferred_element_type=F32)


def dot_t(a, b):
    return lax.dot_general(a, b, (((1,), (1,)), ((), ())), preferred_element_type=F32)


def block_diagonal(x):
    block = lanes(x.shape) // 64
    return jnp.concatenate([jnp.where(block == i, x, jnp.zeros_like(x)) for i in range(4)], axis=0)


def times(x_parts, y_parts):
    yh, yl = y_parts
    n = sum(h.shape[0] for h, _ in x_parts)
    his = [h for h, _ in x_parts]
    los = [l for _, l in x_parts]
    top = dot(jnp.concatenate(his + los, axis=0), yh)
    low = dot(jnp.concatenate(his, axis=0), yl)
    total = top[:n] + top[n:] + low
    outs, at = [], 0
    for h, _ in x_parts:
        outs.append(total[at:at + h.shape[0]])
        at += h.shape[0]
    return outs


def cell_weights(counts_ref, errors_ref, slot):
    shape = (PATCH, OBS)
    patch = lax.broadcasted_iota(jnp.int32, shape, 0)
    count = jnp.zeros(shape, jnp.int32)
    for p in range(PATCH):
        count = jnp.where(patch == p, counts_ref[slot, 0, p], count)
    return jnp.where(lanes(shape) < count, 1.0 / errors_ref[slot, 0], 0.0)


def observe(states_ref, slot, cells, weights, values, xs, perts, innovs, last):
    @pl.loop(0, 8)
    def _(k):
        q, t = k // 4, k % 4
        halves = []
        for u in range(2):
            ms = pl.ds(pl.multiple_of(t * 16 + u * 8, 8), 8)
            parts = [states_ref[slot, i % 8, q * 2 + i // 8, ms, :] for i in range(16)]
            halves.append(butterfly(parts))
        cs = pl.ds(pl.multiple_of(q * 128, 128), 128)
        for p in range(PATCH):
            x = jnp.concatenate([halves[0][p], halves[1][p]], axis=0)
            hi, lo = split(x)
            xs[p, pl.ds(pl.multiple_of(t * 16, 16), 16), cs] = hi
            xs[p, pl.ds(pl.multiple_of(MEM + t * 16, 16), 16), cs] = lo
            if slot == SLOTS - 1:
                last[pl.ds(pl.multiple_of(p * MEM + t * 16, 16), 16), cs] = x

    cell_id = lax.broadcasted_iota(jnp.int32, (256, OBS), 0).astype(F32).astype(BF16)
    one, zero = jnp.ones((256, OBS), BF16), jnp.zeros((256, OBS), BF16)

    @pl.loop(0, PATCH, unroll=4)
    def _(p):
        w = zero
        for corner in range(4):
            idx = cells[slot, corner, 0, pl.ds(p, 1), :].astype(F32)
            idx = jnp.broadcast_to(idx, (256, OBS)).astype(BF16)
            w = w + jnp.where(cell_id == idx, one, zero)
        both = dot(xs[p], w)
        equivalent = 0.25 * (both[:MEM] + both[MEM:])
        mean = jnp.sum(equivalent, axis=0, keepdims=True) * (1.0 / MEM)
        weight = weights[slot, pl.ds(p, 1), :]
        pert = ((equivalent - mean) * weight).astype(BF16)
        perts[p // 4, pl.ds(pl.multiple_of((p % 4) * MEM, MEM), MEM), slot * OBS:(slot + 1) * OBS] = pert
        innovs[slot, pl.ds(p, 1), :] = (values[slot, 0, pl.ds(p, 1), :] - mean) * weight


def transforms_of(perts, innovs, tts):
    shape = (MEM, 256)
    block = lanes(shape) // 64
    eye = (lax.broadcasted_iota(jnp.int32, shape, 0) == (lanes(shape) & 63)).astype(F32)
    innov = jnp.concatenate([innovs[s] for s in range(SLOTS)], axis=1).astype(BF16)
    ys, zs, alongs, sizes = [], [], [], []
    for g in range(4):
        pg = perts[g]
        full = dot_t(pg, pg)
        gram = full[0:MEM]
        for i in range(1, 4):
            gram = jnp.where(block == i, full[i * MEM:(i + 1) * MEM], gram)
        al = dot_t(innov, pg)
        row = lax.broadcasted_iota(jnp.int32, al.shape, 0)
        al = jnp.sum(jnp.where(row == g * 4 + lanes(al.shape) // 64, al, 0.0), axis=0, keepdims=True)
        alongs.append(al)
        amat = gram + (MEM - 1.0) * eye
        sq = jnp.sum(amat * amat, axis=0, keepdims=True)
        blk1 = lanes((1, 256)) // 64
        size = jnp.zeros((1, 256), F32)
        for i in range(4):
            total = jnp.sum(jnp.where(blk1 == i, sq, 0.0), axis=1, keepdims=True)
            size = jnp.where(blk1 == i, total, size)
        size = jnp.sqrt(size)
        sizes.append(size)
        ys.append(amat / size)
        zs.append(None)
    for it in range(NS_ITERS):
        mixers = []
        for g in range(4):
            yh, yl = split(ys[g])
            if it == 0:
                zy = ys[g]
            else:
                (zy,) = times([split(zs[g])], (block_diagonal(yh), block_diagonal(yl)))
            mixers.append(1.5 * eye - 0.5 * zy)
        for g in range(4):
            mh, ml = split(mixers[g])
            md = (block_diagonal(mh), block_diagonal(ml))
            if it == 0:
                (ys[g],) = times([split(ys[g])], md)
                zs[g] = mixers[g]
            elif it < NS_ITERS - 1:
                ys[g], zs[g] = times([split(ys[g]), split(zs[g])], md)
            else:
                (zs[g],) = times([split(zs[g])], md)
    eye2 = (lax.broadcasted_iota(jnp.int32, (MEM, 128), 0) == (lanes((MEM, 128)) & 63)).astype(F32)
    size0 = jnp.sqrt(jnp.full((1, 128), MEM * (MEM - 1.0) * (MEM - 1.0), F32))
    y0 = (MEM - 1.0) / size0
    z0 = jnp.ones((1, 128), F32)
    for it in range(NS_ITERS):
        m0 = 1.5 - 0.5 * z0 * y0
        y0, z0 = y0 * m0, m0 * z0
    empty = eye2 * (z0 * jnp.sqrt((MEM - 1.0) / size0))

    tts[PATCH] = empty
    turned = []
    for g in range(4):
        zh, zl = split(zs[g])
        zd = (block_diagonal(zh), block_diagonal(zl))
        (first,) = times([split(jnp.broadcast_to(alongs[g], (16, 256)))], zd)
        (second,) = times([split(first)], zd)
        tt = zs[g] * jnp.sqrt((MEM - 1.0) / sizes[g]) + second[0:1] / sizes[g]
        turned.append(tt)
        both = jnp.transpose(jnp.concatenate([tt, tt], axis=0))
        for i in range(4):
            tts[g * 4 + i] = both[i * MEM:(i + 1) * MEM]
    return turned


def analyse_members(turned, last, result):
    for g in range(4):
        th, tl = split(turned[g])
        thd, tld = block_diagonal(th), block_diagonal(tl)
        devs, means = [], []
        for i in range(4):
            x = last[pl.ds((g * 4 + i) * MEM, MEM), :]
            mean = jnp.sum(x, axis=0, keepdims=True) * (1.0 / MEM)
            devs.append(x - mean)
            means.append(mean)
        dh, dl = split(jnp.concatenate(devs, axis=0))
        ana = dot(thd, dh) + dot(tld, dh) + dot(thd, dl)
        for i in range(4):
            result[pl.ds((g * 4 + i) * MEM, MEM), :] = ana[i * MEM:(i + 1) * MEM] + means[i]


def place_members(result, out_ref, chunk):
    @pl.loop(0, 4)
    def _(k):
        q, t = k // 2, chunk * 2 + k % 2
        cs = pl.ds(pl.multiple_of(q * 128, 128), 128)
        parts = [result[pl.ds(pl.multiple_of(p * MEM + t * 8, 8), 8), cs] for p in range(16)]
        for i, x in enumerate(butterfly(parts)):
            out_ref[pl.ds(t * 256 + q * 16 + i, 8, stride=32), :] = x


def cycle_kernel(ens_ref, cu_ref, cv_ref, dd_ref, cells_ref, counts_ref, values_ref, errors_ref, owners_ref,
                 ana_out, held_out, owners_out,
                 perts, innovs, last, owners,
                 out_ref, cells, weights, values, weight_send, xs,
                 tiles, coef_got, coefs, row_send, ring_send, edge_send,
                 row_got, edge_got, corner_got,
                 load_sem, swap_sem, code_send, code_got, peak_send, peak_got, code_sem, csend_sem, crecv_sem,
                 hsend_sem, hrecv_sem,
                 result, tts, back_send, back_got, back_peak, back_peak_got, back_sem,
                 held_send, held_got, held_peak, held_peak_got, tsend_sem, trecv_sem, rings, field, shifts):
    lat, lon = lax.axis_index("lat"), lax.axis_index("lon")
    trow, tcol = tile_to_device(lat, lon)

    def device_at(step):
        row = lax.rem(trow + step[0] + N_LAT, N_LAT)
        col = lax.rem(tcol + step[1] + N_LON, N_LON)
        return tile_to_device(row, col)

    barrier = pltpu.get_barrier_semaphore()
    for step in NEIGHBOURS:
        pl.semaphore_signal(barrier, inc=1, device_id=device_at(step),
                            device_id_type=MESH)
    swapping, partner = swap_partner(lat, lon)
    for k in range(1, N_LON):
        pl.semaphore_signal(barrier, inc=1, device_id=tile_to_device(lat, lax.rem(tcol + k, N_LON)), device_id_type=MESH)

    @pl.when(swapping)
    def _():
        pl.semaphore_signal(barrier, inc=1, device_id=tile_to_device(lat, tcol), device_id_type=MESH)

    moves = [(ref, coef_got.at[8, i]) for i, ref in enumerate((cu_ref, cv_ref, dd_ref))]
    moves += [(cells_ref, cells), (weight_send, weights), (values_ref, values), (owners_ref, owners_out)]
    for slot in range(SLOTS):
        weight_send[slot] = cell_weights(counts_ref, errors_ref, slot)
    load = pltpu.make_async_copy(ens_ref, tiles, load_sem.at[8])
    load.start()
    rows = MEM * LEV * ROWS // 4
    sent = [
        pltpu.make_async_remote_copy(src_ref=src, dst_ref=dst, send_sem=code_sem.at[0, i], recv_sem=code_sem.at[1, i],
                                     device_id=partner, device_id_type=MESH)
        for i, (src, dst) in enumerate(
            [(code_send.at[pl.ds(c * rows, rows)], code_got.at[pl.ds(c * rows, rows)]) for c in range(4)]
            + [(peak_send.at[c], peak_got.at[c]) for c in range(4)])]
    kept = [pltpu.make_async_copy(src, dst, load_sem.at[i]) for i, (src, dst) in enumerate(moves)]
    swapped = [
        pltpu.make_async_remote_copy(src_ref=src, dst_ref=dst, send_sem=load_sem.at[i], recv_sem=swap_sem.at[i],
                                     device_id=partner, device_id_type=MESH)
        for i, (src, dst) in enumerate(moves)]

    def arrive(first, last):
        @pl.when(swapping)
        def _():
            for copy in swapped[first:last]:
                copy.wait()

        @pl.when(jnp.logical_not(swapping))
        def _():
            for copy in kept[first:last]:
                copy.wait()

    pl.semaphore_wait(barrier, jnp.where(swapping, 8 + N_LON, 7 + N_LON))

    @pl.when(swapping)
    def _():
        for copy in swapped[:3]:
            copy.start()
        load.wait()
        for c in range(4):
            encode(tiles, code_send, peak_send, c)
            sent[c].start()
            sent[4 + c].start()
        for copy in swapped[3:]:
            copy.start()

    @pl.when(jnp.logical_not(swapping))
    def _():
        for copy in kept:
            copy.start()
        load.wait()

    arrive(0, 3)
    opposite = (N_, S_, E_, W_, NE_, NW_, SE_, SW_)
    ccopies = []
    for d, step in enumerate(NEIGHBOURS):
        copy = pltpu.make_async_remote_copy(
            src_ref=coef_got.at[8], dst_ref=coef_got.at[opposite[d]],
            send_sem=csend_sem.at[d], recv_sem=crecv_sem.at[opposite[d]],
            device_id=device_at(step), device_id_type=MESH)
        copy.start()
        ccopies.append(copy)

    lane16 = lanes((16, COLS))
    lane1 = lanes((8, COLS))

    def pack(src, s, ms):
        rings = []
        for half in range(2):
            ring = out_ref[src, half * 4, 0, ms, :]
            for k in range(1, 16):
                turned = pltpu.roll(out_ref[src, half * 4 + k // LEV, k % LEV, ms, :], k * 8, 1)
                inside = ((lane16 + (4 - k * 8 + 128)) & 127) < 8
                ring = jnp.where(inside, turned, ring)
            ring_send[s, half, ms, :] = ring.astype(BF16)
            rings.append(ring)
        edge_send[s, 0, ms, :] = jnp.where((lane16 & 7) < 4, rings[0], pltpu.roll(rings[1], 4, 1)).astype(BF16)
        edge_send[s, 1, ms, :] = jnp.where((lane16 & 7) >= 4, rings[0], pltpu.roll(rings[1], 124, 1)).astype(BF16)
        for side, first in ((0, 0), (1, ROWS - 3)):
            for r in range(3):
                for l in range(LEV):
                    row_send[s, side, r, l, ms, :] = out_ref[src, first + r, l, ms, :].astype(BF16)

    def start_copies(plan):
        copies = []
        for d, src_ref, dst_ref, landed, group in plan:
            copy = pltpu.make_async_remote_copy(
                src_ref=src_ref, dst_ref=dst_ref,
                send_sem=hsend_sem.at[group, d], recv_sem=hrecv_sem.at[group, landed],
                device_id=device_at(NEIGHBOURS[d]), device_id_type=MESH)
            copy.start()
            copies.append(copy)
        return copies

    def send_edges(s):
        low, high = ring_send.at[s, 0], ring_send.at[s, 1]
        return start_copies((
            (W_, edge_send.at[s, 0], edge_got.at[s, 1], E_, s),
            (E_, edge_send.at[s, 1], edge_got.at[s, 0], W_, s),
            (SW_, low, corner_got.at[s, 3], NE_, s),
            (SE_, low, corner_got.at[s, 2], NW_, s),
            (NW_, high, corner_got.at[s, 1], SE_, s),
            (NE_, high, corner_got.at[s, 0], SW_, s),
        ))

    def send_halos(src, s):
        @pl.loop(0, MEM // 16)
        def _(t):
            pack(src, s, pl.ds(pl.multiple_of(t * 16, 16), 16))

        return start_copies((
            (S_, row_send.at[s, 0], row_got.at[s, 1], N_, s),
            (N_, row_send.at[s, 1], row_got.at[s, 0], S_, s),
        )) + send_edges(s)

    copies = []
    for c in range(4):
        @pl.when(swapping)
        def _():
            sent[c].wait()
            sent[4 + c].wait()
            decode(code_got, peak_got, tiles, c)

        for r in range(ROWS):
            for l in range(LEV):
                for t in (2 * c, 2 * c + 1):
                    out_ref[0, r, l, pl.ds(t * 8, 8), :] = tiles[pl.ds(t * 256 + l * ROWS + r, 8, stride=32), :]
        ms = pl.ds(c * 16, 16)
        pack(0, 0, ms)
        copies += start_copies((
            (S_, row_send.at[0, 0, :, :, ms], row_got.at[0, 1, :, :, ms], N_, SLOTS + c),
            (N_, row_send.at[0, 1, :, :, ms], row_got.at[0, 0, :, :, ms], S_, SLOTS + c),
        ))
    copies += send_edges(0)
    for copy in ccopies:
        copy.wait()
    south_ok = jnp.where(trow > 0, 1.0, 0.0).astype(F32)
    north_ok = jnp.where(trow < N_LAT - 1, 1.0, 0.0).astype(F32)
    lane8 = lanes((ROWS, COLS))
    for block, (cen, west, east, ok) in enumerate(((S_, SW_, SE_, south_ok), (8, W_, E_, None), (N_, NW_, NE_, north_ok))):
        for half in range(2):
            for l in range(LEV):
                def pick(i):
                    if half == 0:
                        return jnp.where(lane8 < 96, coef_got[cen, i, l], coef_got[west, i, l])
                    return jnp.where(lane8 >= 32, coef_got[cen, i, l], coef_got[east, i, l])
                cu, cv, dd = pick(0), pick(1), pick(2)
                aw = jnp.maximum(cu, 0.0) + dd
                ae = dd - jnp.minimum(cu, 0.0)
                as_ = jnp.maximum(cv, 0.0) + dd
                an = dd - jnp.minimum(cv, 0.0)
                ac = 1.0 - (jnp.abs(cu) + jnp.abs(cv) + 4.0 * dd)
                for j, a in enumerate((ac, aw, ae, as_, an)):
                    a = a if ok is None else a * ok
                    for r in ((6, 7), range(8), (0, 1))[block]:
                        coefs[half, l, j, block * 8 + r - 6] = jnp.broadcast_to(a[r:r + 1], (8, COLS))

    from_at = lax.broadcasted_iota(jnp.int32, (256, 256), 0) & 127
    to_at = lanes((256, 256))
    step_at = jnp.where(to_at < 128, 1, 127)
    shifts[...] = jnp.where(((from_at + step_at) & 127) == (to_at & 127), 1.0, 0.0).astype(BF16)

    for s in range(SLOTS):
        for copy in copies:
            copy.wait()
        prev = max(s - 1, 0)

        for t in range(MEM // 16):
            ms = pl.ds(t * 16, 16)
            west, east = edge_got[s, 0, ms, :].astype(F32), edge_got[s, 1, ms, :].astype(F32)
            first = (lane16 & 7) < 4
            rings[0, ms, :] = jnp.where(first, corner_got[s, 1, ms, :].astype(F32), corner_got[s, 0, ms, :].astype(F32)) * south_ok
            rings[1, ms, :] = jnp.where(first, east, west)
            rings[2, ms, :] = jnp.where(first, pltpu.roll(east, 124, 1), pltpu.roll(west, 4, 1))
            rings[3, ms, :] = jnp.where(first, corner_got[s, 3, ms, :].astype(F32), corner_got[s, 2, ms, :].astype(F32)) * north_ok

        for l in range(LEV):
            @pl.loop(0, MEM // 16)
            def _(t):
                ms = pl.ds(pl.multiple_of(t * 16, 16), 16)
                for r in range(-3, ROWS + 3):
                    if 0 <= r < ROWS:
                        mine = out_ref[prev, r, l, ms, :]
                    elif r < 0:
                        mine = row_got[s, 0, r + 3, l, ms, :].astype(F32) * south_ok
                    else:
                        mine = row_got[s, 1, r - ROWS, l, ms, :].astype(F32) * north_ok
                    turn = (((r + 4) % 4) * LEV + l) * 8
                    aux = rings[(r + 4) // 4, ms, :]
                    aux = pltpu.roll(aux, 128 - turn, 1) if turn else aux
                    field[0, l, 0, r + 3, ms, :] = jnp.where(lane16 < 96, mine, aux)
                    field[0, l, 1, r + 3, ms, :] = jnp.where(lane16 >= 32, mine, aux)

        for step in range(STEPS):
            src, dst = step % 2, (step + 1) % 2

            @pl.loop(0, LEV)
            def _(l):
                inner = range(1 + step, ROWS + 5 - step)
                pieces = [jnp.concatenate(split(field[src, l, half, r, pl.ds(0, MEM // 2), :]), axis=1)
                          for r in inner for half in range(2)]
                moved = dot(jnp.concatenate(pieces, axis=0), shifts[...])
                for r in inner:
                    factors = [[coefs[half, l, j, r - 1] for j in range(5)] for half in range(2)]
                    for t in range(MEM // 8):
                        ms = pl.ds(t * 8, 8)
                        new = []
                        for half in range(2):
                            ac, aw, ae, as_, an = factors[half]
                            v = field[src, l, half, r, ms, :]
                            if t < MEM // 16:
                                at = ((r - inner[0]) * 2 + half) * (MEM // 2) + t * 8
                                west, east = moved[at:at + 8, :COLS], moved[at:at + 8, COLS:]
                            else:
                                west, east = pltpu.roll(v, 1, 1), pltpu.roll(v, COLS - 1, 1)
                            new.append((ac * v + as_ * field[src, l, half, r - 1, ms, :])
                                       + an * field[src, l, half, r + 1, ms, :]
                                       + (aw * west + ae * east))
                        if step < STEPS - 1:
                            field[dst, l, 0, r, ms, :] = new[0]
                            field[dst, l, 1, r, ms, :] = new[1]
                        else:
                            out_ref[s, r - 3, l, ms, :] = jnp.where(lane1 < 64, new[0], new[1])

        if s < SLOTS - 1:
            copies = send_halos(s, s + 1)
        if s == 0:
            arrive(3, 7)
            listed = pltpu.make_async_copy(owners_out, owners, load_sem.at[7])
            listed.start()
            listed.wait()
        observe(out_ref, s, cells, weights, values, xs, perts, innovs, last)


    turned = transforms_of(perts, innovs, tts)

    ids = [owners[0, 0, p] for p in range(PATCH)]
    left = lanes((MEM, COLS)) < MEM
    for o in range(N_LON):
        first, second = jnp.int32(PATCH), jnp.int32(PATCH)
        for p in range(PATCH):
            named = ids[p] == o
            second = jnp.where(jnp.logical_and(named, first < PATCH), p, second)
            first = jnp.where(jnp.logical_and(named, first == PATCH), p, first)
        pair = jnp.where(left, tts[first], tts[second])
        peak = jnp.maximum(jnp.max(jnp.abs(pair), axis=0, keepdims=True), 1e-30)
        held_peak[o] = peak
        held_send[o] = jnp.round(pair * (CODE / peak)).astype(jnp.int32).astype(jnp.int16)

    def parcel(k, half):
        owner = lax.rem(lon + k, N_LON)
        src, dst = ((held_send, held_got), (held_peak, held_peak_got))[half]
        return pltpu.make_async_remote_copy(
            src_ref=src.at[owner], dst_ref=dst.at[tcol], send_sem=tsend_sem.at[half, k],
            recv_sem=trecv_sem.at[half, tcol], device_id=(trow, owner), device_id_type=MESH)

    def landed(k, half):
        source = lax.rem(tcol + k, N_LON)
        src, dst = ((held_send, held_got), (held_peak, held_peak_got))[half]
        pltpu.make_async_remote_copy(
            src_ref=src.at[0], dst_ref=dst.at[source], send_sem=tsend_sem.at[half, k],
            recv_sem=trecv_sem.at[half, source], device_id=(trow, lon), device_id_type=MESH).wait_recv()

    keeps = [pltpu.make_async_copy(src.at[lon], dst.at[tcol], tsend_sem.at[i, 0])
             for i, (src, dst) in enumerate(((held_send, held_got), (held_peak, held_peak_got)))]

    @pl.when(swapping)
    def _():
        for half in range(2):
            parcel(0, half).start()

    @pl.when(jnp.logical_not(swapping))
    def _():
        for copy in keeps:
            copy.start()

    for k in range(1, N_LON):
        for half in range(2):
            parcel(k, half).start()

    analyse_members(turned, last, result)
    backs = [
        pltpu.make_async_remote_copy(src_ref=src, dst_ref=dst, send_sem=back_sem.at[0, i], recv_sem=back_sem.at[1, i],
                                     device_id=partner, device_id_type=MESH)
        for i, (src, dst) in enumerate(
            [(back_send.at[pl.ds(c * rows, rows)], back_got.at[pl.ds(c * rows, rows)]) for c in range(4)]
            + [(back_peak.at[c], back_peak_got.at[c]) for c in range(4)])]
    for c in range(4):
        place_members(result, ana_out, c)

        @pl.when(swapping)
        def _():
            encode(ana_out, back_send, back_peak, c)
            backs[c].start()
            backs[4 + c].start()

    @pl.when(swapping)
    def _():
        for half in range(2):
            parcel(0, half).wait_send()
            landed(0, half)

    @pl.when(jnp.logical_not(swapping))
    def _():
        for copy in keeps:
            copy.wait()

    for k in range(1, N_LON):
        for half in range(2):
            parcel(k, half).wait_send()
            landed(k, half)

    @pl.loop(0, N_LON, unroll=2)
    def _(o):
        pair = held_got[o].astype(jnp.int32).astype(F32) * (held_peak_got[o] * (1.0 / CODE))
        held_out[2 * o] = pair[:, :MEM]
        held_out[2 * o + 1] = pltpu.roll(pair, MEM, 1)[:, :MEM]

    @pl.when(swapping)
    def _():
        for c in range(4):
            backs[c].wait()
            backs[4 + c].wait()
            decode(back_got, back_peak_got, ana_out, c)


VMEM_SPEC = pl.BlockSpec(memory_space=pltpu.VMEM)
SMEM_SPEC = pl.BlockSpec(memory_space=pltpu.SMEM)
ANY_SPEC = pl.BlockSpec(memory_space=pl.ANY)


def cycle(ensemble, cu, cv, dd, cells, counts, values, errors, owners):
    return pl.pallas_call(
        cycle_kernel,
        out_shape=(jax.ShapeDtypeStruct((MEM * LEV * ROWS, COLS), F32),
                   jax.ShapeDtypeStruct((N_LON * PCAP, MEM, MEM), F32),
                   jax.ShapeDtypeStruct(owners.shape, jnp.int32)),
        in_specs=[ANY_SPEC] * 5 + [SMEM_SPEC, ANY_SPEC, VMEM_SPEC, ANY_SPEC],
        out_specs=(VMEM_SPEC, VMEM_SPEC, ANY_SPEC),
        scratch_shapes=[
            pltpu.VMEM((4, 256, SLOTS * OBS), BF16),
            pltpu.VMEM((SLOTS, PATCH, OBS), F32),
            pltpu.VMEM((PATCH * MEM, 256), F32),
            pltpu.SMEM((1, 1, PATCH), jnp.int32),
            pltpu.VMEM((SLOTS, ROWS, LEV, MEM, COLS), F32),
            pltpu.VMEM((SLOTS, 4, 1, PATCH, OBS), jnp.int32),
            pltpu.VMEM((SLOTS, PATCH, OBS), F32),
            pltpu.VMEM((SLOTS, 1, PATCH, OBS), F32),
            pltpu.VMEM((SLOTS, PATCH, OBS), F32),
            pltpu.VMEM((PATCH, 2 * MEM, 256), BF16),
            pltpu.VMEM((MEM * LEV * ROWS, COLS), F32),
            pltpu.VMEM((9, 3, LEV, ROWS, COLS), F32),
            pltpu.VMEM((2, LEV, 5, 12, 8, COLS), F32),
            pltpu.VMEM((SLOTS, 2, 3, LEV, MEM, COLS), BF16),
            pltpu.VMEM((SLOTS, 2, MEM, COLS), BF16),
            pltpu.VMEM((SLOTS, 2, MEM, COLS), BF16),
            pltpu.VMEM((SLOTS, 2, 3, LEV, MEM, COLS), BF16),
            pltpu.VMEM((SLOTS, 2, MEM, COLS), BF16),
            pltpu.VMEM((SLOTS, 4, MEM, COLS), BF16),
            pltpu.SemaphoreType.DMA((9,)),
            pltpu.SemaphoreType.DMA((9,)),
            pltpu.VMEM((MEM * LEV * ROWS, COLS), jnp.int16),
            pltpu.VMEM((MEM * LEV * ROWS, COLS), jnp.int16),
            pltpu.VMEM((4, LEV * ROWS, COLS), F32),
            pltpu.VMEM((4, LEV * ROWS, COLS), F32),
            pltpu.SemaphoreType.DMA((2, 8)),
            pltpu.SemaphoreType.DMA((8,)),
            pltpu.SemaphoreType.DMA((8,)),
            pltpu.SemaphoreType.DMA((2 * SLOTS, 8)),
            pltpu.SemaphoreType.DMA((2 * SLOTS, 8)),
            pltpu.VMEM((PATCH * MEM, 256), F32),
            pltpu.VMEM((PATCH + 1, MEM, COLS), F32),
            pltpu.VMEM((MEM * LEV * ROWS, COLS), jnp.int16),
            pltpu.VMEM((MEM * LEV * ROWS, COLS), jnp.int16),
            pltpu.VMEM((4, LEV * ROWS, COLS), F32),
            pltpu.VMEM((4, LEV * ROWS, COLS), F32),
            pltpu.SemaphoreType.DMA((2, 8)),
            pltpu.VMEM((N_LON, MEM, COLS), jnp.int16),
            pltpu.VMEM((N_LON, MEM, COLS), jnp.int16),
            pltpu.VMEM((N_LON, 1, COLS), F32),
            pltpu.VMEM((N_LON, 1, COLS), F32),
            pltpu.SemaphoreType.DMA((2, N_LON)),
            pltpu.SemaphoreType.DMA((2, N_LON)),
            pltpu.VMEM((4, MEM, COLS), F32),
            pltpu.VMEM((2, LEV, 2, ROWS + 6, MEM, COLS), F32),
            pltpu.VMEM((256, 256), BF16),
        ],
        compiler_params=pltpu.CompilerParams(
            collective_id=0, has_side_effects=True, vmem_limit_bytes=60 * 1024 * 1024),
        name="cycle",
    )(ensemble.reshape(MEM * LEV * ROWS, COLS), cu, cv, dd, cells, counts, values, errors, owners)


def body(ensemble, courant_lon, courant_lat, diffusion, obs_cells, obs_counts, obs_values, obs_errors, owners):
    analysis, held, _ = cycle(ensemble, courant_lon, courant_lat, diffusion,
                              obs_cells, obs_counts, obs_values, obs_errors, owners.transpose(0, 2, 1))
    return analysis.reshape(MEM, LEV, ROWS, COLS), held.reshape(1, 1, N_LON, PCAP, MEM, MEM)


def solution(mesh):
    placed = (
        P(None, None, "lat", "lon"),
        P(None, "lat", "lon"),
        P(None, "lat", "lon"),
        P(None, "lat", "lon"),
        P(None, None, "lat", "lon", None),
        P(None, "lat", "lon"),
        P(None, "lat", "lon", None),
        P(None, "lat", "lon", None),
        P("lat", "lon", None),
    )
    return jax.shard_map(
        body,
        mesh=mesh,
        in_specs=placed,
        out_specs=(P(None, None, "lat", "lon"), P("lat", "lon", None, None, None, None)),
        check_vma=False,
    )
```

```python
import functools

import jax
import jax.numpy as jnp
from jax import lax
from jax.experimental import pallas as pl
from jax.experimental.pallas import tpu as pltpu
from jax.sharding import PartitionSpec as P

PCAP = 2
SLOTS = 4
STEPS = 3
NS_ITERS = 6
BAND = 12
MEM = 64
LEV = 4
ROWS = 8
COLS = 128
PATCH = 16
OBS = 128
N_LAT = 8
N_LON = 16
F32 = jnp.float32
BF16 = jnp.bfloat16
NEIGHBOURS = ((-1, 0), (1, 0), (0, -1), (0, 1), (-1, -1), (-1, 1), (1, -1), (1, 1))
S_, N_, W_, E_, SW_, SE_, NW_, NE_ = range(8)


MESH = pl.DeviceIdType.MESH


def tile_to_device(row, col):
    return row - row % 2 + col % 2, col - col % 2 + row % 2


def swap_partner(lat, lon):
    swapping = (lat % 2 + lon % 2) % 2 == 1
    return swapping, (lat + 1 - 2 * (lat % 2), lon + 1 - 2 * (lon % 2))


def lanes(shape):
    return lax.broadcasted_iota(jnp.int32, shape, len(shape) - 1)


CODE = 32767.0


def peaks_of(ref, chunk):
    def grow(m, peak):
        return jnp.maximum(peak, jnp.abs(ref[pl.ds(pl.multiple_of(m * 32, 32), 32), :]))
    start = chunk * 16
    return jnp.maximum(lax.fori_loop(start, start + 16, grow, jnp.zeros((32, COLS), F32), unroll=8), 1e-30)


def encode(ref, code_ref, peak_ref, chunk):
    peaks = peaks_of(ref, chunk)
    peak_ref[chunk] = peaks
    factor = CODE / peaks

    @pl.loop(chunk * 16, chunk * 16 + 16, unroll=4)
    def _(m):
        at = pl.ds(pl.multiple_of(m * 32, 32), 32)
        code_ref[at, :] = jnp.round(ref[at, :] * factor).astype(jnp.int32).astype(jnp.int16)


def decode(code_ref, peak_ref, ref, chunk):
    steps = peak_ref[chunk] * (1.0 / CODE)

    @pl.loop(chunk * 16, chunk * 16 + 16, unroll=4)
    def _(m):
        at = pl.ds(pl.multiple_of(m * 32, 32), 32)
        ref[at, :] = code_ref[at, :].astype(jnp.int32).astype(F32) * steps


def butterfly(parts):
    parts = list(parts)
    lane = lanes(parts[0].shape)
    for bit in (1, 2, 4, 8):
        keep = (lane & (8 * bit)) == 0
        for i in range(16):
            if i & bit:
                continue
            a, b = parts[i], parts[i + bit]
            parts[i] = jnp.where(keep, a, pltpu.roll(b, 8 * bit, 1))
            parts[i + bit] = jnp.where(keep, pltpu.roll(a, 128 - 8 * bit, 1), b)
    return parts


def split(x):
    hi = x.astype(BF16)
    return hi, (x - hi.astype(F32)).astype(BF16)


def dot(a, b):
    return jnp.dot(a, b, preferred_element_type=F32)


def dot_t(a, b):
    return lax.dot_general(a, b, (((1,), (1,)), ((), ())), preferred_element_type=F32)


def block_diagonal(x):
    block = lanes(x.shape) // 64
    return jnp.concatenate([jnp.where(block == i, x, jnp.zeros_like(x)) for i in range(4)], axis=0)


def times(x_parts, y_parts):
    yh, yl = y_parts
    n = sum(h.shape[0] for h, _ in x_parts)
    his = [h for h, _ in x_parts]
    los = [l for _, l in x_parts]
    top = dot(jnp.concatenate(his + los, axis=0), yh)
    low = dot(jnp.concatenate(his, axis=0), yl)
    total = top[:n] + top[n:] + low
    outs, at = [], 0
    for h, _ in x_parts:
        outs.append(total[at:at + h.shape[0]])
        at += h.shape[0]
    return outs


def cell_weights(counts_ref, errors_ref, slot):
    shape = (PATCH, OBS)
    patch = lax.broadcasted_iota(jnp.int32, shape, 0)
    count = jnp.zeros(shape, jnp.int32)
    for p in range(PATCH):
        count = jnp.where(patch == p, counts_ref[slot, 0, p], count)
    return jnp.where(lanes(shape) < count, 1.0 / errors_ref[slot, 0], 0.0)


def observe(states_ref, slot, cells, weights, values, xs, perts, innovs, last):
    @pl.loop(0, 8)
    def _(k):
        q, t = k // 4, k % 4
        halves = []
        for u in range(2):
            ms = pl.ds(pl.multiple_of(t * 16 + u * 8, 8), 8)
            parts = [states_ref[slot, i % 8, q * 2 + i // 8, ms, :] for i in range(16)]
            halves.append(butterfly(parts))
        cs = pl.ds(pl.multiple_of(q * 128, 128), 128)
        for p in range(PATCH):
            x = jnp.concatenate([halves[0][p], halves[1][p]], axis=0)
            hi, lo = split(x)
            xs[p, pl.ds(pl.multiple_of(t * 16, 16), 16), cs] = hi
            xs[p, pl.ds(pl.multiple_of(MEM + t * 16, 16), 16), cs] = lo
            if slot == SLOTS - 1:
                last[pl.ds(pl.multiple_of(p * MEM + t * 16, 16), 16), cs] = x

    cell_id = lax.broadcasted_iota(jnp.int32, (256, OBS), 0).astype(F32).astype(BF16)
    one, zero = jnp.full((256, OBS), 0.25, BF16), jnp.zeros((256, OBS), BF16)

    @pl.loop(0, PATCH, unroll=8)
    def _(p):
        w = None
        for corner in range(4):
            idx = cells[slot, corner, 0, pl.ds(p, 1), :].astype(F32)
            idx = jnp.broadcast_to(idx, (256, OBS)).astype(BF16)
            hit = jnp.where(cell_id == idx, one, zero)
            w = hit if w is None else w + hit
        both = dot(xs[p], w)
        equivalent = both[:MEM] + both[MEM:]
        mean = jnp.sum(equivalent, axis=0, keepdims=True) * (1.0 / MEM)
        weight = weights[slot, pl.ds(p, 1), :]
        pert = ((equivalent - mean) * weight).astype(BF16)
        perts[p // 4, pl.ds(pl.multiple_of((p % 4) * MEM, MEM), MEM), slot * OBS:(slot + 1) * OBS] = pert
        innovs[slot, pl.ds(p, 1), :] = (values[slot, 0, pl.ds(p, 1), :] - mean) * weight


def transforms_of(perts, innovs, tts):
    shape = (MEM, 256)
    block = lanes(shape) // 64
    eye = (lax.broadcasted_iota(jnp.int32, shape, 0) == (lanes(shape) & 63)).astype(F32)
    innov = jnp.concatenate([innovs[s] for s in range(SLOTS)], axis=1).astype(BF16)
    ys, zs, alongs, sizes = [], [], [], []
    for g in range(4):
        pg = perts[g]
        full = dot_t(pg, pg)
        gram = full[0:MEM]
        for i in range(1, 4):
            gram = jnp.where(block == i, full[i * MEM:(i + 1) * MEM], gram)
        al = dot_t(innov, pg)
        row = lax.broadcasted_iota(jnp.int32, al.shape, 0)
        al = jnp.sum(jnp.where(row == g * 4 + lanes(al.shape) // 64, al, 0.0), axis=0, keepdims=True)
        alongs.append(al)
        amat = gram + (MEM - 1.0) * eye
        sq = jnp.sum(amat * amat, axis=0, keepdims=True)
        blk1 = lanes((1, 256)) // 64
        size = jnp.zeros((1, 256), F32)
        for i in range(4):
            total = jnp.sum(jnp.where(blk1 == i, sq, 0.0), axis=1, keepdims=True)
            size = jnp.where(blk1 == i, total, size)
        size = jnp.sqrt(size)
        sizes.append(size)
        ys.append(amat / size)
        zs.append(None)
    for it in range(NS_ITERS):
        mixers = []
        for g in range(4):
            yh, yl = split(ys[g])
            if it == 0:
                zy = ys[g]
            else:
                (zy,) = times([split(zs[g])], (block_diagonal(yh), block_diagonal(yl)))
            mixers.append(1.5 * eye - 0.5 * zy)
        for g in range(4):
            mh, ml = split(mixers[g])
            md = (block_diagonal(mh), block_diagonal(ml))
            if it == 0:
                (ys[g],) = times([split(ys[g])], md)
                zs[g] = mixers[g]
            elif it < NS_ITERS - 1:
                ys[g], zs[g] = times([split(ys[g]), split(zs[g])], md)
            else:
                (zs[g],) = times([split(zs[g])], md)
    eye2 = (lax.broadcasted_iota(jnp.int32, (MEM, 128), 0) == (lanes((MEM, 128)) & 63)).astype(F32)
    size0 = jnp.sqrt(jnp.full((1, 128), MEM * (MEM - 1.0) * (MEM - 1.0), F32))
    y0 = (MEM - 1.0) / size0
    z0 = jnp.ones((1, 128), F32)
    for it in range(NS_ITERS):
        m0 = 1.5 - 0.5 * z0 * y0
        y0, z0 = y0 * m0, m0 * z0
    empty = eye2 * (z0 * jnp.sqrt((MEM - 1.0) / size0))

    tts[PATCH] = empty
    turned = []
    for g in range(4):
        zh, zl = split(zs[g])
        zd = (block_diagonal(zh), block_diagonal(zl))
        (first,) = times([split(jnp.broadcast_to(alongs[g], (16, 256)))], zd)
        (second,) = times([split(first)], zd)
        tt = zs[g] * jnp.sqrt((MEM - 1.0) / sizes[g]) + second[0:1] / sizes[g]
        turned.append(tt)
        both = jnp.transpose(jnp.concatenate([tt, tt], axis=0))
        for i in range(4):
            tts[g * 4 + i] = both[i * MEM:(i + 1) * MEM]
    return turned


def analyse_members(turned, last, result):
    for g in range(4):
        th, tl = split(turned[g])
        thd, tld = block_diagonal(th), block_diagonal(tl)
        devs, means = [], []
        for i in range(4):
            x = last[pl.ds((g * 4 + i) * MEM, MEM), :]
            mean = jnp.sum(x, axis=0, keepdims=True) * (1.0 / MEM)
            devs.append(x - mean)
            means.append(mean)
        dh, dl = split(jnp.concatenate(devs, axis=0))
        ana = dot(thd, dh) + dot(tld, dh) + dot(thd, dl)
        for i in range(4):
            result[pl.ds((g * 4 + i) * MEM, MEM), :] = ana[i * MEM:(i + 1) * MEM] + means[i]


def place_members(result, out_ref, chunk):
    @pl.loop(0, 4)
    def _(k):
        q, t = k // 2, chunk * 2 + k % 2
        cs = pl.ds(pl.multiple_of(q * 128, 128), 128)
        parts = [result[pl.ds(pl.multiple_of(p * MEM + t * 8, 8), 8), cs] for p in range(16)]
        for i, x in enumerate(butterfly(parts)):
            out_ref[pl.ds(t * 256 + q * 16 + i, 8, stride=32), :] = x


def cycle_kernel(ens_ref, cu_ref, cv_ref, dd_ref, cells_ref, counts_ref, values_ref, errors_ref, owners_ref,
                 ana_out, held_out, owners_out,
                 perts, innovs, last, owners,
                 out_ref, cells, weights, values, weight_send, xs,
                 tiles, coef_got, coefs, row_send, ring_send, edge_send,
                 row_got, edge_got, corner_got,
                 load_sem, swap_sem, code_send, code_got, peak_send, peak_got, code_sem, csend_sem, crecv_sem,
                 hsend_sem, hrecv_sem,
                 result, tts, back_send, back_got, back_peak, back_peak_got, back_sem,
                 held_send, held_got, held_peak, held_peak_got, tsend_sem, trecv_sem, rings, field, shifts):
    lat, lon = lax.axis_index("lat"), lax.axis_index("lon")
    trow, tcol = tile_to_device(lat, lon)

    def device_at(step):
        row = lax.rem(trow + step[0] + N_LAT, N_LAT)
        col = lax.rem(tcol + step[1] + N_LON, N_LON)
        return tile_to_device(row, col)

    barrier = pltpu.get_barrier_semaphore()
    for step in NEIGHBOURS:
        pl.semaphore_signal(barrier, inc=1, device_id=device_at(step),
                            device_id_type=MESH)
    swapping, partner = swap_partner(lat, lon)
    for k in range(1, N_LON):
        pl.semaphore_signal(barrier, inc=1, device_id=tile_to_device(lat, lax.rem(tcol + k, N_LON)), device_id_type=MESH)

    @pl.when(swapping)
    def _():
        pl.semaphore_signal(barrier, inc=1, device_id=tile_to_device(lat, tcol), device_id_type=MESH)

    moves = [(ref, coef_got.at[8, i]) for i, ref in enumerate((cu_ref, cv_ref, dd_ref))]
    moves += [(cells_ref, cells), (weight_send, weights), (values_ref, values), (owners_ref, owners_out)]
    for slot in range(SLOTS):
        weight_send[slot] = cell_weights(counts_ref, errors_ref, slot)
    load = pltpu.make_async_copy(ens_ref, tiles, load_sem.at[8])
    load.start()
    rows = MEM * LEV * ROWS // 4
    sent = [
        pltpu.make_async_remote_copy(src_ref=src, dst_ref=dst, send_sem=code_sem.at[0, i], recv_sem=code_sem.at[1, i],
                                     device_id=partner, device_id_type=MESH)
        for i, (src, dst) in enumerate(
            [(code_send.at[pl.ds(c * rows, rows)], code_got.at[pl.ds(c * rows, rows)]) for c in range(4)]
            + [(peak_send.at[c], peak_got.at[c]) for c in range(4)])]
    kept = [pltpu.make_async_copy(src, dst, load_sem.at[i]) for i, (src, dst) in enumerate(moves)]
    swapped = [
        pltpu.make_async_remote_copy(src_ref=src, dst_ref=dst, send_sem=load_sem.at[i], recv_sem=swap_sem.at[i],
                                     device_id=partner, device_id_type=MESH)
        for i, (src, dst) in enumerate(moves)]

    def arrive(first, last):
        @pl.when(swapping)
        def _():
            for copy in swapped[first:last]:
                copy.wait()

        @pl.when(jnp.logical_not(swapping))
        def _():
            for copy in kept[first:last]:
                copy.wait()

    pl.semaphore_wait(barrier, jnp.where(swapping, 8 + N_LON, 7 + N_LON))

    @pl.when(swapping)
    def _():
        for copy in swapped[:3]:
            copy.start()
        load.wait()
        for c in range(4):
            encode(tiles, code_send, peak_send, c)
            sent[c].start()
            sent[4 + c].start()
        for copy in swapped[3:]:
            copy.start()

    @pl.when(jnp.logical_not(swapping))
    def _():
        for copy in kept:
            copy.start()
        load.wait()

    arrive(0, 3)
    opposite = (N_, S_, E_, W_, NE_, NW_, SE_, SW_)
    ccopies = []
    for d, step in enumerate(NEIGHBOURS):
        copy = pltpu.make_async_remote_copy(
            src_ref=coef_got.at[8], dst_ref=coef_got.at[opposite[d]],
            send_sem=csend_sem.at[d], recv_sem=crecv_sem.at[opposite[d]],
            device_id=device_at(step), device_id_type=MESH)
        copy.start()
        ccopies.append(copy)

    lane16 = lanes((16, COLS))
    lane1 = lanes((8, COLS))

    def pack(src, s, ms):
        rings = []
        for half in range(2):
            ring = out_ref[src, half * 4, 0, ms, :]
            for k in range(1, 16):
                turned = pltpu.roll(out_ref[src, half * 4 + k // LEV, k % LEV, ms, :], k * 8, 1)
                inside = ((lane16 + (4 - k * 8 + 128)) & 127) < 8
                ring = jnp.where(inside, turned, ring)
            ring_send[s, half, ms, :] = ring.astype(BF16)
            rings.append(ring)
        edge_send[s, 0, ms, :] = jnp.where((lane16 & 7) < 4, rings[0], pltpu.roll(rings[1], 4, 1)).astype(BF16)
        edge_send[s, 1, ms, :] = jnp.where((lane16 & 7) >= 4, rings[0], pltpu.roll(rings[1], 124, 1)).astype(BF16)
        for side, first in ((0, 0), (1, ROWS - 3)):
            for r in range(3):
                for l in range(LEV):
                    row_send[s, side, r, l, ms, :] = out_ref[src, first + r, l, ms, :].astype(BF16)

    def start_copies(plan):
        copies = []
        for d, src_ref, dst_ref, landed, group in plan:
            copy = pltpu.make_async_remote_copy(
                src_ref=src_ref, dst_ref=dst_ref,
                send_sem=hsend_sem.at[group, d], recv_sem=hrecv_sem.at[group, landed],
                device_id=device_at(NEIGHBOURS[d]), device_id_type=MESH)
            copy.start()
            copies.append(copy)
        return copies

    def send_edges(s):
        low, high = ring_send.at[s, 0], ring_send.at[s, 1]
        return start_copies((
            (W_, edge_send.at[s, 0], edge_got.at[s, 1], E_, s),
            (E_, edge_send.at[s, 1], edge_got.at[s, 0], W_, s),
            (SW_, low, corner_got.at[s, 3], NE_, s),
            (SE_, low, corner_got.at[s, 2], NW_, s),
            (NW_, high, corner_got.at[s, 1], SE_, s),
            (NE_, high, corner_got.at[s, 0], SW_, s),
        ))

    def send_halos(src, s):
        @pl.loop(0, MEM // 16)
        def _(t):
            pack(src, s, pl.ds(pl.multiple_of(t * 16, 16), 16))

        return start_copies((
            (S_, row_send.at[s, 0], row_got.at[s, 1], N_, s),
            (N_, row_send.at[s, 1], row_got.at[s, 0], S_, s),
        )) + send_edges(s)

    copies = []
    for c in range(4):
        @pl.when(swapping)
        def _():
            sent[c].wait()
            sent[4 + c].wait()
            decode(code_got, peak_got, tiles, c)

        for r in range(ROWS):
            for l in range(LEV):
                for t in (2 * c, 2 * c + 1):
                    out_ref[0, r, l, pl.ds(t * 8, 8), :] = tiles[pl.ds(t * 256 + l * ROWS + r, 8, stride=32), :]
        ms = pl.ds(c * 16, 16)
        pack(0, 0, ms)
        copies += start_copies((
            (S_, row_send.at[0, 0, :, :, ms], row_got.at[0, 1, :, :, ms], N_, SLOTS + c),
            (N_, row_send.at[0, 1, :, :, ms], row_got.at[0, 0, :, :, ms], S_, SLOTS + c),
        ))
    copies += send_edges(0)
    for copy in ccopies:
        copy.wait()
    south_ok = jnp.where(trow > 0, 1.0, 0.0).astype(F32)
    north_ok = jnp.where(trow < N_LAT - 1, 1.0, 0.0).astype(F32)
    lane8 = lanes((ROWS, COLS))
    for block, (cen, west, east, ok) in enumerate(((S_, SW_, SE_, south_ok), (8, W_, E_, None), (N_, NW_, NE_, north_ok))):
        for half in range(2):
            for l in range(LEV):
                def pick(i):
                    if half == 0:
                        return jnp.where(lane8 < 96, coef_got[cen, i, l], coef_got[west, i, l])
                    return jnp.where(lane8 >= 32, coef_got[cen, i, l], coef_got[east, i, l])
                cu, cv, dd = pick(0), pick(1), pick(2)
                aw = jnp.maximum(cu, 0.0) + dd
                ae = dd - jnp.minimum(cu, 0.0)
                as_ = jnp.maximum(cv, 0.0) + dd
                an = dd - jnp.minimum(cv, 0.0)
                ac = 1.0 - (jnp.abs(cu) + jnp.abs(cv) + 4.0 * dd)
                for j, a in enumerate((ac, aw, ae, as_, an)):
                    a = a if ok is None else a * ok
                    for r in ((6, 7), range(8), (0, 1))[block]:
                        coefs[half, l, j, block * 8 + r - 6] = jnp.broadcast_to(a[r:r + 1], (8, COLS))

    from_at = lax.broadcasted_iota(jnp.int32, (256, 256), 0) & 127
    to_at = lanes((256, 256))
    step_at = jnp.where(to_at < 128, 1, 127)
    shifts[...] = jnp.where(((from_at + step_at) & 127) == (to_at & 127), 1.0, 0.0).astype(BF16)

    for s in range(SLOTS):
        for copy in copies:
            copy.wait()
        prev = max(s - 1, 0)

        for t in range(MEM // 16):
            ms = pl.ds(t * 16, 16)
            west, east = edge_got[s, 0, ms, :].astype(F32), edge_got[s, 1, ms, :].astype(F32)
            first = (lane16 & 7) < 4
            rings[0, ms, :] = jnp.where(first, corner_got[s, 1, ms, :].astype(F32), corner_got[s, 0, ms, :].astype(F32)) * south_ok
            rings[1, ms, :] = jnp.where(first, east, west)
            rings[2, ms, :] = jnp.where(first, pltpu.roll(east, 124, 1), pltpu.roll(west, 4, 1))
            rings[3, ms, :] = jnp.where(first, corner_got[s, 3, ms, :].astype(F32), corner_got[s, 2, ms, :].astype(F32)) * north_ok

        for l in range(LEV):
            @pl.loop(0, MEM // 16)
            def _(t):
                ms = pl.ds(pl.multiple_of(t * 16, 16), 16)
                for r in range(-3, ROWS + 3):
                    if 0 <= r < ROWS:
                        mine = out_ref[prev, r, l, ms, :]
                    elif r < 0:
                        mine = row_got[s, 0, r + 3, l, ms, :].astype(F32) * south_ok
                    else:
                        mine = row_got[s, 1, r - ROWS, l, ms, :].astype(F32) * north_ok
                    turn = (((r + 4) % 4) * LEV + l) * 8
                    aux = rings[(r + 4) // 4, ms, :]
                    aux = pltpu.roll(aux, 128 - turn, 1) if turn else aux
                    field[0, l, 0, r + 3, ms, :] = jnp.where(lane16 < 96, mine, aux)
                    field[0, l, 1, r + 3, ms, :] = jnp.where(lane16 >= 32, mine, aux)

        for step in range(STEPS):
            src, dst = step % 2, (step + 1) % 2

            @pl.loop(0, LEV)
            def _(l):
                inner = range(1 + step, ROWS + 5 - step)
                for r in inner:
                    if (r - inner[0]) % BAND == 0:
                        band = [x for x in range(r, r + BAND) if x in inner]
                        pieces = [jnp.concatenate(split(field[src, l, half, x, pl.ds(0, MEM // 2), :]), axis=1)
                                  for x in band for half in range(2)]
                        moved = dot(jnp.concatenate(pieces, axis=0), shifts[...])
                    factors = [[coefs[half, l, j, r - 1] for j in range(5)] for half in range(2)]
                    for t in range(MEM // 8):
                        ms = pl.ds(t * 8, 8)
                        new = []
                        for half in range(2):
                            ac, aw, ae, as_, an = factors[half]
                            v = field[src, l, half, r, ms, :]
                            if t < MEM // 16:
                                at = ((r - band[0]) * 2 + half) * (MEM // 2) + t * 8
                                west, east = moved[at:at + 8, :COLS], moved[at:at + 8, COLS:]
                            else:
                                west, east = pltpu.roll(v, 1, 1), pltpu.roll(v, COLS - 1, 1)
                            new.append((ac * v + as_ * field[src, l, half, r - 1, ms, :])
                                       + an * field[src, l, half, r + 1, ms, :]
                                       + (aw * west + ae * east))
                        if step < STEPS - 1:
                            field[dst, l, 0, r, ms, :] = new[0]
                            field[dst, l, 1, r, ms, :] = new[1]
                        else:
                            out_ref[s, r - 3, l, ms, :] = jnp.where(lane1 < 64, new[0], new[1])

        if s < SLOTS - 1:
            copies = send_halos(s, s + 1)
        if s == 0:
            arrive(3, 7)
            listed = pltpu.make_async_copy(owners_out, owners, load_sem.at[7])
            listed.start()
            listed.wait()
        observe(out_ref, s, cells, weights, values, xs, perts, innovs, last)


    turned = transforms_of(perts, innovs, tts)

    ids = [owners[0, 0, p] for p in range(PATCH)]
    left = lanes((MEM, COLS)) < MEM
    for o in range(N_LON):
        first, second = jnp.int32(PATCH), jnp.int32(PATCH)
        for p in range(PATCH):
            named = ids[p] == o
            second = jnp.where(jnp.logical_and(named, first < PATCH), p, second)
            first = jnp.where(jnp.logical_and(named, first == PATCH), p, first)
        pair = jnp.where(left, tts[first], tts[second])
        peak = jnp.maximum(jnp.max(jnp.abs(pair), axis=0, keepdims=True), 1e-30)
        held_peak[o] = peak
        held_send[o] = jnp.round(pair * (CODE / peak)).astype(jnp.int32).astype(jnp.int16)

    def parcel(k, half):
        owner = lax.rem(lon + k, N_LON)
        src, dst = ((held_send, held_got), (held_peak, held_peak_got))[half]
        return pltpu.make_async_remote_copy(
            src_ref=src.at[owner], dst_ref=dst.at[tcol], send_sem=tsend_sem.at[half, k],
            recv_sem=trecv_sem.at[half, tcol], device_id=(trow, owner), device_id_type=MESH)

    def landed(k, half):
        source = lax.rem(tcol + k, N_LON)
        src, dst = ((held_send, held_got), (held_peak, held_peak_got))[half]
        pltpu.make_async_remote_copy(
            src_ref=src.at[0], dst_ref=dst.at[source], send_sem=tsend_sem.at[half, k],
            recv_sem=trecv_sem.at[half, source], device_id=(trow, lon), device_id_type=MESH).wait_recv()

    keeps = [pltpu.make_async_copy(src.at[lon], dst.at[tcol], tsend_sem.at[i, 0])
             for i, (src, dst) in enumerate(((held_send, held_got), (held_peak, held_peak_got)))]

    @pl.when(swapping)
    def _():
        for half in range(2):
            parcel(0, half).start()

    @pl.when(jnp.logical_not(swapping))
    def _():
        for copy in keeps:
            copy.start()

    for k in range(1, N_LON):
        for half in range(2):
            parcel(k, half).start()

    analyse_members(turned, last, result)
    backs = [
        pltpu.make_async_remote_copy(src_ref=src, dst_ref=dst, send_sem=back_sem.at[0, i], recv_sem=back_sem.at[1, i],
                                     device_id=partner, device_id_type=MESH)
        for i, (src, dst) in enumerate(
            [(back_send.at[pl.ds(c * rows, rows)], back_got.at[pl.ds(c * rows, rows)]) for c in range(4)]
            + [(back_peak.at[c], back_peak_got.at[c]) for c in range(4)])]
    for c in range(4):
        place_members(result, ana_out, c)

        @pl.when(swapping)
        def _():
            encode(ana_out, back_send, back_peak, c)
            backs[c].start()
            backs[4 + c].start()

    @pl.when(swapping)
    def _():
        for half in range(2):
            parcel(0, half).wait_send()
            landed(0, half)

    @pl.when(jnp.logical_not(swapping))
    def _():
        for copy in keeps:
            copy.wait()

    for k in range(1, N_LON):
        for half in range(2):
            parcel(k, half).wait_send()
            landed(k, half)

    @pl.loop(0, N_LON, unroll=2)
    def _(o):
        pair = held_got[o].astype(jnp.int32).astype(F32) * (held_peak_got[o] * (1.0 / CODE))
        held_out[2 * o] = pair[:, :MEM]
        held_out[2 * o + 1] = pltpu.roll(pair, MEM, 1)[:, :MEM]

    @pl.when(swapping)
    def _():
        for c in range(4):
            backs[c].wait()
            backs[4 + c].wait()
            decode(back_got, back_peak_got, ana_out, c)


VMEM_SPEC = pl.BlockSpec(memory_space=pltpu.VMEM)
SMEM_SPEC = pl.BlockSpec(memory_space=pltpu.SMEM)
HBM_SPEC = pl.BlockSpec(memory_space=pltpu.HBM)


def cycle(ensemble, cu, cv, dd, cells, counts, values, errors, owners):
    return pl.pallas_call(
        cycle_kernel,
        out_shape=(jax.ShapeDtypeStruct((MEM * LEV * ROWS, COLS), F32),
                   jax.ShapeDtypeStruct((N_LON * PCAP, MEM, MEM), F32),
                   jax.ShapeDtypeStruct(owners.shape, jnp.int32)),
        in_specs=[HBM_SPEC] * 5 + [SMEM_SPEC, HBM_SPEC, VMEM_SPEC, HBM_SPEC],
        out_specs=(VMEM_SPEC, VMEM_SPEC, HBM_SPEC),
        scratch_shapes=[
            pltpu.VMEM((4, 256, SLOTS * OBS), BF16),
            pltpu.VMEM((SLOTS, PATCH, OBS), F32),
            pltpu.VMEM((PATCH * MEM, 256), F32),
            pltpu.SMEM((1, 1, PATCH), jnp.int32),
            pltpu.VMEM((SLOTS, ROWS, LEV, MEM, COLS), F32),
            pltpu.VMEM((SLOTS, 4, 1, PATCH, OBS), jnp.int32),
            pltpu.VMEM((SLOTS, PATCH, OBS), F32),
            pltpu.VMEM((SLOTS, 1, PATCH, OBS), F32),
            pltpu.VMEM((SLOTS, PATCH, OBS), F32),
            pltpu.VMEM((PATCH, 2 * MEM, 256), BF16),
            pltpu.VMEM((MEM * LEV * ROWS, COLS), F32),
            pltpu.VMEM((9, 3, LEV, ROWS, COLS), F32),
            pltpu.VMEM((2, LEV, 5, 12, 8, COLS), F32),
            pltpu.VMEM((SLOTS, 2, 3, LEV, MEM, COLS), BF16),
            pltpu.VMEM((SLOTS, 2, MEM, COLS), BF16),
            pltpu.VMEM((SLOTS, 2, MEM, COLS), BF16),
            pltpu.VMEM((SLOTS, 2, 3, LEV, MEM, COLS), BF16),
            pltpu.VMEM((SLOTS, 2, MEM, COLS), BF16),
            pltpu.VMEM((SLOTS, 4, MEM, COLS), BF16),
            pltpu.SemaphoreType.DMA((9,)),
            pltpu.SemaphoreType.DMA((9,)),
            pltpu.VMEM((MEM * LEV * ROWS, COLS), jnp.int16),
            pltpu.VMEM((MEM * LEV * ROWS, COLS), jnp.int16),
            pltpu.VMEM((4, LEV * ROWS, COLS), F32),
            pltpu.VMEM((4, LEV * ROWS, COLS), F32),
            pltpu.SemaphoreType.DMA((2, 8)),
            pltpu.SemaphoreType.DMA((8,)),
            pltpu.SemaphoreType.DMA((8,)),
            pltpu.SemaphoreType.DMA((2 * SLOTS, 8)),
            pltpu.SemaphoreType.DMA((2 * SLOTS, 8)),
            pltpu.VMEM((PATCH * MEM, 256), F32),
            pltpu.VMEM((PATCH + 1, MEM, COLS), F32),
            pltpu.VMEM((MEM * LEV * ROWS, COLS), jnp.int16),
            pltpu.VMEM((MEM * LEV * ROWS, COLS), jnp.int16),
            pltpu.VMEM((4, LEV * ROWS, COLS), F32),
            pltpu.VMEM((4, LEV * ROWS, COLS), F32),
            pltpu.SemaphoreType.DMA((2, 8)),
            pltpu.VMEM((N_LON, MEM, COLS), jnp.int16),
            pltpu.VMEM((N_LON, MEM, COLS), jnp.int16),
            pltpu.VMEM((N_LON, 1, COLS), F32),
            pltpu.VMEM((N_LON, 1, COLS), F32),
            pltpu.SemaphoreType.DMA((2, N_LON)),
            pltpu.SemaphoreType.DMA((2, N_LON)),
            pltpu.VMEM((4, MEM, COLS), F32),
            pltpu.VMEM((2, LEV, 2, ROWS + 6, MEM, COLS), F32),
            pltpu.VMEM((256, 256), BF16),
        ],
        compiler_params=pltpu.CompilerParams(
            collective_id=0, has_side_effects=True, vmem_limit_bytes=42 * 1024 * 1024),
        name="cycle",
    )(ensemble.reshape(MEM * LEV * ROWS, COLS), cu, cv, dd, cells, counts, values, errors, owners)


def body(ensemble, courant_lon, courant_lat, diffusion, obs_cells, obs_counts, obs_values, obs_errors, owners):
    analysis, held, _ = cycle(ensemble, courant_lon, courant_lat, diffusion,
                              obs_cells, obs_counts, obs_values, obs_errors, owners.transpose(0, 2, 1))
    return analysis.reshape(MEM, LEV, ROWS, COLS), held.reshape(1, 1, N_LON, PCAP, MEM, MEM)


def solution(mesh):
    placed = (
        P(None, None, "lat", "lon"),
        P(None, "lat", "lon"),
        P(None, "lat", "lon"),
        P(None, "lat", "lon"),
        P(None, None, "lat", "lon", None),
        P(None, "lat", "lon"),
        P(None, "lat", "lon", None),
        P(None, "lat", "lon", None),
        P("lat", "lon", None),
    )
    return jax.shard_map(
        body,
        mesh=mesh,
        in_specs=placed,
        out_specs=(P(None, None, "lat", "lon"), P("lat", "lon", None, None, None, None)),
        check_vma=False,
    )
```

```python
import functools

import jax
import jax.numpy as jnp
from jax import lax
from jax.experimental import pallas as pl
from jax.experimental.pallas import tpu as pltpu
from jax.sharding import PartitionSpec as P

PCAP = 2
SLOTS = 4
STEPS = 3
NS_ITERS = 6
MEM = 64
LEV = 4
ROWS = 8
COLS = 128
PATCH = 16
OBS = 128
N_LAT = 8
N_LON = 16
F32 = jnp.float32
BF16 = jnp.bfloat16
NEIGHBOURS = ((-1, 0), (1, 0), (0, -1), (0, 1), (-1, -1), (-1, 1), (1, -1), (1, 1))
S_, N_, W_, E_, SW_, SE_, NW_, NE_ = range(8)


MESH = pl.DeviceIdType.MESH


def tile_to_device(row, col):
    return row - row % 2 + col % 2, col - col % 2 + row % 2


def swap_partner(lat, lon):
    swapping = (lat % 2 + lon % 2) % 2 == 1
    return swapping, (lat + 1 - 2 * (lat % 2), lon + 1 - 2 * (lon % 2))


def lanes(shape):
    return lax.broadcasted_iota(jnp.int32, shape, len(shape) - 1)


CODE = 32767.0


def peaks_of(ref, chunk):
    def grow(m, peak):
        return jnp.maximum(peak, jnp.abs(ref[pl.ds(pl.multiple_of(m * 32, 32), 32), :]))
    start = chunk * 16
    return jnp.maximum(lax.fori_loop(start, start + 16, grow, jnp.zeros((32, COLS), F32), unroll=8), 1e-30)


def encode(ref, code_ref, peak_ref, chunk):
    peaks = peaks_of(ref, chunk)
    peak_ref[chunk] = peaks
    factor = CODE / peaks

    @pl.loop(chunk * 16, chunk * 16 + 16, unroll=4)
    def _(m):
        at = pl.ds(pl.multiple_of(m * 32, 32), 32)
        code_ref[at, :] = jnp.round(ref[at, :] * factor).astype(jnp.int32).astype(jnp.int16)


def decode(code_ref, peak_ref, ref, chunk):
    steps = peak_ref[chunk] * (1.0 / CODE)

    @pl.loop(chunk * 16, chunk * 16 + 16, unroll=4)
    def _(m):
        at = pl.ds(pl.multiple_of(m * 32, 32), 32)
        ref[at, :] = code_ref[at, :].astype(jnp.int32).astype(F32) * steps


def butterfly(parts):
    parts = list(parts)
    lane = lanes(parts[0].shape)
    for bit in (1, 2, 4, 8):
        keep = (lane & (8 * bit)) == 0
        for i in range(16):
            if i & bit:
                continue
            a, b = parts[i], parts[i + bit]
            parts[i] = jnp.where(keep, a, pltpu.roll(b, 8 * bit, 1))
            parts[i + bit] = jnp.where(keep, pltpu.roll(a, 128 - 8 * bit, 1), b)
    return parts


def split(x):
    hi = x.astype(BF16)
    return hi, (x - hi.astype(F32)).astype(BF16)


def dot(a, b):
    return jnp.dot(a, b, preferred_element_type=F32)


def dot_t(a, b):
    return lax.dot_general(a, b, (((1,), (1,)), ((), ())), preferred_element_type=F32)


def block_diagonal(x):
    block = lanes(x.shape) // 64
    return jnp.concatenate([jnp.where(block == i, x, jnp.zeros_like(x)) for i in range(4)], axis=0)


def times(x_parts, y_parts):
    yh, yl = y_parts
    n = sum(h.shape[0] for h, _ in x_parts)
    his = [h for h, _ in x_parts]
    los = [l for _, l in x_parts]
    top = dot(jnp.concatenate(his + los, axis=0), yh)
    low = dot(jnp.concatenate(his, axis=0), yl)
    total = top[:n] + top[n:] + low
    outs, at = [], 0
    for h, _ in x_parts:
        outs.append(total[at:at + h.shape[0]])
        at += h.shape[0]
    return outs


def cell_weights(counts_ref, errors_ref, slot):
    shape = (PATCH, OBS)
    patch = lax.broadcasted_iota(jnp.int32, shape, 0)
    count = jnp.zeros(shape, jnp.int32)
    for p in range(PATCH):
        count = jnp.where(patch == p, counts_ref[slot, 0, p], count)
    return jnp.where(lanes(shape) < count, 1.0 / errors_ref[slot, 0], 0.0)


def observe(states_ref, slot, cells, weights, values, xs, perts, innovs, last):
    @pl.loop(0, 8)
    def _(k):
        q, t = k // 4, k % 4
        halves = []
        for u in range(2):
            ms = pl.ds(pl.multiple_of(t * 16 + u * 8, 8), 8)
            parts = [states_ref[slot, i % 8, q * 2 + i // 8, ms, :] for i in range(16)]
            halves.append(butterfly(parts))
        cs = pl.ds(pl.multiple_of(q * 128, 128), 128)
        for p in range(PATCH):
            x = jnp.concatenate([halves[0][p], halves[1][p]], axis=0)
            hi, lo = split(x)
            xs[p, pl.ds(pl.multiple_of(t * 16, 16), 16), cs] = hi
            xs[p, pl.ds(pl.multiple_of(MEM + t * 16, 16), 16), cs] = lo
            if slot == SLOTS - 1:
                last[pl.ds(pl.multiple_of(p * MEM + t * 16, 16), 16), cs] = x

    cell_id = lax.broadcasted_iota(jnp.int32, (256, OBS), 0).astype(F32).astype(BF16)
    one, zero = jnp.full((256, OBS), 0.25, BF16), jnp.zeros((256, OBS), BF16)

    @pl.loop(0, PATCH, unroll=8)
    def _(p):
        w = None
        for corner in range(4):
            idx = cells[slot, corner, 0, pl.ds(p, 1), :].astype(F32)
            idx = jnp.broadcast_to(idx, (256, OBS)).astype(BF16)
            hit = jnp.where(cell_id == idx, one, zero)
            w = hit if w is None else w + hit
        both = dot(xs[p], w)
        equivalent = both[:MEM] + both[MEM:]
        mean = jnp.sum(equivalent, axis=0, keepdims=True) * (1.0 / MEM)
        weight = weights[slot, pl.ds(p, 1), :]
        pert = ((equivalent - mean) * weight).astype(BF16)
        perts[p // 4, pl.ds(pl.multiple_of((p % 4) * MEM, MEM), MEM), slot * OBS:(slot + 1) * OBS] = pert
        innovs[slot, pl.ds(p, 1), :] = (values[slot, 0, pl.ds(p, 1), :] - mean) * weight


def transforms_of(perts, innovs, tts):
    shape = (MEM, 256)
    block = lanes(shape) // 64
    eye = (lax.broadcasted_iota(jnp.int32, shape, 0) == (lanes(shape) & 63)).astype(F32)
    innov = jnp.concatenate([innovs[s] for s in range(SLOTS)], axis=1).astype(BF16)
    ys, zs, alongs, sizes = [], [], [], []
    for g in range(4):
        pg = perts[g]
        full = dot_t(pg, pg)
        gram = full[0:MEM]
        for i in range(1, 4):
            gram = jnp.where(block == i, full[i * MEM:(i + 1) * MEM], gram)
        al = dot_t(innov, pg)
        row = lax.broadcasted_iota(jnp.int32, al.shape, 0)
        al = jnp.sum(jnp.where(row == g * 4 + lanes(al.shape) // 64, al, 0.0), axis=0, keepdims=True)
        alongs.append(al)
        amat = gram + (MEM - 1.0) * eye
        sq = jnp.sum(amat * amat, axis=0, keepdims=True)
        blk1 = lanes((1, 256)) // 64
        size = jnp.zeros((1, 256), F32)
        for i in range(4):
            total = jnp.sum(jnp.where(blk1 == i, sq, 0.0), axis=1, keepdims=True)
            size = jnp.where(blk1 == i, total, size)
        size = jnp.sqrt(size)
        sizes.append(size)
        ys.append(amat / size)
        zs.append(None)
    for it in range(NS_ITERS):
        mixers = []
        for g in range(4):
            yh, yl = split(ys[g])
            if it == 0:
                zy = ys[g]
            else:
                (zy,) = times([split(zs[g])], (block_diagonal(yh), block_diagonal(yl)))
            mixers.append(1.5 * eye - 0.5 * zy)
        for g in range(4):
            mh, ml = split(mixers[g])
            md = (block_diagonal(mh), block_diagonal(ml))
            if it == 0:
                (ys[g],) = times([split(ys[g])], md)
                zs[g] = mixers[g]
            elif it < NS_ITERS - 1:
                ys[g], zs[g] = times([split(ys[g]), split(zs[g])], md)
            else:
                (zs[g],) = times([split(zs[g])], md)
    eye2 = (lax.broadcasted_iota(jnp.int32, (MEM, 128), 0) == (lanes((MEM, 128)) & 63)).astype(F32)
    size0 = jnp.sqrt(jnp.full((1, 128), MEM * (MEM - 1.0) * (MEM - 1.0), F32))
    y0 = (MEM - 1.0) / size0
    z0 = jnp.ones((1, 128), F32)
    for it in range(NS_ITERS):
        m0 = 1.5 - 0.5 * z0 * y0
        y0, z0 = y0 * m0, m0 * z0
    empty = eye2 * (z0 * jnp.sqrt((MEM - 1.0) / size0))

    tts[PATCH] = empty
    turned = []
    for g in range(4):
        zh, zl = split(zs[g])
        zd = (block_diagonal(zh), block_diagonal(zl))
        (first,) = times([split(jnp.broadcast_to(alongs[g], (16, 256)))], zd)
        (second,) = times([split(first)], zd)
        tt = zs[g] * jnp.sqrt((MEM - 1.0) / sizes[g]) + second[0:1] / sizes[g]
        turned.append(tt)
        both = jnp.transpose(jnp.concatenate([tt, tt], axis=0))
        for i in range(4):
            tts[g * 4 + i] = both[i * MEM:(i + 1) * MEM]
    return turned


def analyse_members(turned, last, result):
    for g in range(4):
        th, tl = split(turned[g])
        thd, tld = block_diagonal(th), block_diagonal(tl)
        devs, means = [], []
        for i in range(4):
            x = last[pl.ds((g * 4 + i) * MEM, MEM), :]
            mean = jnp.sum(x, axis=0, keepdims=True) * (1.0 / MEM)
            devs.append(x - mean)
            means.append(mean)
        dh, dl = split(jnp.concatenate(devs, axis=0))
        ana = dot(thd, dh) + dot(tld, dh) + dot(thd, dl)
        for i in range(4):
            result[pl.ds((g * 4 + i) * MEM, MEM), :] = ana[i * MEM:(i + 1) * MEM] + means[i]


def place_members(result, out_ref, chunk):
    @pl.loop(0, 4)
    def _(k):
        q, t = k // 2, chunk * 2 + k % 2
        cs = pl.ds(pl.multiple_of(q * 128, 128), 128)
        parts = [result[pl.ds(pl.multiple_of(p * MEM + t * 8, 8), 8), cs] for p in range(16)]
        for i, x in enumerate(butterfly(parts)):
            out_ref[pl.ds(t * 256 + q * 16 + i, 8, stride=32), :] = x


def cycle_kernel(ens_ref, cu_ref, cv_ref, dd_ref, cells_ref, counts_ref, values_ref, errors_ref, owners_ref,
                 ana_out, held_out, owners_out,
                 perts, innovs, last, owners,
                 out_ref, cells, weights, values, weight_send, xs,
                 tiles, coef_got, coefs, row_send, ring_send, edge_send,
                 row_got, edge_got, corner_got,
                 load_sem, swap_sem, code_send, code_got, peak_send, peak_got, code_sem, csend_sem, crecv_sem,
                 hsend_sem, hrecv_sem,
                 result, tts, back_send, back_got, back_peak, back_peak_got, back_sem,
                 held_send, held_got, held_peak, held_peak_got, tsend_sem, trecv_sem, rings, field, shifts):
    lat, lon = lax.axis_index("lat"), lax.axis_index("lon")
    trow, tcol = tile_to_device(lat, lon)

    def device_at(step):
        row = lax.rem(trow + step[0] + N_LAT, N_LAT)
        col = lax.rem(tcol + step[1] + N_LON, N_LON)
        return tile_to_device(row, col)

    barrier = pltpu.get_barrier_semaphore()
    for step in NEIGHBOURS:
        pl.semaphore_signal(barrier, inc=1, device_id=device_at(step),
                            device_id_type=MESH)
    swapping, partner = swap_partner(lat, lon)
    for k in range(1, N_LON):
        pl.semaphore_signal(barrier, inc=1, device_id=tile_to_device(lat, lax.rem(tcol + k, N_LON)), device_id_type=MESH)

    @pl.when(swapping)
    def _():
        pl.semaphore_signal(barrier, inc=1, device_id=tile_to_device(lat, tcol), device_id_type=MESH)

    moves = [(ref, coef_got.at[8, i]) for i, ref in enumerate((cu_ref, cv_ref, dd_ref))]
    moves += [(cells_ref, cells), (weight_send, weights), (values_ref, values), (owners_ref, owners_out)]
    for slot in range(SLOTS):
        weight_send[slot] = cell_weights(counts_ref, errors_ref, slot)
    load = pltpu.make_async_copy(ens_ref, tiles, load_sem.at[8])
    load.start()
    rows = MEM * LEV * ROWS // 4
    sent = [
        pltpu.make_async_remote_copy(src_ref=src, dst_ref=dst, send_sem=code_sem.at[0, i], recv_sem=code_sem.at[1, i],
                                     device_id=partner, device_id_type=MESH)
        for i, (src, dst) in enumerate(
            [(code_send.at[pl.ds(c * rows, rows)], code_got.at[pl.ds(c * rows, rows)]) for c in range(4)]
            + [(peak_send.at[c], peak_got.at[c]) for c in range(4)])]
    kept = [pltpu.make_async_copy(src, dst, load_sem.at[i]) for i, (src, dst) in enumerate(moves)]
    swapped = [
        pltpu.make_async_remote_copy(src_ref=src, dst_ref=dst, send_sem=load_sem.at[i], recv_sem=swap_sem.at[i],
                                     device_id=partner, device_id_type=MESH)
        for i, (src, dst) in enumerate(moves)]

    def arrive(first, last):
        @pl.when(swapping)
        def _():
            for copy in swapped[first:last]:
                copy.wait()

        @pl.when(jnp.logical_not(swapping))
        def _():
            for copy in kept[first:last]:
                copy.wait()

    pl.semaphore_wait(barrier, jnp.where(swapping, 8 + N_LON, 7 + N_LON))

    @pl.when(swapping)
    def _():
        for copy in swapped[:3]:
            copy.start()
        load.wait()
        for c in range(4):
            encode(tiles, code_send, peak_send, c)
            sent[c].start()
            sent[4 + c].start()
        for copy in swapped[3:]:
            copy.start()

    @pl.when(jnp.logical_not(swapping))
    def _():
        for copy in kept:
            copy.start()
        load.wait()

    arrive(0, 3)
    opposite = (N_, S_, E_, W_, NE_, NW_, SE_, SW_)
    ccopies = []
    for d, step in enumerate(NEIGHBOURS):
        copy = pltpu.make_async_remote_copy(
            src_ref=coef_got.at[8], dst_ref=coef_got.at[opposite[d]],
            send_sem=csend_sem.at[d], recv_sem=crecv_sem.at[opposite[d]],
            device_id=device_at(step), device_id_type=MESH)
        copy.start()
        ccopies.append(copy)

    lane16 = lanes((16, COLS))
    lane1 = lanes((8, COLS))

    def pack(src, s, ms):
        rings = []
        for half in range(2):
            ring = out_ref[src, half * 4, 0, ms, :]
            for k in range(1, 16):
                turned = pltpu.roll(out_ref[src, half * 4 + k // LEV, k % LEV, ms, :], k * 8, 1)
                inside = ((lane16 + (4 - k * 8 + 128)) & 127) < 8
                ring = jnp.where(inside, turned, ring)
            ring_send[s, half, ms, :] = ring.astype(BF16)
            rings.append(ring)
        edge_send[s, 0, ms, :] = jnp.where((lane16 & 7) < 4, rings[0], pltpu.roll(rings[1], 4, 1)).astype(BF16)
        edge_send[s, 1, ms, :] = jnp.where((lane16 & 7) >= 4, rings[0], pltpu.roll(rings[1], 124, 1)).astype(BF16)
        for side, first in ((0, 0), (1, ROWS - 3)):
            for r in range(3):
                for l in range(LEV):
                    row_send[s, side, r, l, ms, :] = out_ref[src, first + r, l, ms, :].astype(BF16)

    def start_copies(plan):
        copies = []
        for d, src_ref, dst_ref, landed, group in plan:
            copy = pltpu.make_async_remote_copy(
                src_ref=src_ref, dst_ref=dst_ref,
                send_sem=hsend_sem.at[group, d], recv_sem=hrecv_sem.at[group, landed],
                device_id=device_at(NEIGHBOURS[d]), device_id_type=MESH)
            copy.start()
            copies.append(copy)
        return copies

    def send_edges(s):
        low, high = ring_send.at[s, 0], ring_send.at[s, 1]
        return start_copies((
            (W_, edge_send.at[s, 0], edge_got.at[s, 1], E_, s),
            (E_, edge_send.at[s, 1], edge_got.at[s, 0], W_, s),
            (SW_, low, corner_got.at[s, 3], NE_, s),
            (SE_, low, corner_got.at[s, 2], NW_, s),
            (NW_, high, corner_got.at[s, 1], SE_, s),
            (NE_, high, corner_got.at[s, 0], SW_, s),
        ))

    def send_halos(src, s):
        @pl.loop(0, MEM // 16)
        def _(t):
            pack(src, s, pl.ds(pl.multiple_of(t * 16, 16), 16))

        return start_copies((
            (S_, row_send.at[s, 0], row_got.at[s, 1], N_, s),
            (N_, row_send.at[s, 1], row_got.at[s, 0], S_, s),
        )) + send_edges(s)

    copies = []
    for c in range(4):
        @pl.when(swapping)
        def _():
            sent[c].wait()
            sent[4 + c].wait()
            decode(code_got, peak_got, tiles, c)

        for r in range(ROWS):
            for l in range(LEV):
                for t in (2 * c, 2 * c + 1):
                    out_ref[0, r, l, pl.ds(t * 8, 8), :] = tiles[pl.ds(t * 256 + l * ROWS + r, 8, stride=32), :]
        ms = pl.ds(c * 16, 16)
        pack(0, 0, ms)
        copies += start_copies((
            (S_, row_send.at[0, 0, :, :, ms], row_got.at[0, 1, :, :, ms], N_, SLOTS + c),
            (N_, row_send.at[0, 1, :, :, ms], row_got.at[0, 0, :, :, ms], S_, SLOTS + c),
        ))
    copies += send_edges(0)
    for copy in ccopies:
        copy.wait()
    south_ok = jnp.where(trow > 0, 1.0, 0.0).astype(F32)
    north_ok = jnp.where(trow < N_LAT - 1, 1.0, 0.0).astype(F32)
    lane8 = lanes((ROWS, COLS))
    for block, (cen, west, east, ok) in enumerate(((S_, SW_, SE_, south_ok), (8, W_, E_, None), (N_, NW_, NE_, north_ok))):
        for half in range(2):
            for l in range(LEV):
                def pick(i):
                    if half == 0:
                        return jnp.where(lane8 < 96, coef_got[cen, i, l], coef_got[west, i, l])
                    return jnp.where(lane8 >= 32, coef_got[cen, i, l], coef_got[east, i, l])
                cu, cv, dd = pick(0), pick(1), pick(2)
                aw = jnp.maximum(cu, 0.0) + dd
                ae = dd - jnp.minimum(cu, 0.0)
                as_ = jnp.maximum(cv, 0.0) + dd
                an = dd - jnp.minimum(cv, 0.0)
                ac = 1.0 - (jnp.abs(cu) + jnp.abs(cv) + 4.0 * dd)
                for j, a in enumerate((ac, aw, ae, as_, an)):
                    a = a if ok is None else a * ok
                    for r in ((6, 7), range(8), (0, 1))[block]:
                        coefs[half, l, j, block * 8 + r - 6] = jnp.broadcast_to(a[r:r + 1], (8, COLS))

    from_at = lax.broadcasted_iota(jnp.int32, (256, 256), 0) & 127
    to_at = lanes((256, 256))
    step_at = jnp.where(to_at < 128, 1, 127)
    shifts[...] = jnp.where(((from_at + step_at) & 127) == (to_at & 127), 1.0, 0.0).astype(BF16)

    for s in range(SLOTS):
        for copy in copies:
            copy.wait()
        prev = max(s - 1, 0)

        for t in range(MEM // 16):
            ms = pl.ds(t * 16, 16)
            west, east = edge_got[s, 0, ms, :].astype(F32), edge_got[s, 1, ms, :].astype(F32)
            first = (lane16 & 7) < 4
            rings[0, ms, :] = jnp.where(first, corner_got[s, 1, ms, :].astype(F32), corner_got[s, 0, ms, :].astype(F32)) * south_ok
            rings[1, ms, :] = jnp.where(first, east, west)
            rings[2, ms, :] = jnp.where(first, pltpu.roll(east, 124, 1), pltpu.roll(west, 4, 1))
            rings[3, ms, :] = jnp.where(first, corner_got[s, 3, ms, :].astype(F32), corner_got[s, 2, ms, :].astype(F32)) * north_ok

        for l in range(LEV):
            @pl.loop(0, MEM // 16)
            def _(t):
                ms = pl.ds(pl.multiple_of(t * 16, 16), 16)
                for r in range(-3, ROWS + 3):
                    if 0 <= r < ROWS:
                        mine = out_ref[prev, r, l, ms, :]
                    elif r < 0:
                        mine = row_got[s, 0, r + 3, l, ms, :].astype(F32) * south_ok
                    else:
                        mine = row_got[s, 1, r - ROWS, l, ms, :].astype(F32) * north_ok
                    turn = (((r + 4) % 4) * LEV + l) * 8
                    aux = rings[(r + 4) // 4, ms, :]
                    aux = pltpu.roll(aux, 128 - turn, 1) if turn else aux
                    field[0, l, 0, r + 3, ms, :] = jnp.where(lane16 < 96, mine, aux)
                    field[0, l, 1, r + 3, ms, :] = jnp.where(lane16 >= 32, mine, aux)

        for step in range(STEPS):
            src, dst = step % 2, (step + 1) % 2

            @pl.loop(0, LEV)
            def _(l):
                inner = range(1 + step, ROWS + 5 - step)
                pieces = [jnp.concatenate(split(field[src, l, half, r, pl.ds(0, MEM // 2), :]), axis=1)
                          for r in inner for half in range(2)]
                moved = dot(jnp.concatenate(pieces, axis=0), shifts[...])
                for r in inner:
                    factors = [[coefs[half, l, j, r - 1] for j in range(5)] for half in range(2)]
                    for t in range(MEM // 8):
                        ms = pl.ds(t * 8, 8)
                        new = []
                        for half in range(2):
                            ac, aw, ae, as_, an = factors[half]
                            v = field[src, l, half, r, ms, :]
                            if t < MEM // 16:
                                at = ((r - inner[0]) * 2 + half) * (MEM // 2) + t * 8
                                west, east = moved[at:at + 8, :COLS], moved[at:at + 8, COLS:]
                            else:
                                west, east = pltpu.roll(v, 1, 1), pltpu.roll(v, COLS - 1, 1)
                            new.append((ac * v + as_ * field[src, l, half, r - 1, ms, :])
                                       + an * field[src, l, half, r + 1, ms, :]
                                       + (aw * west + ae * east))
                        if step < STEPS - 1:
                            field[dst, l, 0, r, ms, :] = new[0]
                            field[dst, l, 1, r, ms, :] = new[1]
                        else:
                            out_ref[s, r - 3, l, ms, :] = jnp.where(lane1 < 64, new[0], new[1])

        if s < SLOTS - 1:
            copies = send_halos(s, s + 1)
        if s == 0:
            arrive(3, 7)
            listed = pltpu.make_async_copy(owners_out, owners, load_sem.at[7])
            listed.start()
            listed.wait()
        observe(out_ref, s, cells, weights, values, xs, perts, innovs, last)


    turned = transforms_of(perts, innovs, tts)

    ids = [owners[0, 0, p] for p in range(PATCH)]
    left = lanes((MEM, COLS)) < MEM
    for o in range(N_LON):
        first, second = jnp.int32(PATCH), jnp.int32(PATCH)
        for p in range(PATCH):
            named = ids[p] == o
            second = jnp.where(jnp.logical_and(named, first < PATCH), p, second)
            first = jnp.where(jnp.logical_and(named, first == PATCH), p, first)
        pair = jnp.where(left, tts[first], tts[second])
        peak = jnp.maximum(jnp.max(jnp.abs(pair), axis=0, keepdims=True), 1e-30)
        held_peak[o] = peak
        held_send[o] = jnp.round(pair * (CODE / peak)).astype(jnp.int32).astype(jnp.int16)

    def parcel(k, half):
        owner = lax.rem(lon + k, N_LON)
        src, dst = ((held_send, held_got), (held_peak, held_peak_got))[half]
        return pltpu.make_async_remote_copy(
            src_ref=src.at[owner], dst_ref=dst.at[tcol], send_sem=tsend_sem.at[half, k],
            recv_sem=trecv_sem.at[half, tcol], device_id=(trow, owner), device_id_type=MESH)

    def landed(k, half):
        source = lax.rem(tcol + k, N_LON)
        src, dst = ((held_send, held_got), (held_peak, held_peak_got))[half]
        pltpu.make_async_remote_copy(
            src_ref=src.at[0], dst_ref=dst.at[source], send_sem=tsend_sem.at[half, k],
            recv_sem=trecv_sem.at[half, source], device_id=(trow, lon), device_id_type=MESH).wait_recv()

    keeps = [pltpu.make_async_copy(src.at[lon], dst.at[tcol], tsend_sem.at[i, 0])
             for i, (src, dst) in enumerate(((held_send, held_got), (held_peak, held_peak_got)))]

    @pl.when(swapping)
    def _():
        for half in range(2):
            parcel(0, half).start()

    @pl.when(jnp.logical_not(swapping))
    def _():
        for copy in keeps:
            copy.start()

    for k in range(1, N_LON):
        for half in range(2):
            parcel(k, half).start()

    analyse_members(turned, last, result)
    backs = [
        pltpu.make_async_remote_copy(src_ref=src, dst_ref=dst, send_sem=back_sem.at[0, i], recv_sem=back_sem.at[1, i],
                                     device_id=partner, device_id_type=MESH)
        for i, (src, dst) in enumerate(
            [(back_send.at[pl.ds(c * rows, rows)], back_got.at[pl.ds(c * rows, rows)]) for c in range(4)]
            + [(back_peak.at[c], back_peak_got.at[c]) for c in range(4)])]
    for c in range(4):
        place_members(result, ana_out, c)

        @pl.when(swapping)
        def _():
            encode(ana_out, back_send, back_peak, c)
            backs[c].start()
            backs[4 + c].start()

    @pl.when(swapping)
    def _():
        for half in range(2):
            parcel(0, half).wait_send()
            landed(0, half)

    @pl.when(jnp.logical_not(swapping))
    def _():
        for copy in keeps:
            copy.wait()

    for k in range(1, N_LON):
        for half in range(2):
            parcel(k, half).wait_send()
            landed(k, half)

    @pl.loop(0, N_LON, unroll=2)
    def _(o):
        pair = held_got[o].astype(jnp.int32).astype(F32) * (held_peak_got[o] * (1.0 / CODE))
        held_out[2 * o] = pair[:, :MEM]
        held_out[2 * o + 1] = pltpu.roll(pair, MEM, 1)[:, :MEM]

    @pl.when(swapping)
    def _():
        for c in range(4):
            backs[c].wait()
            backs[4 + c].wait()
            decode(back_got, back_peak_got, ana_out, c)


VMEM_SPEC = pl.BlockSpec(memory_space=pltpu.VMEM)
SMEM_SPEC = pl.BlockSpec(memory_space=pltpu.SMEM)
ANY_SPEC = pl.BlockSpec(memory_space=pl.ANY)


def cycle(ensemble, cu, cv, dd, cells, counts, values, errors, owners):
    return pl.pallas_call(
        cycle_kernel,
        out_shape=(jax.ShapeDtypeStruct((MEM * LEV * ROWS, COLS), F32),
                   jax.ShapeDtypeStruct((N_LON * PCAP, MEM, MEM), F32),
                   jax.ShapeDtypeStruct(owners.shape, jnp.int32)),
        in_specs=[ANY_SPEC] * 5 + [SMEM_SPEC, ANY_SPEC, VMEM_SPEC, ANY_SPEC],
        out_specs=(VMEM_SPEC, VMEM_SPEC, ANY_SPEC),
        scratch_shapes=[
            pltpu.VMEM((4, 256, SLOTS * OBS), BF16),
            pltpu.VMEM((SLOTS, PATCH, OBS), F32),
            pltpu.VMEM((PATCH * MEM, 256), F32),
            pltpu.SMEM((1, 1, PATCH), jnp.int32),
            pltpu.VMEM((SLOTS, ROWS, LEV, MEM, COLS), F32),
            pltpu.VMEM((SLOTS, 4, 1, PATCH, OBS), jnp.int32),
            pltpu.VMEM((SLOTS, PATCH, OBS), F32),
            pltpu.VMEM((SLOTS, 1, PATCH, OBS), F32),
            pltpu.VMEM((SLOTS, PATCH, OBS), F32),
            pltpu.VMEM((PATCH, 2 * MEM, 256), BF16),
            pltpu.VMEM((MEM * LEV * ROWS, COLS), F32),
            pltpu.VMEM((9, 3, LEV, ROWS, COLS), F32),
            pltpu.VMEM((2, LEV, 5, 12, 8, COLS), F32),
            pltpu.VMEM((SLOTS, 2, 3, LEV, MEM, COLS), BF16),
            pltpu.VMEM((SLOTS, 2, MEM, COLS), BF16),
            pltpu.VMEM((SLOTS, 2, MEM, COLS), BF16),
            pltpu.VMEM((SLOTS, 2, 3, LEV, MEM, COLS), BF16),
            pltpu.VMEM((SLOTS, 2, MEM, COLS), BF16),
            pltpu.VMEM((SLOTS, 4, MEM, COLS), BF16),
            pltpu.SemaphoreType.DMA((9,)),
            pltpu.SemaphoreType.DMA((9,)),
            pltpu.VMEM((MEM * LEV * ROWS, COLS), jnp.int16),
            pltpu.VMEM((MEM * LEV * ROWS, COLS), jnp.int16),
            pltpu.VMEM((4, LEV * ROWS, COLS), F32),
            pltpu.VMEM((4, LEV * ROWS, COLS), F32),
            pltpu.SemaphoreType.DMA((2, 8)),
            pltpu.SemaphoreType.DMA((8,)),
            pltpu.SemaphoreType.DMA((8,)),
            pltpu.SemaphoreType.DMA((2 * SLOTS, 8)),
            pltpu.SemaphoreType.DMA((2 * SLOTS, 8)),
            pltpu.VMEM((PATCH * MEM, 256), F32),
            pltpu.VMEM((PATCH + 1, MEM, COLS), F32),
            pltpu.VMEM((MEM * LEV * ROWS, COLS), jnp.int16),
            pltpu.VMEM((MEM * LEV * ROWS, COLS), jnp.int16),
            pltpu.VMEM((4, LEV * ROWS, COLS), F32),
            pltpu.VMEM((4, LEV * ROWS, COLS), F32),
            pltpu.SemaphoreType.DMA((2, 8)),
            pltpu.VMEM((N_LON, MEM, COLS), jnp.int16),
            pltpu.VMEM((N_LON, MEM, COLS), jnp.int16),
            pltpu.VMEM((N_LON, 1, COLS), F32),
            pltpu.VMEM((N_LON, 1, COLS), F32),
            pltpu.SemaphoreType.DMA((2, N_LON)),
            pltpu.SemaphoreType.DMA((2, N_LON)),
            pltpu.VMEM((4, MEM, COLS), F32),
            pltpu.VMEM((2, LEV, 2, ROWS + 6, MEM, COLS), F32),
            pltpu.VMEM((256, 256), BF16),
        ],
        compiler_params=pltpu.CompilerParams(
            collective_id=0, has_side_effects=True, vmem_limit_bytes=60 * 1024 * 1024),
        name="cycle",
    )(ensemble.reshape(MEM * LEV * ROWS, COLS), cu, cv, dd, cells, counts, values, errors, owners)


def body(ensemble, courant_lon, courant_lat, diffusion, obs_cells, obs_counts, obs_values, obs_errors, owners):
    analysis, held, _ = cycle(ensemble, courant_lon, courant_lat, diffusion,
                              obs_cells, obs_counts, obs_values, obs_errors, owners.transpose(0, 2, 1))
    return analysis.reshape(MEM, LEV, ROWS, COLS), held.reshape(1, 1, N_LON, PCAP, MEM, MEM)


def solution(mesh):
    placed = (
        P(None, None, "lat", "lon"),
        P(None, "lat", "lon"),
        P(None, "lat", "lon"),
        P(None, "lat", "lon"),
        P(None, None, "lat", "lon", None),
        P(None, "lat", "lon"),
        P(None, "lat", "lon", None),
        P(None, "lat", "lon", None),
        P("lat", "lon", None),
    )
    return jax.shard_map(
        body,
        mesh=mesh,
        in_specs=placed,
        out_specs=(P(None, None, "lat", "lon"), P("lat", "lon", None, None, None, None)),
        check_vma=False,
    )
```
